32 devices in a mesh: groups: 2 (over y), samples: 8 (over z, x), section: 1, mp: 2 (over core).
Axes of the slice: x: 2, y: 2, z: 4, core: 2. Of those that a mesh axis runs over, the one named last changes fastest.
Arguments:
- stored_inputs: bfloat16 [1, 16, 128, 2048], P('section', ('groups', 'samples'), None, 'mp'), parts along dimension 1
- top_cotangent: bfloat16 [16, 128, 2048], P(('groups', 'samples'), None, 'mp'), parts along dimension 0, may hold values from -0.375 to 0.375
- layer_weights: bfloat16 [1, 2048, 2048], P('section', 'samples', 'mp'), may hold values from -0.125 to 0.125
- block_layout: int32 [1, 2, 2], P('section'), may hold values 0 or 1
- region_mask: int32 [128], replicated, may hold values from 0 to 1, as said below
- partner_samples: int32 [16], P('groups'), parts along dimension 0, may hold values from 0 to 7, as said below
- spins: int32 [16, 128], P(('groups', 'samples')), parts along dimension 0, may hold values from 0 to 1
Outputs:
- weight_grad: float32 [2, 2048, 2048], P(('groups', 'section'), 'samples', 'mp'), parts along dimension 0
- layer_cotangents: bfloat16 [1, 16, 128, 2048], P('section', ('groups', 'samples'), None, 'mp'), parts along dimension 1
- embed_grad: float32 [4, 2048], P('groups', 'mp'), parts along dimension 0
The draws below stay inside these ranges and needn't reach their ends.
There are 2 independent parts, one for each index of `groups`. The reference program is written for one: setup_inputs(seed, part) draws one part's arguments, and reference() takes and returns one part's arrays. A program takes and returns all parts, laid end to end along the dimension named above; an argument that names none is the same for every part. Nothing has to cross between parts.
Inputs may be any that keep to these rules, and one draw needn't show every extreme that they name: `region_mask`: exactly 64 of the 128 entries are 1, the others 0. The samples pair up: partner_samples[partner_samples[r]] = r and partner_samples[r] != r for every sample r. `block_layout`: a query block always sees its own block, whatever the diagonal entry holds.
All inputs are finite; a program needn't handle non-finite values.
Results may differ from the reference program's by a relative error of at most 0.03.
Values may be sent and summed in bfloat16 or wider, within the bound.
A program may use at most 64 MiB of HBM per device.

```python
import jax
import jax.numpy as jnp
from jax import lax

D = 2048
HEAD = 128
BLOCK = 64
SEQ = 128
SPINS = 2
MB = 1
LAYERS = 1
SHARDS = 8
SAMPLES = 8
NB = 2
NA = 64


def draw_stored_inputs(key, part):
    first_key = jax.random.fold_in(key, 0)
    shape = (LAYERS, SAMPLES, SEQ, D)
    return jnp.clip(jax.random.normal(first_key, shape, jnp.float32), -6.0, 6.0).astype(jnp.bfloat16)


def draw_region_mask(key, part):
    order = jax.random.permutation(key, SEQ)
    return jnp.zeros((SEQ,), jnp.int32).at[order[:NA]].set(1)


def draw_partner_samples(key, part):
    shard_key, slot_key, other_key, order_key = jax.random.split(jax.random.fold_in(key, 7), 4)
    shard = jax.random.randint(shard_key, (), 0, SHARDS, dtype=jnp.int32)
    slot_first = jax.random.randint(slot_key, (), 0, MB, dtype=jnp.int32)
    slot_second = jax.random.randint(other_key, (), 0, MB, dtype=jnp.int32)
    first = (shard * MB + slot_first).astype(jnp.int32)
    second = ((shard + SHARDS - 1) % SHARDS * MB + slot_second).astype(jnp.int32)
    scores = jax.random.permutation(order_key, SAMPLES).astype(jnp.int32)
    scores = scores.at[first].set(-2).at[second].set(-1)
    order = jnp.argsort(scores, stable=True).astype(jnp.int32)
    firsts = order[0::2]
    seconds = order[1::2]
    swap_partner = jnp.zeros((SAMPLES,), jnp.int32).at[firsts].set(seconds).at[seconds].set(firsts)
    return swap_partner.astype(jnp.int32)


def touch_ends(values, key, least, top_value):
    extent = values.shape
    place = [jax.random.randint(jax.random.fold_in(key, axis), (), 0, extent[axis]) for axis in range(len(extent))]
    values = values.at[tuple(place)].set(least)
    longest = extent.index(max(extent))
    place[longest] = (place[longest] + 1) % extent[longest]
    return values.at[tuple(place)].set(top_value)


def strengthened(entries, own_key, source, target, parts, factor):
    def block_of(dim):
        return (jnp.arange(entries.shape[dim]) // (entries.shape[dim] // parts)).reshape((-1,) + (1,) * (entries.ndim - 1 - dim))

    near = jax.random.permutation(own_key, parts)[block_of(target)]
    far = (block_of(target) + parts // 2) % parts
    return jnp.where((block_of(source) == near) | (block_of(source) == far), factor * entries, entries)


def level_of(key, dims, cuts, least, high):
    factor_of = 1.0
    for position, parts in cuts:
        draws = jax.random.uniform(jax.random.fold_in(jax.random.fold_in(key, 6), position), (parts,), jnp.float32, least / len(cuts), high / len(cuts))
        factor_of = factor_of * jnp.repeat(jnp.exp(draws), dims[position] // parts).reshape((-1,) + (1,) * (len(dims) - 1 - position))
    return factor_of


def bell_draw(own_key, shape, scale, bound, pieces=(), kind=jnp.bfloat16):
    entries = jax.random.normal(own_key, shape, jnp.float32) * scale
    if len(pieces) > 0:
        entries = level_of(own_key, shape, pieces, -0.22, 0.18) * entries
    return jnp.clip(entries, min=-bound, max=bound).astype(kind)


def bell_draw_with(key, shape, width, most, cuts, heavy, kind=jnp.bfloat16):
    result = width * jax.random.normal(key, shape, jnp.float32)
    if cuts:
        result = result * level_of(key, shape, cuts, -0.22, 0.18)
    return jnp.clip(strengthened(result, jax.random.fold_in(key, 3), *heavy), -most, most).astype(kind)


def setup_inputs(seed: int = 0, part: int = 0) -> dict:
    splits = jax.random.split(jax.random.key(seed), 8)
    part_splits = jax.random.split(jax.random.fold_in(splits[7], part), 8)
    stored_inputs = draw_stored_inputs(jax.random.fold_in(jax.random.fold_in(splits[7], part), 71), part)
    top_cotangent = bell_draw_with(part_splits[1], (SAMPLES, SEQ, D), 0.0625, 0.375, ((0, 8), (2, 2)), (0, 2, 8, 2.0))
    layer_weights = bell_draw(splits[2], (LAYERS, D, D), D ** -0.5, 0.125, ((1, 8), (2, 2)))
    block_layout = touch_ends((jax.random.randint(splits[3], (LAYERS, NB, NB), 0, 2) < 1).astype(jnp.int32), jax.random.fold_in(splits[3], 1), 0, 1)
    region_mask = draw_region_mask(jax.random.fold_in(splits[7], 71), part)
    partner_samples = draw_partner_samples(jax.random.fold_in(jax.random.fold_in(splits[7], part), 71), part)
    spins = touch_ends(jax.random.randint(part_splits[6], (SAMPLES, SEQ), 0, SPINS), jax.random.fold_in(part_splits[6], 1), 0, SPINS - 1).astype(jnp.int32)
    return {"stored_inputs": stored_inputs, "top_cotangent": top_cotangent, "layer_weights": layer_weights, "block_layout": block_layout, "region_mask": region_mask, "partner_samples": partner_samples, "spins": spins}


def rounded(value):
    return lax.optimization_barrier(value.astype(jnp.bfloat16)).astype(jnp.float32)


def layer_backward(grad_out, inputs, weight, allowed, attention_scale):
    head_count = D // HEAD
    inputs_h = inputs.astype(jnp.float32).reshape(SAMPLES, SEQ, head_count, HEAD)
    grad_attn = jnp.dot(grad_out.reshape(SAMPLES * SEQ, D), weight, preferred_element_type=jnp.float32)
    grad_attn = rounded(grad_attn).reshape(SAMPLES, SEQ, head_count, HEAD)
    scores = jnp.einsum('bqhd,bkhd->bhqk', inputs_h, inputs_h) * attention_scale
    scores = jnp.where(allowed, scores, -jnp.inf)
    top_score = jnp.max(scores, axis=-1, keepdims=True)
    expo_terms = jnp.exp(scores - top_score)
    probs = expo_terms / jnp.sum(expo_terms, axis=-1, keepdims=True)
    probs_low = rounded(probs)
    attended = rounded(jnp.einsum('bhqk,bkhd->bqhd', probs_low, inputs_h))
    grad_probs = jnp.einsum('bqhd,bkhd->bhqk', grad_attn, inputs_h)
    grad_scores = rounded(probs * (grad_probs - jnp.sum(grad_probs * probs, axis=-1, keepdims=True)))
    grad_in = grad_out.astype(jnp.float32).reshape(SAMPLES, SEQ, head_count, HEAD)
    grad_in = grad_in + jnp.einsum('bhqk,bqhd->bkhd', probs_low, grad_attn)
    grad_in = grad_in + attention_scale * (jnp.einsum('bhqk,bkhd->bqhd', grad_scores, inputs_h) + jnp.einsum('bhqk,bqhd->bkhd', grad_scores, inputs_h))
    return grad_in.reshape(SAMPLES, SEQ, D).astype(jnp.bfloat16), attended.reshape(SAMPLES, SEQ, D).astype(jnp.bfloat16)


def shard_term(total, pair):
    grad_rows, attended_rows = pair
    term = jnp.dot(grad_rows.T, attended_rows, preferred_element_type=jnp.float32)
    return total + rounded(term), None


def reference(stored_inputs, top_cotangent, layer_weights, block_layout, region_mask, partner_samples, spins):
    attention_scale = 4.0 / HEAD
    pos_block = jnp.arange(SEQ) // BLOCK
    grad_now = top_cotangent
    cotangents = [None] * LAYERS
    gradients = [None] * LAYERS
    for layer in reversed(range(LAYERS)):
        allowed = (block_layout[layer][pos_block[:, None], pos_block[None, :]] > 0) | (pos_block[:, None] == pos_block[None, :])
        grad_in, attended = layer_backward(grad_now, stored_inputs[layer], layer_weights[layer], allowed, attention_scale)
        grad_rows = grad_now.reshape(SHARDS, MB * SEQ, D)
        attended_rows = attended.reshape(SHARDS, MB * SEQ, D)
        total, unused = lax.scan(shard_term, jnp.zeros((D, D), jnp.float32), (grad_rows, attended_rows))
        gradients[layer] = total
        cotangents[layer] = grad_in
        grad_now = grad_in
    partner_ids = partner_samples.astype(jnp.int32)
    first = cotangents[0]
    site = jnp.where(region_mask[None, :, None] > 0, first[partner_ids], first)
    cotangents[0] = site
    onehot = (spins[:, :, None] == jnp.arange(SPINS, dtype=jnp.int32)[None, None, :]).astype(jnp.float32)
    embed_grad = jnp.einsum('btv,btd->vd', onehot, site.astype(jnp.float32))
    return jnp.stack(gradients), jnp.stack(cotangents), embed_grad
```

```python
import jax
import jax.numpy as jnp
from jax import lax
from jax.experimental import pallas as pl
from jax.experimental.pallas import tpu as pltpu
from jax.sharding import PartitionSpec as P

HEAD = 128
BLOCK = 64
SPINS = 2


def for_sending(value):

    def short(part):
        return part.astype(jnp.bfloat16) if part.dtype == jnp.float32 else part

    return jax.tree.map(short, value)


def passed_along(block, axis, distance):
    devices = range(lax.axis_size(axis))
    route = [(i - distance, i) for i in devices if i - distance in devices]
    return lax.ppermute(block, axis, route)


def softmax_parts(inputs_h, allowed, attention_scale):
    scores = (
        jnp.einsum("qhd,khd->hqk", inputs_h, inputs_h, preferred_element_type=jnp.float32)
        * attention_scale
    )
    scores = jnp.where(allowed[None], scores, -jnp.inf)
    top_score = jnp.max(scores, axis=-1, keepdims=True)
    expo_terms = jnp.exp(scores - top_score)
    probs = expo_terms / jnp.sum(expo_terms, axis=-1, keepdims=True)
    return (probs, probs.astype(jnp.bfloat16))


def local(
    stored_inputs, top_cotangent, layer_weights, block_layout, region_mask, partner_samples, spins
):
    section_index = lax.axis_index("section")
    section_count = lax.axis_size("section")
    micro_count = stored_inputs.shape[1]
    seq_len = stored_inputs.shape[2]
    half_width = stored_inputs.shape[3]
    head_count = half_width // HEAD
    attention_scale = 4.0 / HEAD
    weights = lax.all_gather(layer_weights[0], "samples", axis=0, tiled=True)
    pos_block = jnp.arange(seq_len) // BLOCK
    block_onehot = (pos_block[:, None] == jnp.arange(block_layout.shape[1])[None, :]).astype(
        jnp.float32
    )
    linked = jnp.dot(jnp.dot(block_onehot, block_layout[0].astype(jnp.float32)), block_onehot.T)
    allowed = (linked > 0.5) | (pos_block[:, None] == pos_block[None, :])
    every_layer_input = stored_inputs[0]
    inputs_h = every_layer_input[0].reshape(seq_len, head_count, HEAD)
    probs, probs_low = softmax_parts(inputs_h, allowed, attention_scale)
    attended = jnp.einsum(
        "hqk,khd->qhd", probs_low, inputs_h, preferred_element_type=jnp.float32
    ).astype(jnp.bfloat16)
    probs_list = [probs]
    low_list = [probs_low]
    attend_list = [attended.reshape(seq_len, half_width)]
    probs_all = jnp.stack(probs_list)
    low_all = jnp.stack(low_list)
    attend_store = jnp.stack(attend_list)

    def layer_back(grad_full, grad_own, inputs, probs, probs_low):
        grad_attn = jnp.dot(grad_full, weights, preferred_element_type=jnp.float32).astype(
            jnp.bfloat16
        )
        inputs_h = inputs.reshape(seq_len, head_count, HEAD)
        grad_h = grad_attn.reshape(seq_len, head_count, HEAD)
        grad_probs = jnp.einsum(
            "qhd,khd->hqk", grad_h, inputs_h, preferred_element_type=jnp.float32
        )
        grad_scores = (
            probs * (grad_probs - jnp.sum(grad_probs * probs, axis=-1, keepdims=True))
        ).astype(jnp.bfloat16)
        through = jnp.einsum("hqk,qhd->khd", probs_low, grad_h, preferred_element_type=jnp.float32)
        through = through + attention_scale * (
            jnp.einsum("hqk,khd->qhd", grad_scores, inputs_h, preferred_element_type=jnp.float32)
            + jnp.einsum("hqk,qhd->khd", grad_scores, inputs_h, preferred_element_type=jnp.float32)
        )
        grad_in = grad_own.astype(jnp.float32) + through.reshape(seq_len, half_width)
        return grad_in.astype(jnp.bfloat16)

    def resting(grad_full, grad_own, inputs, probs, probs_low):
        return jnp.zeros((seq_len, half_width), jnp.bfloat16)

    carried_state = jnp.zeros((seq_len, half_width), jnp.bfloat16)
    out_list = []
    grad_list = []
    total_steps = micro_count + section_count - 1
    for step_number in range(total_steps):
        micro_index = step_number - (section_count - 1 - section_index)
        active = (micro_index >= 0) & (micro_index < micro_count)
        slot_index = jnp.clip(micro_index, 0, micro_count - 1)
        from_top = lax.dynamic_index_in_dim(top_cotangent, slot_index, 0, keepdims=False)
        incoming = jnp.where(section_index == section_count - 1, from_top, carried_state)
        grad_full = lax.all_gather(incoming, "mp", axis=1, tiled=True)
        inputs_now = lax.dynamic_index_in_dim(every_layer_input, slot_index, 0, keepdims=False)
        probs_now = lax.dynamic_index_in_dim(probs_all, slot_index, 0, keepdims=False)
        low_now = lax.dynamic_index_in_dim(low_all, slot_index, 0, keepdims=False)
        grad_in = lax.cond(
            active, layer_back, resting, grad_full, incoming, inputs_now, probs_now, low_now
        )
        out_list.append(grad_in)
        grad_list.append(grad_full)
        if step_number < total_steps - 1:
            carried_state = jax.tree.map(
                lambda part, own: part.astype(own.dtype),
                passed_along(for_sending(grad_in), "section", -1),
                grad_in,
            )
    offset = section_count - 1 - section_index
    out_store = lax.dynamic_slice_in_dim(jnp.stack(out_list), offset, micro_count, 0)
    grad_store = lax.dynamic_slice_in_dim(jnp.stack(grad_list), offset, micro_count, 0)
    summed_weight = lax.psum_scatter(
        jnp.einsum(
            "mtf,mta->fa", grad_store, attend_store, preferred_element_type=jnp.float32
        ).astype(jnp.bfloat16),
        "samples",
        scatter_dimension=0,
        tiled=True,
    ).astype(jnp.float32)
    region_count = seq_len // 2
    place_in = jnp.arange(seq_len)
    rank_in_region = (
        jnp.sum(jnp.where(place_in[None, :] <= place_in[:, None], region_mask[None, :], 0), axis=1) - 1
    )
    select = (
        (rank_in_region[None, :] == jnp.arange(region_count)[:, None]) & (region_mask[None, :] > 0)
    ).astype(jnp.bfloat16)
    tiles = jnp.einsum("at,mtd->mad", select, out_store, preferred_element_type=jnp.float32).astype(
        jnp.bfloat16
    )
    shard_index = lax.axis_index("samples")
    my_partners = lax.dynamic_slice_in_dim(
        partner_samples, shard_index * micro_count, micro_count, 0
    )
    shard_count = lax.axis_size("samples")
    dest_shard = my_partners // micro_count
    dest_slot = my_partners % micro_count
    route = (
        (dest_shard[:, None, None] == jnp.arange(shard_count)[None, :, None])
        & (dest_slot[:, None, None] == jnp.arange(micro_count)[None, None, :])
    ).astype(jnp.bfloat16)
    outgoing = jnp.einsum("mku,mad->kuad", route, tiles, preferred_element_type=jnp.float32).astype(
        jnp.bfloat16
    )
    arrived = lax.all_to_all(outgoing, "samples", split_axis=0, concat_axis=0, tiled=True)
    ones_row = jnp.ones((shard_count,), jnp.bfloat16)
    received = jnp.einsum(
        "k,kuad->uad", ones_row, arrived, preferred_element_type=jnp.float32
    ).astype(jnp.bfloat16)
    placed = jnp.einsum("at,mad->mtd", select, received, preferred_element_type=jnp.float32)
    kept = jnp.where(region_mask[None, :, None] > 0, jnp.zeros_like(out_store), out_store)
    site_cot = (kept.astype(jnp.float32) + placed).astype(jnp.bfloat16)
    cotangents = jnp.where(section_index == 0, site_cot, out_store)
    onehot = (spins[:, :, None] == jnp.arange(SPINS)[None, None, :]).astype(jnp.bfloat16)
    embed_term = jnp.einsum("mtv,mtd->vd", onehot, site_cot, preferred_element_type=jnp.float32)
    embed_term = jnp.where(section_index == 0, embed_term, jnp.zeros_like(embed_term))
    embed_grad = lax.psum(embed_term, ("samples", "section"))
    return (summed_weight[None], cotangents[None], embed_grad)


NZ = 4
NC = 4
GROUPS = ((0, 1), (2,), (3,))
END_ORDER = (
    ("attE", 0), ("ga",), ("p2", 0), ("s2", 0), ("gb",), ("p01", 0),
    ("s0", 0), ("s1", 0), ("p2", 1), ("p01", 1), ("s0", 1), ("s1", 1),
    ("s2", 1), ("attE", 1), ("p2", 2), ("p01", 2), ("s0", 2), ("s1", 2),
    ("s2", 2), ("attE", 2), ("p2", 3), ("p01", 3), ("s0", 3), ("s1", 3),
    ("s2", 3), ("attE", 3), ("back", 0), ("back", 1), ("across", 0), ("back", 2),
    ("across", 1), ("emb",), ("across", 2), ("wt", 0), ("wt", 1), ("wt", 2),
    ("wt", 3), ("fin", 0), ("fin", 1), ("fin", 2), ("finw",),
)
INNER_ORDER = (
    ("gather",), ("attIi", 0), ("attIo", 0), ("part", 0), ("far0", 0), ("far1", 0),
    ("r3", 0), ("r1", 0), ("attIi", 1), ("attIo", 1), ("part", 1), ("far0", 1),
    ("far1", 1), ("r3", 1), ("r1", 1), ("near", 0), ("r0", 0), ("attIi", 2),
    ("attIo", 2), ("part", 2), ("far0", 2), ("far1", 2), ("r3", 2), ("r1", 2),
    ("near", 1), ("r0", 1), ("attIi", 3), ("attIo", 3), ("part", 3), ("far0", 3),
    ("far1", 3), ("r3", 3), ("r1", 3), ("near", 2), ("r0", 2), ("near", 3),
    ("r0", 3), ("back", 0), ("back", 1), ("across", 0), ("back", 2), ("across", 1),
    ("emb",), ("across", 2), ("wt", 0), ("wt", 1), ("wt", 2), ("wt", 3),
    ("fin", 0), ("fin", 1), ("fin", 2), ("finw",),
)
MESH = pl.DeviceIdType.MESH
F32 = jnp.float32
BF = jnp.bfloat16
T = jax.named_scope


def dot(a, b, ca=1, cb=0):
    return lax.dot_general(a, b, (((ca,), (cb,)), ((), ())), preferred_element_type=F32)


def kernel(
    x_hbm, g_hbm, w_hbm, layout_hbm, mask_hbm, partner_hbm, spin_hbm,
    wg_ref, cot_ref, emb_ref,
    x_ref, g_ref, layout_ref, mask_ref, partner_ref, spin_ref, gq, w2, pf, pb, near_in, far_in, att, probs, ga, g0,
    swz, xsend, xrecv, spall, embs, wsend, wrecv, wown,
    in_s, gq_s, gq_r, gf_s, gf_r, w_s, w_r, sp_s, sp_r, in_at_s, out_at_s, at_r, ps_s, near_r, far_r,
    sw_s, sw_r, xs_s, xs_r, em_s, em_r, wr_s, wr_r,
):
    s = lax.axis_index("samples")
    m = lax.axis_index("mp")
    z = s // 2
    x = s % 2
    flip = z < NZ // 2
    is_end = (z == 0) | (z == NZ - 1)
    outward = jnp.where(flip, -2, 2)
    scale = 4.0 / HEAD
    tokens, width = x_ref.shape
    heads = width // HEAD
    rows = w_hbm.shape[0]
    half = width // 2
    wide = width // NC
    per = wide // HEAD
    sibling = {"mp": 1 - m}
    beside = {"samples": 2 * z + 1 - x}
    inner_way = {"samples": lax.rem(s - outward + 8, 8)}
    outer_way = {"samples": lax.rem(s + outward + 8, 8)}

    def actual(n):
        return jnp.where(flip, NZ - 1 - n, n)

    def rdma(src, dst, ss, rs, dev):
        return pltpu.make_async_remote_copy(
            src_ref=src, dst_ref=dst, send_sem=ss, recv_sem=rs, device_id=dev, device_id_type=MESH
        )

    def send(cond, make):
        if cond is None:
            make().start()
        else:
            pl.when(cond)(lambda: make().start())

    def sent(cond, src, ss):
        def wait():
            rdma(src, src, ss, ss, sibling).wait_send()

        if cond is None:
            wait()
        else:
            pl.when(cond)(wait)

    def got(cond, dst, rs):
        def wait():
            rdma(dst, dst, rs, rs, sibling).wait_recv()

        if cond is None:
            wait()
        else:
            pl.when(cond)(wait)

    loads = [
        pltpu.make_async_copy(g_hbm, g_ref, in_s.at[0]),
        pltpu.make_async_copy(w_hbm, w2.at[x], in_s.at[1]),
        pltpu.make_async_copy(x_hbm, x_ref, in_s.at[2]),
        pltpu.make_async_copy(spin_hbm, spin_ref, in_s.at[3]),
        pltpu.make_async_copy(layout_hbm, layout_ref, in_s.at[4]),
        pltpu.make_async_copy(mask_hbm, mask_ref, in_s.at[5]),
        pltpu.make_async_copy(partner_hbm, partner_ref, in_s.at[6]),
    ]
    for load in loads:
        load.start()
    barrier = pltpu.get_barrier_semaphore()
    for k in range(1, 8):
        pl.semaphore_signal(
            barrier, inc=1, device_id={"samples": lax.rem(s + k, 8)}, device_id_type=MESH
        )
    pl.semaphore_signal(barrier, inc=1, device_id=sibling, device_id_type=MESH)
    for load in loads:
        load.wait()

    qb = lax.broadcasted_iota(jnp.int32, (tokens, tokens), 0) // BLOCK
    kb = lax.broadcasted_iota(jnp.int32, (tokens, tokens), 1) // BLOCK
    linked = jnp.where(qb < kb, layout_ref[0, 1], layout_ref[1, 0])
    allowed = (qb == kb) | (linked > 0)

    def attention():
        for h in range(heads):
            xh = x_ref[:, pl.ds(h * HEAD, HEAD)]
            scores = jnp.where(allowed, dot(xh, xh, 1, 1) * scale, -jnp.inf)
            expo = jnp.exp(scores - jnp.max(scores, axis=-1, keepdims=True))
            p = expo / jnp.sum(expo, axis=-1, keepdims=True)
            probs[h] = p
            att[h // per, z, :, pl.ds(h % per * HEAD, HEAD)] = dot(p.astype(BF), xh).astype(BF)

    @pl.when(flip)
    def _():
        with T("attn"):
            attention()

    with T("barrier"):
        pl.semaphore_wait(barrier, 8)

    for far in (False, True):
        jj = m if far else 1 - m
        dz = 2 * m + jj
        for_me = dz == z
        columns = pl.ds(pl.multiple_of(jj * half, half), half)
        piece = g_ref.at[:, columns]
        send(
            jnp.logical_not(for_me),
            lambda piece=piece, dz=dz: rdma(
                piece, gq.at[z], gq_s, gq_r.at[z], {"samples": 2 * dz + x}
            ),
        )
        send(
            for_me,
            lambda piece=piece: rdma(piece, gq.at[z], gq_s, gf_r.at[z], sibling),
        )

        @pl.when(for_me)
        def _(columns=columns):
            gq[z] = g_ref[:, columns]

    for c in range(NC):
        block = w2.at[x, :, pl.ds(c * wide, wide)]
        send(None, lambda block=block, c=c: rdma(block, block, w_s, w_r.at[c], beside))
    for k in range(1, 8):
        other = lax.rem(s + k, 8)
        send(
            None,
            lambda other=other: rdma(spin_ref, spall.at[s], sp_s, sp_r, {"samples": other}),
        )
    spall[s] = spin_ref[...]

    @pl.when(jnp.logical_not(flip))
    def _():
        with T("attn"):
            attention()

    mask = mask_ref[...]
    tri = (
        lax.broadcasted_iota(jnp.int32, (tokens, tokens), 0)
        <= lax.broadcasted_iota(jnp.int32, (tokens, tokens), 1)
    ).astype(F32).astype(BF)
    mask_rows = jnp.broadcast_to(mask, (8, tokens)).astype(F32)
    rank = dot(mask_rows.astype(BF), tri)[:1] - 1.0
    region = tokens // 2
    place = lax.broadcasted_iota(jnp.int32, (region, tokens), 0).astype(F32)
    select = jnp.where((rank == place) & (mask > 0), 1.0, 0.0).astype(BF)

    first_core = m == z // 2

    def gather(order, own):
        for n in order:
            zz = actual(n)
            got(first_core, gq.at[zz], gq_r.at[zz])
            send(
                first_core,
                lambda zz=zz: rdma(gq.at[zz], gq.at[zz], gf_s, gf_r.at[zz], sibling),
            )
        for n in (own, *order) if own else order:
            zz = actual(n)
            got(jnp.logical_not(first_core), gq.at[zz], gf_r.at[zz])

    def att_to(c, n, slot, inward):
        zz = actual(n)
        way, ss = (inner_way, in_at_s) if inward else (outer_way, out_at_s)
        send(None, lambda: rdma(att.at[c, zz], att.at[c, zz], ss, at_r.at[c, slot], way))

    def att_got(c, n, slot):
        got(None, att.at[c, actual(n)], at_r.at[c, slot])

    def weights_in(c):
        got(None, w2.at[1 - x, :, pl.ds(c * wide, wide)], w_r.at[c])

    def partials(c, first, count):
        cols = pl.ds(c * wide, wide)
        some = gq[pl.ds(first, count)].reshape(count * tokens, 2 * rows)
        sums = dot(some[:, :rows], w2[0, :, cols]) + dot(some[:, rows:], w2[1, :, cols])
        return sums.reshape(count, tokens, wide)

    def weight_terms(c):
        total = jnp.zeros((2 * rows, wide), F32)
        for zz in range(NZ):
            total += dot(gq[zz], att[c, zz], 0, 0).astype(BF).astype(F32)
        cols = pl.ds(c * wide, wide)

        @pl.when(x == 0)
        def _():
            wown[:, cols] = total[:rows]
            wsend[c] = total[rows:].astype(BF)

        @pl.when(x == 1)
        def _():
            wown[:, cols] = total[rows:]
            wsend[c] = total[:rows].astype(BF)

        send(None, lambda: rdma(wsend.at[c], wrecv.at[c], wr_s, wr_r, beside))

    def backward(b, total_of):
        chunks = GROUPS[b]
        for c in chunks:
            ga[:, c * wide : (c + 1) * wide] = total_of(c).astype(BF)
        for h in range(chunks[0] * per, (chunks[-1] + 1) * per):
            cols = slice(h * HEAD, (h + 1) * HEAD)
            xh = x_ref[:, cols]
            gh = ga[:, cols]
            p = probs[h]
            gp = dot(gh, xh, 1, 1)
            gs = (p * (gp - jnp.sum(gp * p, axis=-1, keepdims=True))).astype(BF)
            through = dot(p.astype(BF), gh, 0, 0) + scale * (dot(gs, xh) + dot(gs, xh, 0, 0))
            g0[:, cols] = (g_ref[:, cols].astype(F32) + through).astype(BF)
        for c in chunks:
            swz[c, s % 4] = dot(select, g0[:, c * wide : (c + 1) * wide]).astype(BF)
        part = pl.ds(chunks[0], len(chunks))
        for k in (3, 2, 1):
            other = s // 4 * 4 + lax.rem(s + k, 4)
            rows_now = swz.at[part, s % 4]
            send(
                None,
                lambda rows_now=rows_now, other=other: rdma(
                    rows_now, rows_now, sw_s, sw_r.at[b, s % 4], {"samples": other}
                ),
            )

    def rows_of(c, which):
        rows_now = swz[c, 0]
        for k in range(1, 4):
            rows_now = jnp.where(which == k, swz[c, k], rows_now)
        return rows_now

    def across(b):
        part = pl.ds(GROUPS[b][0], len(GROUPS[b]))
        for k in range(1, 4):
            got(None, swz.at[part, 0], sw_r.at[b, lax.rem(s + k, 4)])
        dest = lax.rem(s + 4, 8)
        wanted = lax.rem(partner_ref[dest], 4)
        for c in GROUPS[b]:
            xsend[c] = rows_of(c, wanted)
        send(
            None,
            lambda: rdma(xsend.at[part], xrecv.at[part], xs_s, xs_r.at[b], {"samples": dest}),
        )

    def embed():
        got(None, spall.at[pl.ds(0, 7)], sp_r)
        spins = jnp.where(mask > 0, spall[partner_ref[s]], spin_ref[...])
        onehot = jnp.where(
            spins == lax.broadcasted_iota(jnp.int32, (8, tokens), 0), 1.0, 0.0
        ).astype(BF)
        embs[s] = dot(onehot, g0[...])[:SPINS]
        for k in range(1, 8):
            other = lax.rem(s + k, 8)
            send(
                None,
                lambda other=other: rdma(embs.at[s], embs.at[s], em_s, em_r, {"samples": other}),
            )

    mine = partner_ref[s]
    eye = lax.broadcasted_iota(jnp.int32, (tokens, tokens), 0) == lax.broadcasted_iota(
        jnp.int32, (tokens, tokens), 1
    )
    keep = jnp.where(eye & (mask == 0), 1.0, 0.0).astype(BF)

    def rows_in(b):
        chunks = GROUPS[b]
        got(None, xrecv.at[pl.ds(chunks[0], len(chunks))], xs_r.at[b])
        for c in chunks:
            cols = slice(c * wide, (c + 1) * wide)
            chosen = jnp.where(mine // 4 == s // 4, rows_of(c, lax.rem(mine, 4)), xrecv[c])
            cot_ref[:, cols] = (dot(keep, g0[:, cols]) + dot(select, chosen, 0, 0)).astype(BF)

    def weights_out():
        got(None, wrecv, wr_r)
        for c in range(NC):
            cols = slice(c * wide, (c + 1) * wide)
            wg_ref[:, cols] = wown[:, cols] + wrecv[c].astype(F32)

    def end_tasks():
        def total_of(c):
            got(None, far_in.at[c, 0], far_r.at[c, 0])
            return pf[c, actual(3)] + far_in[c, 0].astype(F32)

        def part_out(c, n):
            zz = actual(n)
            send(
                None,
                lambda: rdma(
                    pb.at[c, zz], near_in.at[c, n], ps_s, near_r.at[c, n], inner_way
                ),
            )

        weights_seen = set()

        def weights(c):
            if c not in weights_seen:
                weights_seen.add(c)
                weights_in(c)

        def p2(c):
            weights(c)
            first = jnp.where(flip, 0, 2)
            sums = partials(c, first, 2)
            pf[c, pl.ds(first, 2)] = sums
            pb[c, pl.ds(first, 2)] = sums.astype(BF)

        def p01(c):
            weights(c)
            first = jnp.where(flip, 2, 0)
            pb[c, pl.ds(first, 2)] = partials(c, first, 2).astype(BF)

        def wt(c):
            for slot in range(3):
                att_got(c, 2 - slot, slot)
            weight_terms(c)

        return {
            "ga": lambda: gather((2,), 3),
            "gb": lambda: gather((1, 0), None),
            "attE": lambda c: att_to(c, 3, 0, True),
            "s0": lambda c: part_out(c, 0), "s1": lambda c: part_out(c, 1), "s2": lambda c: part_out(c, 2),
            "p2": p2, "p01": p01, "wt": wt,
            "back": lambda b: backward(b, total_of),
            "across": across, "emb": embed, "fin": rows_in, "finw": weights_out,
        }

    def inner_tasks():
        def total_of(c):
            got(None, near_in.at[c, 2], near_r.at[c, 2])
            got(None, far_in.at[c, 1], far_r.at[c, 1])
            return pf[c, actual(2)] + near_in[c, 2].astype(F32) + far_in[c, 1].astype(F32)

        def part(c):
            weights_in(c)
            pf[c] = partials(c, 0, NZ)

        def far(c, n):
            got(None, near_in.at[c, n], near_r.at[c, n])
            pb[c, n] = (pf[c, actual(n)] + near_in[c, n].astype(F32)).astype(BF)
            send(
                None,
                lambda: rdma(pb.at[c, n], far_in.at[c, n], ps_s, far_r.at[c, n], inner_way),
            )

        def near(c):
            got(None, far_in.at[c, 0], far_r.at[c, 0])
            pb[c, 3] = (pf[c, actual(3)] + far_in[c, 0].astype(F32)).astype(BF)
            send(
                None,
                lambda: rdma(pb.at[c, 3], far_in.at[c, 0], ps_s, far_r.at[c, 0], outer_way),
            )

        def relay(n, slot, to_slot, inward):
            def run(c):
                att_got(c, n, slot)
                att_to(c, n, to_slot, inward)

            return run

        return {
            "gather": lambda: gather((3, 1, 0), 2),
            "attIi": lambda c: att_to(c, 2, 1, True), "attIo": lambda c: att_to(c, 2, 0, False),
            "part": part, "near": near,
            "far0": lambda c: far(c, 0), "far1": lambda c: far(c, 1),
            "r3": relay(3, 0, 2, True),
            "r1": relay(1, 1, 1, False),
            "r0": relay(0, 2, 2, False),
            "wt": weight_terms, "back": lambda b: backward(b, total_of),
            "across": across, "emb": embed, "fin": rows_in, "finw": weights_out,
        }

    def run(tasks, order):
        for name, *at in order:
            with T("_".join([name, *map(str, at)])):
                tasks[name](*at)

    @pl.when(is_end)
    def _():
        run(end_tasks(), END_ORDER)
        sent(None, att.at[:, 0], in_at_s)

    @pl.when(jnp.logical_not(is_end))
    def _():
        run(inner_tasks(), INNER_ORDER)
        sent(None, att.at[:, pl.ds(0, 2)], in_at_s)
        sent(None, att.at[:, pl.ds(0, 3)], out_at_s)

    with T("embw"):
        got(None, embs.at[pl.ds(0, 7)], em_r)
    total = embs[0]
    for k in range(1, 8):
        total += embs[k]
    emb_ref[...] = total
    with T("sends_done"):
        sent(None, g_ref, gq_s)
        sent(first_core, gq.at[pl.ds(0, 3)], gf_s)
        sent(None, w2.at[0], w_s)
        sent(None, spall.at[pl.ds(0, 7)], sp_s)
        sent(None, embs.at[pl.ds(0, 7)], em_s)
        sent(None, pb.at[:, pl.ds(0, 3)], ps_s)
        sent(None, swz.at[:, pl.ds(0, 3)], sw_s)
        sent(None, xsend, xs_s)
        sent(None, wsend, wr_s)


def put_out(wg_ref, cot_ref, emb_ref, wg_out, cot_out, emb_out, done):
    copies = [
        pltpu.make_async_copy(wg_ref, wg_out, done.at[0]),
        pltpu.make_async_copy(cot_ref, cot_out, done.at[1]),
        pltpu.make_async_copy(emb_ref, emb_out, done.at[2]),
    ]
    for copy in copies:
        copy.start()
    for copy in copies:
        copy.wait()


def one_layer(
    stored_inputs, top_cotangent, layer_weights, block_layout, region_mask, partner_samples, spins
):
    tokens, width = stored_inputs.shape[2:]
    rows = layer_weights.shape[1]
    hbm = pl.BlockSpec(memory_space=pltpu.HBM)
    vmem = pl.BlockSpec(memory_space=pltpu.VMEM)
    region = tokens // 2
    dma = pltpu.SemaphoreType.DMA
    half = width // 2
    wide = width // NC
    shapes = [
        ((NZ, tokens, 2 * rows), BF),
        ((2, rows, width), BF),
        ((NC, NZ, tokens, wide), F32),
        ((NC, NZ, tokens, wide), BF),
        ((NC, 3, tokens, wide), BF),
        ((NC, 2, tokens, wide), BF),
        ((NC, NZ, tokens, wide), BF),
        ((width // HEAD, tokens, tokens), F32),
        ((tokens, width), BF),
        ((tokens, width), BF),
        ((NC, 4, region, wide), BF),
        ((NC, region, wide), BF),
        ((NC, region, wide), BF),
        ((8, 1, tokens), jnp.int32),
        ((8, SPINS, width), F32),
        ((NC, rows, wide), BF),
        ((NC, rows, wide), BF),
        ((rows, width), F32),
    ]
    one = dma
    sems = [
        dma((7,)), one, dma((NZ,)), one, dma((NZ,)), one, dma((NC,)), one, one, one, one, dma((NC, 3)), one,
        dma((NC, 3)), dma((NC, 2)), one, dma((len(GROUPS), 4)), one, dma((len(GROUPS),)), one, one, one, one,
    ]
    wg, cot, emb = pl.pallas_call(
        kernel,
        out_shape=[
            jax.ShapeDtypeStruct((rows, width), F32),
            jax.ShapeDtypeStruct((tokens, width), BF),
            jax.ShapeDtypeStruct((SPINS, width), F32),
        ],
        in_specs=[hbm] * 7,
        out_specs=[vmem] * 3,
        scratch_shapes=[
            pltpu.VMEM((tokens, width), BF),
            pltpu.VMEM((tokens, width), BF),
            pltpu.SMEM((2, 2), jnp.int32),
            pltpu.VMEM((1, tokens), jnp.int32),
            pltpu.SMEM((8,), jnp.int32),
            pltpu.VMEM((1, tokens), jnp.int32),
        ]
        + [pltpu.VMEM(a, b) for a, b in shapes]
        + sems,
        compiler_params=pltpu.CompilerParams(
            collective_id=0, has_side_effects=True, vmem_limit_bytes=48 * 1024 * 1024
        ),
    )(
        *[
            pltpu.with_memory_space_constraint(value, pltpu.HBM)
            for value in (
                stored_inputs[0, 0], top_cotangent[0], layer_weights[0], block_layout[0],
                region_mask[None], partner_samples, spins,
            )
        ]
    )
    anywhere = pl.BlockSpec(memory_space=pl.ANY)
    wg, cot, emb = pl.pallas_call(
        put_out,
        out_shape=[jax.ShapeDtypeStruct(a.shape, a.dtype) for a in (wg, cot, emb)],
        in_specs=[vmem] * 3,
        out_specs=[anywhere] * 3,
        scratch_shapes=[dma((3,))],
        compiler_params=pltpu.CompilerParams(vmem_limit_bytes=8 * 1024 * 1024),
    )(wg, cot, emb)
    return wg[None], cot[None, None], emb


def solution(mesh):
    in_specs = (
        P("section", ("groups", "samples"), None, "mp"),
        P(("groups", "samples"), None, "mp"),
        P("section", "samples", "mp"),
        P("section", None, None),
        P(),
        P("groups"),
        P(("groups", "samples"), None),
    )
    out_specs = (
        P(("groups", "section"), "samples", "mp"),
        P("section", ("groups", "samples"), None, "mp"),
        P("groups", "mp"),
    )
    small = mesh.shape["samples"] == 8 and mesh.shape["section"] == 1 and mesh.shape["mp"] == 2
    body = one_layer if small else local
    return jax.shard_map(body, mesh=mesh, in_specs=in_specs, out_specs=out_specs, check_vma=False)
```

```python
import jax
import jax.numpy as jnp
from jax import lax
from jax.experimental import pallas as pl
from jax.experimental.pallas import tpu as pltpu
from jax.sharding import PartitionSpec as P

HEAD = 128
BLOCK = 64
SPINS = 2


def for_sending(value):

    def short(part):
        return part.astype(jnp.bfloat16) if part.dtype == jnp.float32 else part

    return jax.tree.map(short, value)


def passed_along(block, axis, distance):
    devices = range(lax.axis_size(axis))
    route = [(i - distance, i) for i in devices if i - distance in devices]
    return lax.ppermute(block, axis, route)


def softmax_parts(inputs_h, allowed, attention_scale):
    scores = (
        jnp.einsum("qhd,khd->hqk", inputs_h, inputs_h, preferred_element_type=jnp.float32)
        * attention_scale
    )
    scores = jnp.where(allowed[None], scores, -jnp.inf)
    top_score = jnp.max(scores, axis=-1, keepdims=True)
    expo_terms = jnp.exp(scores - top_score)
    probs = expo_terms / jnp.sum(expo_terms, axis=-1, keepdims=True)
    return (probs, probs.astype(jnp.bfloat16))


def local(
    stored_inputs, top_cotangent, layer_weights, block_layout, region_mask, partner_samples, spins
):
    section_index = lax.axis_index("section")
    section_count = lax.axis_size("section")
    micro_count = stored_inputs.shape[1]
    seq_len = stored_inputs.shape[2]
    half_width = stored_inputs.shape[3]
    head_count = half_width // HEAD
    attention_scale = 4.0 / HEAD
    weights = lax.all_gather(layer_weights[0], "samples", axis=0, tiled=True)
    pos_block = jnp.arange(seq_len) // BLOCK
    block_onehot = (pos_block[:, None] == jnp.arange(block_layout.shape[1])[None, :]).astype(
        jnp.float32
    )
    linked = jnp.dot(jnp.dot(block_onehot, block_layout[0].astype(jnp.float32)), block_onehot.T)
    allowed = (linked > 0.5) | (pos_block[:, None] == pos_block[None, :])
    every_layer_input = stored_inputs[0]
    inputs_h = every_layer_input[0].reshape(seq_len, head_count, HEAD)
    probs, probs_low = softmax_parts(inputs_h, allowed, attention_scale)
    attended = jnp.einsum(
        "hqk,khd->qhd", probs_low, inputs_h, preferred_element_type=jnp.float32
    ).astype(jnp.bfloat16)
    probs_list = [probs]
    low_list = [probs_low]
    attend_list = [attended.reshape(seq_len, half_width)]
    probs_all = jnp.stack(probs_list)
    low_all = jnp.stack(low_list)
    attend_store = jnp.stack(attend_list)

    def layer_back(grad_full, grad_own, inputs, probs, probs_low):
        grad_attn = jnp.dot(grad_full, weights, preferred_element_type=jnp.float32).astype(
            jnp.bfloat16
        )
        inputs_h = inputs.reshape(seq_len, head_count, HEAD)
        grad_h = grad_attn.reshape(seq_len, head_count, HEAD)
        grad_probs = jnp.einsum(
            "qhd,khd->hqk", grad_h, inputs_h, preferred_element_type=jnp.float32
        )
        grad_scores = (
            probs * (grad_probs - jnp.sum(grad_probs * probs, axis=-1, keepdims=True))
        ).astype(jnp.bfloat16)
        through = jnp.einsum("hqk,qhd->khd", probs_low, grad_h, preferred_element_type=jnp.float32)
        through = through + attention_scale * (
            jnp.einsum("hqk,khd->qhd", grad_scores, inputs_h, preferred_element_type=jnp.float32)
            + jnp.einsum("hqk,qhd->khd", grad_scores, inputs_h, preferred_element_type=jnp.float32)
        )
        grad_in = grad_own.astype(jnp.float32) + through.reshape(seq_len, half_width)
        return grad_in.astype(jnp.bfloat16)

    def resting(grad_full, grad_own, inputs, probs, probs_low):
        return jnp.zeros((seq_len, half_width), jnp.bfloat16)

    carried_state = jnp.zeros((seq_len, half_width), jnp.bfloat16)
    out_list = []
    grad_list = []
    total_steps = micro_count + section_count - 1
    for step_number in range(total_steps):
        micro_index = step_number - (section_count - 1 - section_index)
        active = (micro_index >= 0) & (micro_index < micro_count)
        slot_index = jnp.clip(micro_index, 0, micro_count - 1)
        from_top = lax.dynamic_index_in_dim(top_cotangent, slot_index, 0, keepdims=False)
        incoming = jnp.where(section_index == section_count - 1, from_top, carried_state)
        grad_full = lax.all_gather(incoming, "mp", axis=1, tiled=True)
        inputs_now = lax.dynamic_index_in_dim(every_layer_input, slot_index, 0, keepdims=False)
        probs_now = lax.dynamic_index_in_dim(probs_all, slot_index, 0, keepdims=False)
        low_now = lax.dynamic_index_in_dim(low_all, slot_index, 0, keepdims=False)
        grad_in = lax.cond(
            active, layer_back, resting, grad_full, incoming, inputs_now, probs_now, low_now
        )
        out_list.append(grad_in)
        grad_list.append(grad_full)
        if step_number < total_steps - 1:
            carried_state = jax.tree.map(
                lambda part, own: part.astype(own.dtype),
                passed_along(for_sending(grad_in), "section", -1),
                grad_in,
            )
    offset = section_count - 1 - section_index
    out_store = lax.dynamic_slice_in_dim(jnp.stack(out_list), offset, micro_count, 0)
    grad_store = lax.dynamic_slice_in_dim(jnp.stack(grad_list), offset, micro_count, 0)
    summed_weight = lax.psum_scatter(
        jnp.einsum(
            "mtf,mta->fa", grad_store, attend_store, preferred_element_type=jnp.float32
        ).astype(jnp.bfloat16),
        "samples",
        scatter_dimension=0,
        tiled=True,
    ).astype(jnp.float32)
    region_count = seq_len // 2
    place_in = jnp.arange(seq_len)
    rank_in_region = (
        jnp.sum(jnp.where(place_in[None, :] <= place_in[:, None], region_mask[None, :], 0), axis=1) - 1
    )
    select = (
        (rank_in_region[None, :] == jnp.arange(region_count)[:, None]) & (region_mask[None, :] > 0)
    ).astype(jnp.bfloat16)
    tiles = jnp.einsum("at,mtd->mad", select, out_store, preferred_element_type=jnp.float32).astype(
        jnp.bfloat16
    )
    shard_index = lax.axis_index("samples")
    my_partners = lax.dynamic_slice_in_dim(
        partner_samples, shard_index * micro_count, micro_count, 0
    )
    shard_count = lax.axis_size("samples")
    dest_shard = my_partners // micro_count
    dest_slot = my_partners % micro_count
    route = (
        (dest_shard[:, None, None] == jnp.arange(shard_count)[None, :, None])
        & (dest_slot[:, None, None] == jnp.arange(micro_count)[None, None, :])
    ).astype(jnp.bfloat16)
    outgoing = jnp.einsum("mku,mad->kuad", route, tiles, preferred_element_type=jnp.float32).astype(
        jnp.bfloat16
    )
    arrived = lax.all_to_all(outgoing, "samples", split_axis=0, concat_axis=0, tiled=True)
    ones_row = jnp.ones((shard_count,), jnp.bfloat16)
    received = jnp.einsum(
        "k,kuad->uad", ones_row, arrived, preferred_element_type=jnp.float32
    ).astype(jnp.bfloat16)
    placed = jnp.einsum("at,mad->mtd", select, received, preferred_element_type=jnp.float32)
    kept = jnp.where(region_mask[None, :, None] > 0, jnp.zeros_like(out_store), out_store)
    site_cot = (kept.astype(jnp.float32) + placed).astype(jnp.bfloat16)
    cotangents = jnp.where(section_index == 0, site_cot, out_store)
    onehot = (spins[:, :, None] == jnp.arange(SPINS)[None, None, :]).astype(jnp.bfloat16)
    embed_term = jnp.einsum("mtv,mtd->vd", onehot, site_cot, preferred_element_type=jnp.float32)
    embed_term = jnp.where(section_index == 0, embed_term, jnp.zeros_like(embed_term))
    embed_grad = lax.psum(embed_term, ("samples", "section"))
    return (summed_weight[None], cotangents[None], embed_grad)


NZ = 4
NC = 4
GROUPS = ((0, 1), (2,), (3,))
END_ORDER = (
    ("attE", 0), ("attE", 1), ("ga",), ("attE", 2), ("p2", 1), ("gb",),
    ("attE", 3), ("p01", 0), ("s0", 0), ("p01", 1), ("s1", 1), ("p2", 2),
    ("s0", 1), ("p01", 2), ("p2", 3), ("p01", 3), ("s1", 0), ("s1", 3),
    ("s0", 3), ("s0", 2), ("p2", 0), ("s2", 1), ("s2", 0), ("wt", 0),
    ("wt", 2), ("s1", 2), ("s2", 3), ("s2", 2), ("back", 0), ("back", 2),
    ("wt", 1), ("across", 0), ("back", 1), ("emb",), ("wt", 3), ("across", 1),
    ("across", 2), ("fin", 2), ("fin", 0), ("fin", 1), ("finw",),
)
INNER_ORDER = (
    ("gather",), ("attIi", 2), ("attIo", 0), ("attIo", 1), ("attIi", 1), ("attIi", 0),
    ("r3", 0), ("part", 0), ("attIo", 2), ("r1", 1), ("r3", 1), ("r1", 0),
    ("r1", 2), ("r0", 0), ("r3", 2), ("r3", 3), ("r0", 1), ("part", 2),
    ("far0", 0), ("part", 1), ("wt", 0), ("far0", 1), ("r0", 2), ("part", 3),
    ("wt", 1), ("far1", 1), ("near", 0), ("far1", 0), ("far0", 3), ("near", 1),
    ("wt", 2), ("attIi", 3), ("r0", 3), ("attIo", 3), ("far0", 2), ("near", 3),
    ("far1", 3), ("back", 0), ("near", 2), ("far1", 2), ("r1", 3), ("back", 2),
    ("back", 1), ("emb",), ("wt", 3), ("across", 0), ("across", 2), ("across", 1),
    ("fin", 0), ("fin", 1), ("fin", 2), ("finw",),
)
MESH = pl.DeviceIdType.MESH
F32 = jnp.float32
BF = jnp.bfloat16
T = jax.named_scope


def dot(a, b, ca=1, cb=0):
    return lax.dot_general(a, b, (((ca,), (cb,)), ((), ())), preferred_element_type=F32)


def kernel(
    x_hbm, g_hbm, w_hbm, layout_hbm, mask_hbm, partner_hbm, spin_hbm,
    wg_ref, cot_ref, emb_ref,
    x_ref, g_ref, layout_ref, mask_ref, partner_ref, spin_ref, gq, w2, pf, pb, near_in, far_in, att, probs, ga, g0,
    swz, xsend, xrecv, spall, embs, wsend, wrecv, wown,
    in_s, gq_s, gq_r, gf_s, gf_r, w_s, w_r, sp_s, sp_r, in_at_s, out_at_s, at_r, ps_s, near_r, far_r,
    sw_s, sw_r, xs_s, xs_r, em_s, em_r, wr_s, wr_r,
):
    s = lax.axis_index("samples")
    m = lax.axis_index("mp")
    z = s // 2
    x = s % 2
    flip = z < NZ // 2
    is_end = (z == 0) | (z == NZ - 1)
    outward = jnp.where(flip, -2, 2)
    scale = 4.0 / HEAD
    tokens, width = x_ref.shape
    heads = width // HEAD
    rows = w_hbm.shape[0]
    half = width // 2
    wide = width // NC
    per = wide // HEAD
    sibling = {"mp": 1 - m}
    beside = {"samples": 2 * z + 1 - x}
    inner_way = {"samples": lax.rem(s - outward + 8, 8)}
    outer_way = {"samples": lax.rem(s + outward + 8, 8)}

    def actual(n):
        return jnp.where(flip, NZ - 1 - n, n)

    def rdma(src, dst, ss, rs, dev):
        return pltpu.make_async_remote_copy(
            src_ref=src, dst_ref=dst, send_sem=ss, recv_sem=rs, device_id=dev, device_id_type=MESH
        )

    def send(cond, make):
        if cond is None:
            make().start()
        else:
            pl.when(cond)(lambda: make().start())

    def sent(cond, src, ss):
        def wait():
            rdma(src, src, ss, ss, sibling).wait_send()

        if cond is None:
            wait()
        else:
            pl.when(cond)(wait)

    def got(cond, dst, rs):
        def wait():
            rdma(dst, dst, rs, rs, sibling).wait_recv()

        if cond is None:
            wait()
        else:
            pl.when(cond)(wait)

    loads = [
        pltpu.make_async_copy(g_hbm, g_ref, in_s.at[0]),
        pltpu.make_async_copy(w_hbm, w2.at[x], in_s.at[1]),
        pltpu.make_async_copy(x_hbm, x_ref, in_s.at[2]),
        pltpu.make_async_copy(spin_hbm, spin_ref, in_s.at[3]),
        pltpu.make_async_copy(layout_hbm, layout_ref, in_s.at[4]),
        pltpu.make_async_copy(mask_hbm, mask_ref, in_s.at[5]),
        pltpu.make_async_copy(partner_hbm, partner_ref, in_s.at[6]),
    ]
    for load in loads:
        load.start()
    barrier = pltpu.get_barrier_semaphore()
    for k in range(1, 8):
        pl.semaphore_signal(
            barrier, inc=1, device_id={"samples": lax.rem(s + k, 8)}, device_id_type=MESH
        )
    pl.semaphore_signal(barrier, inc=1, device_id=sibling, device_id_type=MESH)
    for load in loads:
        load.wait()

    qb = lax.broadcasted_iota(jnp.int32, (tokens, tokens), 0) // BLOCK
    kb = lax.broadcasted_iota(jnp.int32, (tokens, tokens), 1) // BLOCK
    linked = jnp.where(qb < kb, layout_ref[0, 1], layout_ref[1, 0])
    allowed = (qb == kb) | (linked > 0)

    def attention():
        for h in range(heads):
            xh = x_ref[:, pl.ds(h * HEAD, HEAD)]
            scores = jnp.where(allowed, dot(xh, xh, 1, 1) * scale, -jnp.inf)
            expo = jnp.exp(scores - jnp.max(scores, axis=-1, keepdims=True))
            p = expo / jnp.sum(expo, axis=-1, keepdims=True)
            probs[h] = p
            att[h // per, z, :, pl.ds(h % per * HEAD, HEAD)] = dot(p.astype(BF), xh).astype(BF)

    @pl.when(flip)
    def _():
        with T("attn"):
            attention()

    with T("barrier"):
        pl.semaphore_wait(barrier, 8)

    for far in (False, True):
        jj = m if far else 1 - m
        dz = 2 * m + jj
        for_me = dz == z
        columns = pl.ds(pl.multiple_of(jj * half, half), half)
        piece = g_ref.at[:, columns]
        send(
            jnp.logical_not(for_me),
            lambda piece=piece, dz=dz: rdma(
                piece, gq.at[z], gq_s, gq_r.at[z], {"samples": 2 * dz + x}
            ),
        )
        send(
            for_me,
            lambda piece=piece: rdma(piece, gq.at[z], gq_s, gf_r.at[z], sibling),
        )

        @pl.when(for_me)
        def _(columns=columns):
            gq[z] = g_ref[:, columns]

    for c in range(NC):
        block = w2.at[x, :, pl.ds(c * wide, wide)]
        send(None, lambda block=block, c=c: rdma(block, block, w_s, w_r.at[c], beside))
    for k in range(1, 8):
        other = lax.rem(s + k, 8)
        send(
            None,
            lambda other=other: rdma(spin_ref, spall.at[s], sp_s, sp_r, {"samples": other}),
        )
    spall[s] = spin_ref[...]

    @pl.when(jnp.logical_not(flip))
    def _():
        with T("attn"):
            attention()

    mask = mask_ref[...]
    tri = (
        lax.broadcasted_iota(jnp.int32, (tokens, tokens), 0)
        <= lax.broadcasted_iota(jnp.int32, (tokens, tokens), 1)
    ).astype(F32).astype(BF)
    mask_rows = jnp.broadcast_to(mask, (8, tokens)).astype(F32)
    rank = dot(mask_rows.astype(BF), tri)[:1] - 1.0
    region = tokens // 2
    place = lax.broadcasted_iota(jnp.int32, (region, tokens), 0).astype(F32)
    select = jnp.where((rank == place) & (mask > 0), 1.0, 0.0).astype(BF)

    first_core = m == z // 2

    def gather(order, own):
        for n in order:
            zz = actual(n)
            got(first_core, gq.at[zz], gq_r.at[zz])
            send(
                first_core,
                lambda zz=zz: rdma(gq.at[zz], gq.at[zz], gf_s, gf_r.at[zz], sibling),
            )
        for n in (own, *order) if own else order:
            zz = actual(n)
            got(jnp.logical_not(first_core), gq.at[zz], gf_r.at[zz])

    def att_to(c, n, slot, inward):
        zz = actual(n)
        way, ss = (inner_way, in_at_s) if inward else (outer_way, out_at_s)
        send(None, lambda: rdma(att.at[c, zz], att.at[c, zz], ss, at_r.at[c, slot], way))

    def att_got(c, n, slot):
        got(None, att.at[c, actual(n)], at_r.at[c, slot])

    def weights_in(c):
        got(None, w2.at[1 - x, :, pl.ds(c * wide, wide)], w_r.at[c])

    def partials(c, first, count):
        cols = pl.ds(c * wide, wide)
        some = gq[pl.ds(first, count)].reshape(count * tokens, 2 * rows)
        sums = dot(some[:, :rows], w2[0, :, cols]) + dot(some[:, rows:], w2[1, :, cols])
        return sums.reshape(count, tokens, wide)

    def weight_terms(c):
        total = jnp.zeros((2 * rows, wide), F32)
        for zz in range(NZ):
            total += dot(gq[zz], att[c, zz], 0, 0).astype(BF).astype(F32)
        cols = pl.ds(c * wide, wide)

        @pl.when(x == 0)
        def _():
            wown[:, cols] = total[:rows]
            wsend[c] = total[rows:].astype(BF)

        @pl.when(x == 1)
        def _():
            wown[:, cols] = total[rows:]
            wsend[c] = total[:rows].astype(BF)

        send(None, lambda: rdma(wsend.at[c], wrecv.at[c], wr_s, wr_r, beside))

    def backward(b, total_of):
        chunks = GROUPS[b]
        for c in chunks:
            ga[:, c * wide : (c + 1) * wide] = total_of(c).astype(BF)
        for h in range(chunks[0] * per, (chunks[-1] + 1) * per):
            cols = slice(h * HEAD, (h + 1) * HEAD)
            xh = x_ref[:, cols]
            gh = ga[:, cols]
            p = probs[h]
            gp = dot(gh, xh, 1, 1)
            gs = (p * (gp - jnp.sum(gp * p, axis=-1, keepdims=True))).astype(BF)
            through = dot(p.astype(BF), gh, 0, 0) + scale * (dot(gs, xh) + dot(gs, xh, 0, 0))
            g0[:, cols] = (g_ref[:, cols].astype(F32) + through).astype(BF)
        for c in chunks:
            swz[c, s % 4] = dot(select, g0[:, c * wide : (c + 1) * wide]).astype(BF)
        part = pl.ds(chunks[0], len(chunks))
        for k in (3, 2, 1):
            other = s // 4 * 4 + lax.rem(s + k, 4)
            rows_now = swz.at[part, s % 4]
            send(
                None,
                lambda rows_now=rows_now, other=other: rdma(
                    rows_now, rows_now, sw_s, sw_r.at[b, s % 4], {"samples": other}
                ),
            )

    def rows_of(c, which):
        rows_now = swz[c, 0]
        for k in range(1, 4):
            rows_now = jnp.where(which == k, swz[c, k], rows_now)
        return rows_now

    def across(b):
        part = pl.ds(GROUPS[b][0], len(GROUPS[b]))
        for k in range(1, 4):
            got(None, swz.at[part, 0], sw_r.at[b, lax.rem(s + k, 4)])
        dest = lax.rem(s + 4, 8)
        wanted = lax.rem(partner_ref[dest], 4)
        for c in GROUPS[b]:
            xsend[c] = rows_of(c, wanted)
        send(
            None,
            lambda: rdma(xsend.at[part], xrecv.at[part], xs_s, xs_r.at[b], {"samples": dest}),
        )

    def embed():
        got(None, spall.at[pl.ds(0, 7)], sp_r)
        spins = jnp.where(mask > 0, spall[partner_ref[s]], spin_ref[...])
        onehot = jnp.where(
            spins == lax.broadcasted_iota(jnp.int32, (8, tokens), 0), 1.0, 0.0
        ).astype(BF)
        embs[s] = dot(onehot, g0[...])[:SPINS]
        for k in range(1, 8):
            other = lax.rem(s + k, 8)
            send(
                None,
                lambda other=other: rdma(embs.at[s], embs.at[s], em_s, em_r, {"samples": other}),
            )

    mine = partner_ref[s]
    eye = lax.broadcasted_iota(jnp.int32, (tokens, tokens), 0) == lax.broadcasted_iota(
        jnp.int32, (tokens, tokens), 1
    )
    keep = jnp.where(eye & (mask == 0), 1.0, 0.0).astype(BF)

    def rows_in(b):
        chunks = GROUPS[b]
        got(None, xrecv.at[pl.ds(chunks[0], len(chunks))], xs_r.at[b])
        for c in chunks:
            cols = slice(c * wide, (c + 1) * wide)
            chosen = jnp.where(mine // 4 == s // 4, rows_of(c, lax.rem(mine, 4)), xrecv[c])
            cot_ref[:, cols] = (dot(keep, g0[:, cols]) + dot(select, chosen, 0, 0)).astype(BF)

    def weights_out():
        got(None, wrecv, wr_r)
        for c in range(NC):
            cols = slice(c * wide, (c + 1) * wide)
            wg_ref[:, cols] = wown[:, cols] + wrecv[c].astype(F32)

    def end_tasks():
        def total_of(c):
            got(None, far_in.at[c, 0], far_r.at[c, 0])
            return pf[c, actual(3)] + far_in[c, 0].astype(F32)

        def part_out(c, n):
            zz = actual(n)
            send(
                None,
                lambda: rdma(
                    pb.at[c, zz], near_in.at[c, n], ps_s, near_r.at[c, n], inner_way
                ),
            )

        weights_seen = set()

        def weights(c):
            if c not in weights_seen:
                weights_seen.add(c)
                weights_in(c)

        def p2(c):
            weights(c)
            first = jnp.where(flip, 0, 2)
            sums = partials(c, first, 2)
            pf[c, pl.ds(first, 2)] = sums
            pb[c, pl.ds(first, 2)] = sums.astype(BF)

        def p01(c):
            weights(c)
            first = jnp.where(flip, 2, 0)
            pb[c, pl.ds(first, 2)] = partials(c, first, 2).astype(BF)

        def wt(c):
            for slot in range(3):
                att_got(c, 2 - slot, slot)
            weight_terms(c)

        return {
            "ga": lambda: gather((2,), 3),
            "gb": lambda: gather((1, 0), None),
            "attE": lambda c: att_to(c, 3, 0, True),
            "s0": lambda c: part_out(c, 0), "s1": lambda c: part_out(c, 1), "s2": lambda c: part_out(c, 2),
            "p2": p2, "p01": p01, "wt": wt,
            "back": lambda b: backward(b, total_of),
            "across": across, "emb": embed, "fin": rows_in, "finw": weights_out,
        }

    def inner_tasks():
        def total_of(c):
            got(None, near_in.at[c, 2], near_r.at[c, 2])
            got(None, far_in.at[c, 1], far_r.at[c, 1])
            return pf[c, actual(2)] + near_in[c, 2].astype(F32) + far_in[c, 1].astype(F32)

        def part(c):
            weights_in(c)
            pf[c] = partials(c, 0, NZ)

        def far(c, n):
            got(None, near_in.at[c, n], near_r.at[c, n])
            pb[c, n] = (pf[c, actual(n)] + near_in[c, n].astype(F32)).astype(BF)
            send(
                None,
                lambda: rdma(pb.at[c, n], far_in.at[c, n], ps_s, far_r.at[c, n], inner_way),
            )

        def near(c):
            got(None, far_in.at[c, 0], far_r.at[c, 0])
            pb[c, 3] = (pf[c, actual(3)] + far_in[c, 0].astype(F32)).astype(BF)
            send(
                None,
                lambda: rdma(pb.at[c, 3], far_in.at[c, 0], ps_s, far_r.at[c, 0], outer_way),
            )

        def relay(n, slot, to_slot, inward):
            def run(c):
                att_got(c, n, slot)
                att_to(c, n, to_slot, inward)

            return run

        return {
            "gather": lambda: gather((3, 1, 0), 2),
            "attIi": lambda c: att_to(c, 2, 1, True), "attIo": lambda c: att_to(c, 2, 0, False),
            "part": part, "near": near,
            "far0": lambda c: far(c, 0), "far1": lambda c: far(c, 1),
            "r3": relay(3, 0, 2, True),
            "r1": relay(1, 1, 1, False),
            "r0": relay(0, 2, 2, False),
            "wt": weight_terms, "back": lambda b: backward(b, total_of),
            "across": across, "emb": embed, "fin": rows_in, "finw": weights_out,
        }

    def run(tasks, order):
        for name, *at in order:
            with T("_".join([name, *map(str, at)])):
                tasks[name](*at)

    @pl.when(is_end)
    def _():
        run(end_tasks(), END_ORDER)
        sent(None, att.at[:, 0], in_at_s)

    @pl.when(jnp.logical_not(is_end))
    def _():
        run(inner_tasks(), INNER_ORDER)
        sent(None, att.at[:, pl.ds(0, 2)], in_at_s)
        sent(None, att.at[:, pl.ds(0, 3)], out_at_s)

    with T("embw"):
        got(None, embs.at[pl.ds(0, 7)], em_r)
    total = embs[0]
    for k in range(1, 8):
        total += embs[k]
    emb_ref[...] = total
    with T("sends_done"):
        sent(None, g_ref, gq_s)
        sent(first_core, gq.at[pl.ds(0, 3)], gf_s)
        sent(None, w2.at[0], w_s)
        sent(None, spall.at[pl.ds(0, 7)], sp_s)
        sent(None, embs.at[pl.ds(0, 7)], em_s)
        sent(None, pb.at[:, pl.ds(0, 3)], ps_s)
        sent(None, swz.at[:, pl.ds(0, 3)], sw_s)
        sent(None, xsend, xs_s)
        sent(None, wsend, wr_s)


def put_out(wg_ref, cot_ref, emb_ref, wg_out, cot_out, emb_out, done):
    copies = [
        pltpu.make_async_copy(wg_ref, wg_out, done.at[0]),
        pltpu.make_async_copy(cot_ref, cot_out, done.at[1]),
        pltpu.make_async_copy(emb_ref, emb_out, done.at[2]),
    ]
    for copy in copies:
        copy.start()
    for copy in copies:
        copy.wait()


def one_layer(
    stored_inputs, top_cotangent, layer_weights, block_layout, region_mask, partner_samples, spins
):
    tokens, width = stored_inputs.shape[2:]
    rows = layer_weights.shape[1]
    hbm = pl.BlockSpec(memory_space=pltpu.HBM)
    vmem = pl.BlockSpec(memory_space=pltpu.VMEM)
    region = tokens // 2
    dma = pltpu.SemaphoreType.DMA
    half = width // 2
    wide = width // NC
    shapes = [
        ((NZ, tokens, 2 * rows), BF),
        ((2, rows, width), BF),
        ((NC, NZ, tokens, wide), F32),
        ((NC, NZ, tokens, wide), BF),
        ((NC, 3, tokens, wide), BF),
        ((NC, 2, tokens, wide), BF),
        ((NC, NZ, tokens, wide), BF),
        ((width // HEAD, tokens, tokens), F32),
        ((tokens, width), BF),
        ((tokens, width), BF),
        ((NC, 4, region, wide), BF),
        ((NC, region, wide), BF),
        ((NC, region, wide), BF),
        ((8, 1, tokens), jnp.int32),
        ((8, SPINS, width), F32),
        ((NC, rows, wide), BF),
        ((NC, rows, wide), BF),
        ((rows, width), F32),
    ]
    one = dma
    sems = [
        dma((7,)), one, dma((NZ,)), one, dma((NZ,)), one, dma((NC,)), one, one, one, one, dma((NC, 3)), one,
        dma((NC, 3)), dma((NC, 2)), one, dma((len(GROUPS), 4)), one, dma((len(GROUPS),)), one, one, one, one,
    ]
    wg, cot, emb = pl.pallas_call(
        kernel,
        out_shape=[
            jax.ShapeDtypeStruct((rows, width), F32),
            jax.ShapeDtypeStruct((tokens, width), BF),
            jax.ShapeDtypeStruct((SPINS, width), F32),
        ],
        in_specs=[hbm] * 7,
        out_specs=[vmem] * 3,
        scratch_shapes=[
            pltpu.VMEM((tokens, width), BF),
            pltpu.VMEM((tokens, width), BF),
            pltpu.SMEM((2, 2), jnp.int32),
            pltpu.VMEM((1, tokens), jnp.int32),
            pltpu.SMEM((8,), jnp.int32),
            pltpu.VMEM((1, tokens), jnp.int32),
        ]
        + [pltpu.VMEM(a, b) for a, b in shapes]
        + sems,
        compiler_params=pltpu.CompilerParams(
            collective_id=0, has_side_effects=True, vmem_limit_bytes=48 * 1024 * 1024
        ),
    )(
        *[
            pltpu.with_memory_space_constraint(value, pltpu.HBM)
            for value in (
                stored_inputs[0, 0], top_cotangent[0], layer_weights[0], block_layout[0],
                region_mask[None], partner_samples, spins,
            )
        ]
    )
    anywhere = pl.BlockSpec(memory_space=pl.ANY)
    wg, cot, emb = pl.pallas_call(
        put_out,
        out_shape=[jax.ShapeDtypeStruct(a.shape, a.dtype) for a in (wg, cot, emb)],
        in_specs=[vmem] * 3,
        out_specs=[anywhere] * 3,
        scratch_shapes=[dma((3,))],
        compiler_params=pltpu.CompilerParams(vmem_limit_bytes=8 * 1024 * 1024),
    )(wg, cot, emb)
    return wg[None], cot[None, None], emb


def solution(mesh):
    in_specs = (
        P("section", ("groups", "samples"), None, "mp"),
        P(("groups", "samples"), None, "mp"),
        P("section", "samples", "mp"),
        P("section", None, None),
        P(),
        P("groups"),
        P(("groups", "samples"), None),
    )
    out_specs = (
        P(("groups", "section"), "samples", "mp"),
        P("section", ("groups", "samples"), None, "mp"),
        P("groups", "mp"),
    )
    small = mesh.shape["samples"] == 8 and mesh.shape["section"] == 1 and mesh.shape["mp"] == 2
    body = one_layer if small else local
    return jax.shard_map(body, mesh=mesh, in_specs=in_specs, out_specs=out_specs, check_vma=False)
```

```python
import jax
import jax.numpy as jnp
from jax import lax
from jax.experimental import pallas as pl
from jax.experimental.pallas import tpu as pltpu
from jax.sharding import PartitionSpec as P

HEAD = 128
BLOCK = 64
SPINS = 2


def for_sending(value):

    def short(part):
        return part.astype(jnp.bfloat16) if part.dtype == jnp.float32 else part

    return jax.tree.map(short, value)


def passed_along(block, axis, distance):
    devices = range(lax.axis_size(axis))
    route = [(i - distance, i) for i in devices if i - distance in devices]
    return lax.ppermute(block, axis, route)


def softmax_parts(inputs_h, allowed, attention_scale):
    scores = (
        jnp.einsum("qhd,khd->hqk", inputs_h, inputs_h, preferred_element_type=jnp.float32)
        * attention_scale
    )
    scores = jnp.where(allowed[None], scores, -jnp.inf)
    top_score = jnp.max(scores, axis=-1, keepdims=True)
    expo_terms = jnp.exp(scores - top_score)
    probs = expo_terms / jnp.sum(expo_terms, axis=-1, keepdims=True)
    return (probs, probs.astype(jnp.bfloat16))


def local(
    stored_inputs, top_cotangent, layer_weights, block_layout, region_mask, partner_samples, spins
):
    section_index = lax.axis_index("section")
    section_count = lax.axis_size("section")
    micro_count = stored_inputs.shape[1]
    seq_len = stored_inputs.shape[2]
    half_width = stored_inputs.shape[3]
    head_count = half_width // HEAD
    attention_scale = 4.0 / HEAD
    weights = lax.all_gather(layer_weights[0], "samples", axis=0, tiled=True)
    pos_block = jnp.arange(seq_len) // BLOCK
    block_onehot = (pos_block[:, None] == jnp.arange(block_layout.shape[1])[None, :]).astype(
        jnp.float32
    )
    linked = jnp.dot(jnp.dot(block_onehot, block_layout[0].astype(jnp.float32)), block_onehot.T)
    allowed = (linked > 0.5) | (pos_block[:, None] == pos_block[None, :])
    every_layer_input = stored_inputs[0]
    inputs_h = every_layer_input[0].reshape(seq_len, head_count, HEAD)
    probs, probs_low = softmax_parts(inputs_h, allowed, attention_scale)
    attended = jnp.einsum(
        "hqk,khd->qhd", probs_low, inputs_h, preferred_element_type=jnp.float32
    ).astype(jnp.bfloat16)
    probs_list = [probs]
    low_list = [probs_low]
    attend_list = [attended.reshape(seq_len, half_width)]
    probs_all = jnp.stack(probs_list)
    low_all = jnp.stack(low_list)
    attend_store = jnp.stack(attend_list)

    def layer_back(grad_full, grad_own, inputs, probs, probs_low):
        grad_attn = jnp.dot(grad_full, weights, preferred_element_type=jnp.float32).astype(
            jnp.bfloat16
        )
        inputs_h = inputs.reshape(seq_len, head_count, HEAD)
        grad_h = grad_attn.reshape(seq_len, head_count, HEAD)
        grad_probs = jnp.einsum(
            "qhd,khd->hqk", grad_h, inputs_h, preferred_element_type=jnp.float32
        )
        grad_scores = (
            probs * (grad_probs - jnp.sum(grad_probs * probs, axis=-1, keepdims=True))
        ).astype(jnp.bfloat16)
        through = jnp.einsum("hqk,qhd->khd", probs_low, grad_h, preferred_element_type=jnp.float32)
        through = through + attention_scale * (
            jnp.einsum("hqk,khd->qhd", grad_scores, inputs_h, preferred_element_type=jnp.float32)
            + jnp.einsum("hqk,qhd->khd", grad_scores, inputs_h, preferred_element_type=jnp.float32)
        )
        grad_in = grad_own.astype(jnp.float32) + through.reshape(seq_len, half_width)
        return grad_in.astype(jnp.bfloat16)

    def resting(grad_full, grad_own, inputs, probs, probs_low):
        return jnp.zeros((seq_len, half_width), jnp.bfloat16)

    carried_state = jnp.zeros((seq_len, half_width), jnp.bfloat16)
    out_list = []
    grad_list = []
    total_steps = micro_count + section_count - 1
    for step_number in range(total_steps):
        micro_index = step_number - (section_count - 1 - section_index)
        active = (micro_index >= 0) & (micro_index < micro_count)
        slot_index = jnp.clip(micro_index, 0, micro_count - 1)
        from_top = lax.dynamic_index_in_dim(top_cotangent, slot_index, 0, keepdims=False)
        incoming = jnp.where(section_index == section_count - 1, from_top, carried_state)
        grad_full = lax.all_gather(incoming, "mp", axis=1, tiled=True)
        inputs_now = lax.dynamic_index_in_dim(every_layer_input, slot_index, 0, keepdims=False)
        probs_now = lax.dynamic_index_in_dim(probs_all, slot_index, 0, keepdims=False)
        low_now = lax.dynamic_index_in_dim(low_all, slot_index, 0, keepdims=False)
        grad_in = lax.cond(
            active, layer_back, resting, grad_full, incoming, inputs_now, probs_now, low_now
        )
        out_list.append(grad_in)
        grad_list.append(grad_full)
        if step_number < total_steps - 1:
            carried_state = jax.tree.map(
                lambda part, own: part.astype(own.dtype),
                passed_along(for_sending(grad_in), "section", -1),
                grad_in,
            )
    offset = section_count - 1 - section_index
    out_store = lax.dynamic_slice_in_dim(jnp.stack(out_list), offset, micro_count, 0)
    grad_store = lax.dynamic_slice_in_dim(jnp.stack(grad_list), offset, micro_count, 0)
    summed_weight = lax.psum_scatter(
        jnp.einsum(
            "mtf,mta->fa", grad_store, attend_store, preferred_element_type=jnp.float32
        ).astype(jnp.bfloat16),
        "samples",
        scatter_dimension=0,
        tiled=True,
    ).astype(jnp.float32)
    region_count = seq_len // 2
    place_in = jnp.arange(seq_len)
    rank_in_region = (
        jnp.sum(jnp.where(place_in[None, :] <= place_in[:, None], region_mask[None, :], 0), axis=1) - 1
    )
    select = (
        (rank_in_region[None, :] == jnp.arange(region_count)[:, None]) & (region_mask[None, :] > 0)
    ).astype(jnp.bfloat16)
    tiles = jnp.einsum("at,mtd->mad", select, out_store, preferred_element_type=jnp.float32).astype(
        jnp.bfloat16
    )
    shard_index = lax.axis_index("samples")
    my_partners = lax.dynamic_slice_in_dim(
        partner_samples, shard_index * micro_count, micro_count, 0
    )
    shard_count = lax.axis_size("samples")
    dest_shard = my_partners // micro_count
    dest_slot = my_partners % micro_count
    route = (
        (dest_shard[:, None, None] == jnp.arange(shard_count)[None, :, None])
        & (dest_slot[:, None, None] == jnp.arange(micro_count)[None, None, :])
    ).astype(jnp.bfloat16)
    outgoing = jnp.einsum("mku,mad->kuad", route, tiles, preferred_element_type=jnp.float32).astype(
        jnp.bfloat16
    )
    arrived = lax.all_to_all(outgoing, "samples", split_axis=0, concat_axis=0, tiled=True)
    ones_row = jnp.ones((shard_count,), jnp.bfloat16)
    received = jnp.einsum(
        "k,kuad->uad", ones_row, arrived, preferred_element_type=jnp.float32
    ).astype(jnp.bfloat16)
    placed = jnp.einsum("at,mad->mtd", select, received, preferred_element_type=jnp.float32)
    kept = jnp.where(region_mask[None, :, None] > 0, jnp.zeros_like(out_store), out_store)
    site_cot = (kept.astype(jnp.float32) + placed).astype(jnp.bfloat16)
    cotangents = jnp.where(section_index == 0, site_cot, out_store)
    onehot = (spins[:, :, None] == jnp.arange(SPINS)[None, None, :]).astype(jnp.bfloat16)
    embed_term = jnp.einsum("mtv,mtd->vd", onehot, site_cot, preferred_element_type=jnp.float32)
    embed_term = jnp.where(section_index == 0, embed_term, jnp.zeros_like(embed_term))
    embed_grad = lax.psum(embed_term, ("samples", "section"))
    return (summed_weight[None], cotangents[None], embed_grad)


NZ = 4
NC = 4
PIECES = (False, True)
GROUPS = ((0, 1), (2,), (3,))
END_ORDER = (
    ("attE", 0), ("attE", 1), ("ga",), ("attE", 2), ("p2", 1), ("gb",),
    ("attE", 3), ("p01", 0), ("s0", 0), ("p01", 1), ("s1", 1), ("p2", 2),
    ("s0", 1), ("p01", 2), ("p2", 3), ("p01", 3), ("s1", 0), ("s1", 3),
    ("s0", 3), ("s0", 2), ("p2", 0), ("s2", 1), ("s2", 0), ("wt", 0),
    ("wt", 2), ("s1", 2), ("s2", 3), ("s2", 2), ("back", 0), ("back", 2),
    ("wt", 1), ("back", 1), ("emb",), ("wt", 3), ("fin", 2), ("fin", 0),
    ("fin", 1), ("finw",), ("embw",),
)
INNER_ORDER = (
    ("gather",), ("attIi", 2), ("attIo", 0), ("attIo", 1), ("attIi", 1), ("attIi", 0),
    ("r3", 0), ("part", 0), ("attIo", 2), ("r1", 1), ("r3", 1), ("r1", 0),
    ("r1", 2), ("r0", 0), ("r3", 2), ("r3", 3), ("r0", 1), ("part", 2),
    ("far0", 0), ("part", 1), ("wt", 0), ("far0", 1), ("r0", 2), ("part", 3),
    ("wt", 1), ("far1", 1), ("near", 0), ("far1", 0), ("far0", 3), ("near", 1),
    ("wt", 2), ("attIi", 3), ("r0", 3), ("attIo", 3), ("far0", 2), ("near", 3),
    ("far1", 3), ("back", 0), ("near", 2), ("far1", 2), ("r1", 3), ("back", 2),
    ("back", 1), ("emb",), ("wt", 3), ("across", 0), ("across", 2), ("across", 1),
    ("fin", 0), ("fin", 1), ("fin", 2), ("finw",), ("embw",),
)
MESH = pl.DeviceIdType.MESH
F32 = jnp.float32
BF = jnp.bfloat16
T = jax.named_scope


def dot(a, b, ca=1, cb=0):
    return lax.dot_general(a, b, (((ca,), (cb,)), ((), ())), preferred_element_type=F32)


def kernel(
    x_hbm, g_hbm, w_hbm, layout_hbm, mask_hbm, partner_hbm, spin_hbm,
    wg_ref, cot_ref, emb_ref,
    x_ref, g_ref, layout_ref, mask_ref, partner_ref, spin_ref, gq, w2, pf, pb, near_in, far_in, att, probs, ga, g0,
    swz, xsend, xrecv, irecv, spall, embs, wsend, wrecv, wown,
    in_s, gq_s, gq_r, gf_s, gf_r, w_s, w_r, sp_s, sp_r, in_at_s, out_at_s, at_r, ps_s, near_r, far_r,
    sw_s, sw_r, xs_s, xs_r, si_r, em_s, em_r, wr_s, wr_r,
):
    s = lax.axis_index("samples")
    m = lax.axis_index("mp")
    z = s // 2
    x = s % 2
    flip = z < NZ // 2
    is_end = (z == 0) | (z == NZ - 1)
    outward = jnp.where(flip, -2, 2)
    scale = 4.0 / HEAD
    tokens, width = x_ref.shape
    heads = width // HEAD
    rows = w_hbm.shape[0]
    half = width // 2
    wide = width // NC
    per = wide // HEAD
    sibling = {"mp": 1 - m}
    beside = {"samples": 2 * z + 1 - x}
    inner_way = {"samples": lax.rem(s - outward + 8, 8)}
    outer_way = {"samples": lax.rem(s + outward + 8, 8)}

    def actual(n):
        return jnp.where(flip, NZ - 1 - n, n)

    def rdma(src, dst, ss, rs, dev):
        return pltpu.make_async_remote_copy(
            src_ref=src, dst_ref=dst, send_sem=ss, recv_sem=rs, device_id=dev, device_id_type=MESH
        )

    def send(cond, make):
        if cond is None:
            make().start()
        else:
            pl.when(cond)(lambda: make().start())

    def sent(cond, src, ss):
        def wait():
            rdma(src, src, ss, ss, sibling).wait_send()

        if cond is None:
            wait()
        else:
            pl.when(cond)(wait)

    def got(cond, dst, rs):
        def wait():
            rdma(dst, dst, rs, rs, sibling).wait_recv()

        if cond is None:
            wait()
        else:
            pl.when(cond)(wait)

    loads = [
        pltpu.make_async_copy(g_hbm, g_ref, in_s.at[0]),
        pltpu.make_async_copy(w_hbm, w2.at[x], in_s.at[1]),
        pltpu.make_async_copy(x_hbm, x_ref, in_s.at[2]),
        pltpu.make_async_copy(spin_hbm, spin_ref, in_s.at[3]),
        pltpu.make_async_copy(layout_hbm, layout_ref, in_s.at[4]),
        pltpu.make_async_copy(mask_hbm, mask_ref, in_s.at[5]),
        pltpu.make_async_copy(partner_hbm, partner_ref, in_s.at[6]),
    ]
    for load in loads:
        load.start()
    barrier = pltpu.get_barrier_semaphore()
    for k in range(1, 8):
        pl.semaphore_signal(
            barrier, inc=1, device_id={"samples": lax.rem(s + k, 8)}, device_id_type=MESH
        )
    pl.semaphore_signal(barrier, inc=1, device_id=sibling, device_id_type=MESH)
    for load in loads:
        load.wait()

    qb = lax.broadcasted_iota(jnp.int32, (tokens, tokens), 0) // BLOCK
    kb = lax.broadcasted_iota(jnp.int32, (tokens, tokens), 1) // BLOCK
    linked = jnp.where(qb < kb, layout_ref[0, 1], layout_ref[1, 0])
    allowed = (qb == kb) | (linked > 0)

    def attention():
        for h in range(heads):
            xh = x_ref[:, pl.ds(h * HEAD, HEAD)]
            scores = jnp.where(allowed, dot(xh, xh, 1, 1) * scale, -jnp.inf)
            expo = jnp.exp(scores - jnp.max(scores, axis=-1, keepdims=True))
            p = expo / jnp.sum(expo, axis=-1, keepdims=True)
            probs[h] = p
            att[h // per, z, :, pl.ds(h % per * HEAD, HEAD)] = dot(p.astype(BF), xh).astype(BF)

    @pl.when(flip)
    def _():
        with T("attn"):
            attention()

    with T("barrier"):
        pl.semaphore_wait(barrier, 8)

    for far in PIECES:
        jj = m if far else 1 - m
        dz = 2 * m + jj
        for_me = dz == z
        columns = pl.ds(pl.multiple_of(jj * half, half), half)
        piece = g_ref.at[:, columns]
        send(
            jnp.logical_not(for_me),
            lambda piece=piece, dz=dz: rdma(
                piece, gq.at[z], gq_s, gq_r.at[z], {"samples": 2 * dz + x}
            ),
        )
        send(
            for_me,
            lambda piece=piece: rdma(piece, gq.at[z], gq_s, gf_r.at[z], sibling),
        )

        @pl.when(for_me)
        def _(columns=columns):
            gq[z] = g_ref[:, columns]

    for c in range(NC):
        block = w2.at[x, :, pl.ds(c * wide, wide)]
        send(None, lambda block=block, c=c: rdma(block, block, w_s, w_r.at[c], beside))
    for k in range(1, 8):
        other = lax.rem(s + k, 8)
        send(
            None,
            lambda other=other: rdma(spin_ref, spall.at[s], sp_s, sp_r, {"samples": other}),
        )
    spall[s] = spin_ref[...]

    @pl.when(jnp.logical_not(flip))
    def _():
        with T("attn"):
            attention()

    mask = mask_ref[...]
    tri = (
        lax.broadcasted_iota(jnp.int32, (tokens, tokens), 0)
        <= lax.broadcasted_iota(jnp.int32, (tokens, tokens), 1)
    ).astype(F32).astype(BF)
    mask_rows = jnp.broadcast_to(mask, (8, tokens)).astype(F32)
    rank = dot(mask_rows.astype(BF), tri)[:1] - 1.0
    region = tokens // 2
    place = lax.broadcasted_iota(jnp.int32, (region, tokens), 0).astype(F32)
    select = jnp.where((rank == place) & (mask > 0), 1.0, 0.0).astype(BF)

    first_core = m == z // 2

    def gather(order, own):
        for n in order:
            zz = actual(n)
            got(first_core, gq.at[zz], gq_r.at[zz])
            send(
                first_core,
                lambda zz=zz: rdma(gq.at[zz], gq.at[zz], gf_s, gf_r.at[zz], sibling),
            )
        for n in (own, *order) if own else order:
            zz = actual(n)
            got(jnp.logical_not(first_core), gq.at[zz], gf_r.at[zz])

    def att_to(c, n, slot, inward):
        zz = actual(n)
        way, ss = (inner_way, in_at_s) if inward else (outer_way, out_at_s)
        send(None, lambda: rdma(att.at[c, zz], att.at[c, zz], ss, at_r.at[c, slot], way))

    def att_got(c, n, slot):
        got(None, att.at[c, actual(n)], at_r.at[c, slot])

    def weights_in(c):
        got(None, w2.at[1 - x, :, pl.ds(c * wide, wide)], w_r.at[c])

    def partials(c, first, count):
        cols = pl.ds(c * wide, wide)
        some = gq[pl.ds(first, count)].reshape(count * tokens, 2 * rows)
        sums = dot(some[:, :rows], w2[0, :, cols]) + dot(some[:, rows:], w2[1, :, cols])
        return sums.reshape(count, tokens, wide)

    def weight_terms(c):
        total = jnp.zeros((2 * rows, wide), F32)
        for zz in range(NZ):
            total += dot(gq[zz], att[c, zz], 0, 0).astype(BF).astype(F32)
        cols = pl.ds(c * wide, wide)

        @pl.when(x == 0)
        def _():
            wown[:, cols] = total[:rows]
            wsend[c] = total[rows:].astype(BF)

        @pl.when(x == 1)
        def _():
            wown[:, cols] = total[rows:]
            wsend[c] = total[:rows].astype(BF)

        send(None, lambda: rdma(wsend.at[c], wrecv.at[c], wr_s, wr_r, beside))

    def backward(b, total_of):
        chunks = GROUPS[b]
        for c in chunks:
            ga[:, c * wide : (c + 1) * wide] = total_of(c).astype(BF)
        for h in range(chunks[0] * per, (chunks[-1] + 1) * per):
            cols = slice(h * HEAD, (h + 1) * HEAD)
            xh = x_ref[:, cols]
            gh = ga[:, cols]
            p = probs[h]
            gp = dot(gh, xh, 1, 1)
            gs = (p * (gp - jnp.sum(gp * p, axis=-1, keepdims=True))).astype(BF)
            through = dot(p.astype(BF), gh, 0, 0) + scale * (dot(gs, xh) + dot(gs, xh, 0, 0))
            g0[:, cols] = (g_ref[:, cols].astype(F32) + through).astype(BF)
        for c in chunks:
            swz[c, s % 4] = dot(select, g0[:, c * wide : (c + 1) * wide]).astype(BF)

    def tile_to(b, other):
        rows_now = swz.at[pl.ds(GROUPS[b][0], len(GROUPS[b])), s % 4]
        send(
            None,
            lambda: rdma(rows_now, rows_now, sw_s, sw_r.at[b, s % 4], {"samples": other}),
        )

    def rows_of(c, which):
        rows_now = swz[c, 0]
        for k in range(1, 4):
            rows_now = jnp.where(which == k, swz[c, k], rows_now)
        return rows_now

    def embed():
        got(None, spall.at[pl.ds(0, 7)], sp_r)
        spins = jnp.where(mask > 0, spall[partner_ref[s]], spin_ref[...])
        onehot = jnp.where(
            spins == lax.broadcasted_iota(jnp.int32, (8, tokens), 0), 1.0, 0.0
        ).astype(BF)
        embs[s] = dot(onehot, g0[...])[:SPINS]
        for k in range(1, 8):
            other = lax.rem(s + k, 8)
            send(
                None,
                lambda other=other: rdma(embs.at[s], embs.at[s], em_s, em_r, {"samples": other}),
            )

    mine = partner_ref[s]
    eye = lax.broadcasted_iota(jnp.int32, (tokens, tokens), 0) == lax.broadcasted_iota(
        jnp.int32, (tokens, tokens), 1
    )
    keep = jnp.where(eye & (mask == 0), 1.0, 0.0).astype(BF)

    def rows_in(b, other_of):
        chunks = GROUPS[b]
        got(None, xrecv.at[pl.ds(chunks[0], len(chunks))], xs_r.at[b])
        for c in chunks:
            cols = slice(c * wide, (c + 1) * wide)
            chosen = jnp.where(mine // 4 == s // 4, other_of(c), xrecv[c])
            cot_ref[:, cols] = (dot(keep, g0[:, cols]) + dot(select, chosen, 0, 0)).astype(BF)

    def embed_sum():
        got(None, embs.at[pl.ds(0, 7)], em_r)
        total = embs[0]
        for k in range(1, 8):
            total += embs[k]
        emb_ref[...] = total

    def weights_out():
        got(None, wrecv, wr_r)
        for c in range(NC):
            cols = slice(c * wide, (c + 1) * wide)
            wg_ref[:, cols] = wown[:, cols] + wrecv[c].astype(F32)

    def end_tasks():
        def total_of(c):
            got(None, far_in.at[c, 0], far_r.at[c, 0])
            return pf[c, actual(3)] + far_in[c, 0].astype(F32)

        def part_out(c, n):
            zz = actual(n)
            send(
                None,
                lambda: rdma(
                    pb.at[c, zz], near_in.at[c, n], ps_s, near_r.at[c, n], inner_way
                ),
            )

        weights_seen = set()

        def weights(c):
            if c not in weights_seen:
                weights_seen.add(c)
                weights_in(c)

        def p2(c):
            weights(c)
            first = jnp.where(flip, 0, 2)
            sums = partials(c, first, 2)
            pf[c, pl.ds(first, 2)] = sums
            pb[c, pl.ds(first, 2)] = sums.astype(BF)

        def p01(c):
            weights(c)
            first = jnp.where(flip, 2, 0)
            pb[c, pl.ds(first, 2)] = partials(c, first, 2).astype(BF)

        def back(b):
            backward(b, total_of)
            tile_to(b, s - outward + 1 - 2 * x)
            tile_to(b, s - outward)

        def fin(b):
            got(None, irecv.at[pl.ds(GROUPS[b][0], len(GROUPS[b]))], si_r.at[b])
            rows_in(b, lambda c: irecv[c])

        def wt(c):
            for slot in range(3):
                att_got(c, 2 - slot, slot)
            weight_terms(c)

        return {
            "ga": lambda: gather((2,), 3),
            "gb": lambda: gather((1, 0), None),
            "attE": lambda c: att_to(c, 3, 0, True),
            "s0": lambda c: part_out(c, 0), "s1": lambda c: part_out(c, 1), "s2": lambda c: part_out(c, 2),
            "p2": p2, "p01": p01, "wt": wt,
            "back": back, "emb": embed, "fin": fin, "finw": weights_out, "embw": embed_sum,
        }

    def inner_tasks():
        def total_of(c):
            got(None, near_in.at[c, 2], near_r.at[c, 2])
            got(None, far_in.at[c, 1], far_r.at[c, 1])
            return pf[c, actual(2)] + near_in[c, 2].astype(F32) + far_in[c, 1].astype(F32)

        def part(c):
            weights_in(c)
            pf[c] = partials(c, 0, NZ)

        def far(c, n):
            got(None, near_in.at[c, n], near_r.at[c, n])
            pb[c, n] = (pf[c, actual(n)] + near_in[c, n].astype(F32)).astype(BF)
            send(
                None,
                lambda: rdma(pb.at[c, n], far_in.at[c, n], ps_s, far_r.at[c, n], inner_way),
            )

        def near(c):
            got(None, far_in.at[c, 0], far_r.at[c, 0])
            pb[c, 3] = (pf[c, actual(3)] + far_in[c, 0].astype(F32)).astype(BF)
            send(
                None,
                lambda: rdma(pb.at[c, 3], far_in.at[c, 0], ps_s, far_r.at[c, 0], outer_way),
            )

        def back(b):
            backward(b, total_of)
            tile_to(b, 2 * z + 1 - x)

        def across(b):
            part = pl.ds(GROUPS[b][0], len(GROUPS[b]))
            for k in range(1, 4):
                got(None, swz.at[part, 0], sw_r.at[b, lax.rem(s + k, 4)])
            for k, dest in enumerate((s - 2 * outward, s - outward, s + outward)):
                wanted = lax.rem(partner_ref[dest], 4)
                for c in GROUPS[b]:
                    xsend[k, c] = rows_of(c, wanted)
                into, rs = (irecv, si_r) if k == 2 else (xrecv, xs_r)
                send(
                    None,
                    lambda k=k, dest=dest, into=into, rs=rs: rdma(
                        xsend.at[k, part], into.at[part], xs_s, rs.at[b], {"samples": dest}
                    ),
                )

        def fin(b):
            rows_in(b, lambda c: rows_of(c, lax.rem(mine, 4)))

        def relay(n, slot, to_slot, inward):
            def run(c):
                att_got(c, n, slot)
                att_to(c, n, to_slot, inward)

            return run

        return {
            "gather": lambda: gather((3, 1, 0), 2),
            "attIi": lambda c: att_to(c, 2, 1, True), "attIo": lambda c: att_to(c, 2, 0, False),
            "part": part, "near": near,
            "far0": lambda c: far(c, 0), "far1": lambda c: far(c, 1),
            "r3": relay(3, 0, 2, True),
            "r1": relay(1, 1, 1, False),
            "r0": relay(0, 2, 2, False),
            "wt": weight_terms, "back": back, "across": across, "emb": embed, "fin": fin, "finw": weights_out,
            "embw": embed_sum,
        }

    def run(tasks, order):
        for name, *at in order:
            with T("_".join([name, *map(str, at)])):
                tasks[name](*at)

    @pl.when(is_end)
    def _():
        run(end_tasks(), END_ORDER)
        sent(None, att.at[:, 0], in_at_s)
        sent(None, swz.at[:, pl.ds(0, 2)], sw_s)

    @pl.when(jnp.logical_not(is_end))
    def _():
        run(inner_tasks(), INNER_ORDER)
        sent(None, att.at[:, pl.ds(0, 2)], in_at_s)
        sent(None, att.at[:, pl.ds(0, 3)], out_at_s)
        sent(None, swz.at[:, 0], sw_s)
        sent(None, xsend, xs_s)

    with T("sends_done"):
        sent(None, g_ref, gq_s)
        sent(first_core, gq.at[pl.ds(0, 3)], gf_s)
        sent(None, w2.at[0], w_s)
        sent(None, spall.at[pl.ds(0, 7)], sp_s)
        sent(None, embs.at[pl.ds(0, 7)], em_s)
        sent(None, pb.at[:, pl.ds(0, 3)], ps_s)
        sent(None, wsend, wr_s)


def put_out(wg_ref, cot_ref, emb_ref, wg_out, cot_out, emb_out, done):
    copies = [
        pltpu.make_async_copy(wg_ref, wg_out, done.at[0]),
        pltpu.make_async_copy(cot_ref, cot_out, done.at[1]),
        pltpu.make_async_copy(emb_ref, emb_out, done.at[2]),
    ]
    for copy in copies:
        copy.start()
    for copy in copies:
        copy.wait()


def one_layer(
    stored_inputs, top_cotangent, layer_weights, block_layout, region_mask, partner_samples, spins
):
    tokens, width = stored_inputs.shape[2:]
    rows = layer_weights.shape[1]
    hbm = pl.BlockSpec(memory_space=pltpu.HBM)
    vmem = pl.BlockSpec(memory_space=pltpu.VMEM)
    region = tokens // 2
    dma = pltpu.SemaphoreType.DMA
    half = width // 2
    wide = width // NC
    shapes = [
        ((NZ, tokens, 2 * rows), BF),
        ((2, rows, width), BF),
        ((NC, NZ, tokens, wide), F32),
        ((NC, NZ, tokens, wide), BF),
        ((NC, 3, tokens, wide), BF),
        ((NC, 2, tokens, wide), BF),
        ((NC, NZ, tokens, wide), BF),
        ((width // HEAD, tokens, tokens), F32),
        ((tokens, width), BF),
        ((tokens, width), BF),
        ((NC, 4, region, wide), BF),
        ((3, NC, region, wide), BF),
        ((NC, region, wide), BF),
        ((NC, region, wide), BF),
        ((8, 1, tokens), jnp.int32),
        ((8, SPINS, width), F32),
        ((NC, rows, wide), BF),
        ((NC, rows, wide), BF),
        ((rows, width), F32),
    ]
    one = dma
    sems = [
        dma((7,)), one, dma((NZ,)), one, dma((NZ,)), one, dma((NC,)), one, one, one, one, dma((NC, 3)), one,
        dma((NC, 3)), dma((NC, 2)), one, dma((len(GROUPS), 4)), one, dma((len(GROUPS),)), dma((len(GROUPS),)),
        one, one, one, one,
    ]
    wg, cot, emb = pl.pallas_call(
        kernel,
        out_shape=[
            jax.ShapeDtypeStruct((rows, width), F32),
            jax.ShapeDtypeStruct((tokens, width), BF),
            jax.ShapeDtypeStruct((SPINS, width), F32),
        ],
        in_specs=[hbm] * 7,
        out_specs=[vmem] * 3,
        scratch_shapes=[
            pltpu.VMEM((tokens, width), BF),
            pltpu.VMEM((tokens, width), BF),
            pltpu.SMEM((2, 2), jnp.int32),
            pltpu.VMEM((1, tokens), jnp.int32),
            pltpu.SMEM((8,), jnp.int32),
            pltpu.VMEM((1, tokens), jnp.int32),
        ]
        + [pltpu.VMEM(a, b) for a, b in shapes]
        + sems,
        compiler_params=pltpu.CompilerParams(
            collective_id=0, has_side_effects=True, vmem_limit_bytes=48 * 1024 * 1024
        ),
    )(
        *[
            pltpu.with_memory_space_constraint(value, pltpu.HBM)
            for value in (
                stored_inputs[0, 0], top_cotangent[0], layer_weights[0], block_layout[0],
                region_mask[None], partner_samples, spins,
            )
        ]
    )
    anywhere = pl.BlockSpec(memory_space=pl.ANY)
    wg, cot, emb = pl.pallas_call(
        put_out,
        out_shape=[jax.ShapeDtypeStruct(a.shape, a.dtype) for a in (wg, cot, emb)],
        in_specs=[vmem] * 3,
        out_specs=[anywhere] * 3,
        scratch_shapes=[dma((3,))],
        compiler_params=pltpu.CompilerParams(vmem_limit_bytes=8 * 1024 * 1024),
    )(wg, cot, emb)
    return wg[None], cot[None, None], emb


def solution(mesh):
    in_specs = (
        P("section", ("groups", "samples"), None, "mp"),
        P(("groups", "samples"), None, "mp"),
        P("section", "samples", "mp"),
        P("section", None, None),
        P(),
        P("groups"),
        P(("groups", "samples"), None),
    )
    out_specs = (
        P(("groups", "section"), "samples", "mp"),
        P("section", ("groups", "samples"), None, "mp"),
        P("groups", "mp"),
    )
    small = mesh.shape["samples"] == 8 and mesh.shape["section"] == 1 and mesh.shape["mp"] == 2
    body = one_layer if small else local
    return jax.shard_map(body, mesh=mesh, in_specs=in_specs, out_specs=out_specs, check_vma=False)
```

```python
import jax
import jax.numpy as jnp
from jax import lax
from jax.experimental import pallas as pl
from jax.experimental.pallas import tpu as pltpu
from jax.sharding import PartitionSpec as P

HEAD = 128
BLOCK = 64
SPINS = 2


def for_sending(value):

    def short(part):
        return part.astype(jnp.bfloat16) if part.dtype == jnp.float32 else part

    return jax.tree.map(short, value)


def passed_along(block, axis, distance):
    devices = range(lax.axis_size(axis))
    route = [(i - distance, i) for i in devices if i - distance in devices]
    return lax.ppermute(block, axis, route)


def softmax_parts(inputs_h, allowed, attention_scale):
    scores = (
        jnp.einsum("qhd,khd->hqk", inputs_h, inputs_h, preferred_element_type=jnp.float32)
        * attention_scale
    )
    scores = jnp.where(allowed[None], scores, -jnp.inf)
    top_score = jnp.max(scores, axis=-1, keepdims=True)
    expo_terms = jnp.exp(scores - top_score)
    probs = expo_terms / jnp.sum(expo_terms, axis=-1, keepdims=True)
    return (probs, probs.astype(jnp.bfloat16))


def local(
    stored_inputs, top_cotangent, layer_weights, block_layout, region_mask, partner_samples, spins
):
    section_index = lax.axis_index("section")
    section_count = lax.axis_size("section")
    micro_count = stored_inputs.shape[1]
    seq_len = stored_inputs.shape[2]
    half_width = stored_inputs.shape[3]
    head_count = half_width // HEAD
    attention_scale = 4.0 / HEAD
    weights = lax.all_gather(layer_weights[0], "samples", axis=0, tiled=True)
    pos_block = jnp.arange(seq_len) // BLOCK
    block_onehot = (pos_block[:, None] == jnp.arange(block_layout.shape[1])[None, :]).astype(
        jnp.float32
    )
    linked = jnp.dot(jnp.dot(block_onehot, block_layout[0].astype(jnp.float32)), block_onehot.T)
    allowed = (linked > 0.5) | (pos_block[:, None] == pos_block[None, :])
    every_layer_input = stored_inputs[0]
    inputs_h = every_layer_input[0].reshape(seq_len, head_count, HEAD)
    probs, probs_low = softmax_parts(inputs_h, allowed, attention_scale)
    attended = jnp.einsum(
        "hqk,khd->qhd", probs_low, inputs_h, preferred_element_type=jnp.float32
    ).astype(jnp.bfloat16)
    probs_list = [probs]
    low_list = [probs_low]
    attend_list = [attended.reshape(seq_len, half_width)]
    probs_all = jnp.stack(probs_list)
    low_all = jnp.stack(low_list)
    attend_store = jnp.stack(attend_list)

    def layer_back(grad_full, grad_own, inputs, probs, probs_low):
        grad_attn = jnp.dot(grad_full, weights, preferred_element_type=jnp.float32).astype(
            jnp.bfloat16
        )
        inputs_h = inputs.reshape(seq_len, head_count, HEAD)
        grad_h = grad_attn.reshape(seq_len, head_count, HEAD)
        grad_probs = jnp.einsum(
            "qhd,khd->hqk", grad_h, inputs_h, preferred_element_type=jnp.float32
        )
        grad_scores = (
            probs * (grad_probs - jnp.sum(grad_probs * probs, axis=-1, keepdims=True))
        ).astype(jnp.bfloat16)
        through = jnp.einsum("hqk,qhd->khd", probs_low, grad_h, preferred_element_type=jnp.float32)
        through = through + attention_scale * (
            jnp.einsum("hqk,khd->qhd", grad_scores, inputs_h, preferred_element_type=jnp.float32)
            + jnp.einsum("hqk,qhd->khd", grad_scores, inputs_h, preferred_element_type=jnp.float32)
        )
        grad_in = grad_own.astype(jnp.float32) + through.reshape(seq_len, half_width)
        return grad_in.astype(jnp.bfloat16)

    def resting(grad_full, grad_own, inputs, probs, probs_low):
        return jnp.zeros((seq_len, half_width), jnp.bfloat16)

    carried_state = jnp.zeros((seq_len, half_width), jnp.bfloat16)
    out_list = []
    grad_list = []
    total_steps = micro_count + section_count - 1
    for step_number in range(total_steps):
        micro_index = step_number - (section_count - 1 - section_index)
        active = (micro_index >= 0) & (micro_index < micro_count)
        slot_index = jnp.clip(micro_index, 0, micro_count - 1)
        from_top = lax.dynamic_index_in_dim(top_cotangent, slot_index, 0, keepdims=False)
        incoming = jnp.where(section_index == section_count - 1, from_top, carried_state)
        grad_full = lax.all_gather(incoming, "mp", axis=1, tiled=True)
        inputs_now = lax.dynamic_index_in_dim(every_layer_input, slot_index, 0, keepdims=False)
        probs_now = lax.dynamic_index_in_dim(probs_all, slot_index, 0, keepdims=False)
        low_now = lax.dynamic_index_in_dim(low_all, slot_index, 0, keepdims=False)
        grad_in = lax.cond(
            active, layer_back, resting, grad_full, incoming, inputs_now, probs_now, low_now
        )
        out_list.append(grad_in)
        grad_list.append(grad_full)
        if step_number < total_steps - 1:
            carried_state = jax.tree.map(
                lambda part, own: part.astype(own.dtype),
                passed_along(for_sending(grad_in), "section", -1),
                grad_in,
            )
    offset = section_count - 1 - section_index
    out_store = lax.dynamic_slice_in_dim(jnp.stack(out_list), offset, micro_count, 0)
    grad_store = lax.dynamic_slice_in_dim(jnp.stack(grad_list), offset, micro_count, 0)
    summed_weight = lax.psum_scatter(
        jnp.einsum(
            "mtf,mta->fa", grad_store, attend_store, preferred_element_type=jnp.float32
        ).astype(jnp.bfloat16),
        "samples",
        scatter_dimension=0,
        tiled=True,
    ).astype(jnp.float32)
    region_count = seq_len // 2
    place_in = jnp.arange(seq_len)
    rank_in_region = (
        jnp.sum(jnp.where(place_in[None, :] <= place_in[:, None], region_mask[None, :], 0), axis=1) - 1
    )
    select = (
        (rank_in_region[None, :] == jnp.arange(region_count)[:, None]) & (region_mask[None, :] > 0)
    ).astype(jnp.bfloat16)
    tiles = jnp.einsum("at,mtd->mad", select, out_store, preferred_element_type=jnp.float32).astype(
        jnp.bfloat16
    )
    shard_index = lax.axis_index("samples")
    my_partners = lax.dynamic_slice_in_dim(
        partner_samples, shard_index * micro_count, micro_count, 0
    )
    shard_count = lax.axis_size("samples")
    dest_shard = my_partners // micro_count
    dest_slot = my_partners % micro_count
    route = (
        (dest_shard[:, None, None] == jnp.arange(shard_count)[None, :, None])
        & (dest_slot[:, None, None] == jnp.arange(micro_count)[None, None, :])
    ).astype(jnp.bfloat16)
    outgoing = jnp.einsum("mku,mad->kuad", route, tiles, preferred_element_type=jnp.float32).astype(
        jnp.bfloat16
    )
    arrived = lax.all_to_all(outgoing, "samples", split_axis=0, concat_axis=0, tiled=True)
    ones_row = jnp.ones((shard_count,), jnp.bfloat16)
    received = jnp.einsum(
        "k,kuad->uad", ones_row, arrived, preferred_element_type=jnp.float32
    ).astype(jnp.bfloat16)
    placed = jnp.einsum("at,mad->mtd", select, received, preferred_element_type=jnp.float32)
    kept = jnp.where(region_mask[None, :, None] > 0, jnp.zeros_like(out_store), out_store)
    site_cot = (kept.astype(jnp.float32) + placed).astype(jnp.bfloat16)
    cotangents = jnp.where(section_index == 0, site_cot, out_store)
    onehot = (spins[:, :, None] == jnp.arange(SPINS)[None, None, :]).astype(jnp.bfloat16)
    embed_term = jnp.einsum("mtv,mtd->vd", onehot, site_cot, preferred_element_type=jnp.float32)
    embed_term = jnp.where(section_index == 0, embed_term, jnp.zeros_like(embed_term))
    embed_grad = lax.psum(embed_term, ("samples", "section"))
    return (summed_weight[None], cotangents[None], embed_grad)


NZ = 4
NC = 4
PIECES = (False, True)
GROUPS = ((0,), (1,), (2,), (3,))
END_ORDER = (
    ("attE", 0), ("attE", 1), ("ga",), ("attE", 2), ("p2", 1), ("gb",),
    ("attE", 3), ("p01", 0), ("s0", 0), ("p01", 1), ("s1", 1), ("p2", 2),
    ("s0", 1), ("p01", 2), ("p2", 3), ("p01", 3), ("s1", 0), ("s1", 3),
    ("s0", 3), ("s0", 2), ("p2", 0), ("s2", 1), ("s2", 0), ("wt", 0),
    ("s1", 2), ("s2", 3), ("s2", 2), ("back", 0), ("back", 1), ("wt", 2),
    ("back", 3), ("wt", 1), ("back", 2), ("emb",), ("wt", 3), ("fin", 3),
    ("fin", 0), ("fin", 1), ("fin", 2), ("finw",), ("embw",),
)
INNER_ORDER = (
    ("gather",), ("attIi", 2), ("attIo", 0), ("attIo", 1), ("attIi", 1), ("attIi", 0),
    ("r3", 0), ("part", 0), ("attIo", 2), ("r1", 1), ("r3", 1), ("r1", 0),
    ("r1", 2), ("r0", 0), ("r3", 2), ("r3", 3), ("r0", 1), ("part", 2),
    ("far0", 0), ("part", 1), ("wt", 0), ("far0", 1), ("r0", 2), ("part", 3),
    ("wt", 1), ("far1", 1), ("near", 0), ("far1", 0), ("far0", 3), ("near", 1),
    ("wt", 2), ("attIi", 3), ("r0", 3), ("attIo", 3), ("far0", 2), ("near", 3),
    ("far1", 3), ("back", 0), ("back", 1), ("near", 2), ("far1", 2), ("r1", 3),
    ("back", 3), ("across", 0), ("across", 1), ("back", 2), ("emb",), ("wt", 3),
    ("across", 3), ("across", 2), ("fin", 0), ("fin", 1), ("fin", 2), ("fin", 3),
    ("finw",), ("embw",),
)
MESH = pl.DeviceIdType.MESH
F32 = jnp.float32
BF = jnp.bfloat16
T = jax.named_scope


def dot(a, b, ca=1, cb=0):
    return lax.dot_general(a, b, (((ca,), (cb,)), ((), ())), preferred_element_type=F32)


def kernel(
    x_hbm, g_hbm, w_hbm, layout_hbm, mask_hbm, partner_hbm, spin_hbm,
    wg_ref, cot_ref, emb_ref,
    x_ref, g_ref, layout_ref, mask_ref, partner_ref, spin_ref, gq, w2, pf, pb, near_in, far_in, att, probs, ga, g0,
    swz, xsend, xrecv, irecv, spall, embs, wsend, wrecv, wown,
    in_s, gq_s, gq_r, gf_s, gf_r, w_s, w_r, sp_s, sp_r, in_at_s, out_at_s, at_r, ps_s, near_r, far_r,
    sw_s, sw_r, xs_s, xs_r, si_r, em_s, em_r, wr_s, wr_r,
):
    s = lax.axis_index("samples")
    m = lax.axis_index("mp")
    z = s // 2
    x = s % 2
    flip = z < NZ // 2
    is_end = (z == 0) | (z == NZ - 1)
    outward = jnp.where(flip, -2, 2)
    scale = 4.0 / HEAD
    tokens, width = x_ref.shape
    heads = width // HEAD
    rows = w_hbm.shape[0]
    half = width // 2
    wide = width // NC
    per = wide // HEAD
    sibling = {"mp": 1 - m}
    beside = {"samples": 2 * z + 1 - x}
    inner_way = {"samples": lax.rem(s - outward + 8, 8)}
    outer_way = {"samples": lax.rem(s + outward + 8, 8)}

    def actual(n):
        return jnp.where(flip, NZ - 1 - n, n)

    def rdma(src, dst, ss, rs, dev):
        return pltpu.make_async_remote_copy(
            src_ref=src, dst_ref=dst, send_sem=ss, recv_sem=rs, device_id=dev, device_id_type=MESH
        )

    def send(cond, make):
        if cond is None:
            make().start()
        else:
            pl.when(cond)(lambda: make().start())

    def sent(cond, src, ss):
        def wait():
            rdma(src, src, ss, ss, sibling).wait_send()

        if cond is None:
            wait()
        else:
            pl.when(cond)(wait)

    def got(cond, dst, rs):
        def wait():
            rdma(dst, dst, rs, rs, sibling).wait_recv()

        if cond is None:
            wait()
        else:
            pl.when(cond)(wait)

    loads = [
        pltpu.make_async_copy(g_hbm, g_ref, in_s.at[0]),
        pltpu.make_async_copy(w_hbm, w2.at[x], in_s.at[1]),
        pltpu.make_async_copy(x_hbm, x_ref, in_s.at[2]),
        pltpu.make_async_copy(spin_hbm, spin_ref, in_s.at[3]),
        pltpu.make_async_copy(layout_hbm, layout_ref, in_s.at[4]),
        pltpu.make_async_copy(mask_hbm, mask_ref, in_s.at[5]),
        pltpu.make_async_copy(partner_hbm, partner_ref, in_s.at[6]),
    ]
    for load in loads:
        load.start()
    barrier = pltpu.get_barrier_semaphore()
    for k in range(1, 8):
        pl.semaphore_signal(
            barrier, inc=1, device_id={"samples": lax.rem(s + k, 8)}, device_id_type=MESH
        )
    pl.semaphore_signal(barrier, inc=1, device_id=sibling, device_id_type=MESH)
    for load in loads:
        load.wait()

    qb = lax.broadcasted_iota(jnp.int32, (tokens, tokens), 0) // BLOCK
    kb = lax.broadcasted_iota(jnp.int32, (tokens, tokens), 1) // BLOCK
    linked = jnp.where(qb < kb, layout_ref[0, 1], layout_ref[1, 0])
    allowed = (qb == kb) | (linked > 0)

    def attention():
        for h in range(heads):
            xh = x_ref[:, pl.ds(h * HEAD, HEAD)]
            scores = jnp.where(allowed, dot(xh, xh, 1, 1) * scale, -jnp.inf)
            expo = jnp.exp(scores - jnp.max(scores, axis=-1, keepdims=True))
            p = expo / jnp.sum(expo, axis=-1, keepdims=True)
            probs[h] = p
            att[h // per, z, :, pl.ds(h % per * HEAD, HEAD)] = dot(p.astype(BF), xh).astype(BF)

    @pl.when(flip)
    def _():
        with T("attn"):
            attention()

    with T("barrier"):
        pl.semaphore_wait(barrier, 8)

    for far in PIECES:
        jj = m if far else 1 - m
        dz = 2 * m + jj
        for_me = dz == z
        columns = pl.ds(pl.multiple_of(jj * half, half), half)
        piece = g_ref.at[:, columns]
        send(
            jnp.logical_not(for_me),
            lambda piece=piece, dz=dz: rdma(
                piece, gq.at[z], gq_s, gq_r.at[z], {"samples": 2 * dz + x}
            ),
        )
        send(
            for_me,
            lambda piece=piece: rdma(piece, gq.at[z], gq_s, gf_r.at[z], sibling),
        )

        @pl.when(for_me)
        def _(columns=columns):
            gq[z] = g_ref[:, columns]

    for c in range(NC):
        block = w2.at[x, :, pl.ds(c * wide, wide)]
        send(None, lambda block=block, c=c: rdma(block, block, w_s, w_r.at[c], beside))
    for k in range(1, 8):
        other = lax.rem(s + k, 8)
        send(
            None,
            lambda other=other: rdma(spin_ref, spall.at[s], sp_s, sp_r, {"samples": other}),
        )
    spall[s] = spin_ref[...]

    @pl.when(jnp.logical_not(flip))
    def _():
        with T("attn"):
            attention()

    mask = mask_ref[...]
    tri = (
        lax.broadcasted_iota(jnp.int32, (tokens, tokens), 0)
        <= lax.broadcasted_iota(jnp.int32, (tokens, tokens), 1)
    ).astype(F32).astype(BF)
    mask_rows = jnp.broadcast_to(mask, (8, tokens)).astype(F32)
    rank = dot(mask_rows.astype(BF), tri)[:1] - 1.0
    region = tokens // 2
    place = lax.broadcasted_iota(jnp.int32, (region, tokens), 0).astype(F32)
    select = jnp.where((rank == place) & (mask > 0), 1.0, 0.0).astype(BF)

    first_core = m == z // 2

    def gather(order, own):
        for n in order:
            zz = actual(n)
            got(first_core, gq.at[zz], gq_r.at[zz])
            send(
                first_core,
                lambda zz=zz: rdma(gq.at[zz], gq.at[zz], gf_s, gf_r.at[zz], sibling),
            )
        for n in (own, *order) if own else order:
            zz = actual(n)
            got(jnp.logical_not(first_core), gq.at[zz], gf_r.at[zz])

    def att_to(c, n, slot, inward):
        zz = actual(n)
        way, ss = (inner_way, in_at_s) if inward else (outer_way, out_at_s)
        send(None, lambda: rdma(att.at[c, zz], att.at[c, zz], ss, at_r.at[c, slot], way))

    def att_got(c, n, slot):
        got(None, att.at[c, actual(n)], at_r.at[c, slot])

    def weights_in(c):
        got(None, w2.at[1 - x, :, pl.ds(c * wide, wide)], w_r.at[c])

    def partials(c, first, count):
        cols = pl.ds(c * wide, wide)
        some = gq[pl.ds(first, count)].reshape(count * tokens, 2 * rows)
        sums = dot(some[:, :rows], w2[0, :, cols]) + dot(some[:, rows:], w2[1, :, cols])
        return sums.reshape(count, tokens, wide)

    def weight_terms(c):
        total = jnp.zeros((2 * rows, wide), F32)
        for zz in range(NZ):
            total += dot(gq[zz], att[c, zz], 0, 0).astype(BF).astype(F32)
        cols = pl.ds(c * wide, wide)

        @pl.when(x == 0)
        def _():
            wown[:, cols] = total[:rows]
            wsend[c] = total[rows:].astype(BF)

        @pl.when(x == 1)
        def _():
            wown[:, cols] = total[rows:]
            wsend[c] = total[:rows].astype(BF)

        send(None, lambda: rdma(wsend.at[c], wrecv.at[c], wr_s, wr_r, beside))

    def backward(b, total_of):
        chunks = GROUPS[b]
        for c in chunks:
            ga[:, c * wide : (c + 1) * wide] = total_of(c).astype(BF)
        for h in range(chunks[0] * per, (chunks[-1] + 1) * per):
            cols = slice(h * HEAD, (h + 1) * HEAD)
            xh = x_ref[:, cols]
            gh = ga[:, cols]
            p = probs[h]
            gp = dot(gh, xh, 1, 1)
            gs = (p * (gp - jnp.sum(gp * p, axis=-1, keepdims=True))).astype(BF)
            through = dot(p.astype(BF), gh, 0, 0) + scale * (dot(gs, xh) + dot(gs, xh, 0, 0))
            g0[:, cols] = (g_ref[:, cols].astype(F32) + through).astype(BF)
        for c in chunks:
            swz[c, s % 4] = dot(select, g0[:, c * wide : (c + 1) * wide]).astype(BF)

    def tile_to(b, other):
        rows_now = swz.at[pl.ds(GROUPS[b][0], len(GROUPS[b])), s % 4]
        send(
            None,
            lambda: rdma(rows_now, rows_now, sw_s, sw_r.at[b, s % 4], {"samples": other}),
        )

    def rows_of(c, which):
        rows_now = swz[c, 0]
        for k in range(1, 4):
            rows_now = jnp.where(which == k, swz[c, k], rows_now)
        return rows_now

    def embed():
        got(None, spall.at[pl.ds(0, 7)], sp_r)
        spins = jnp.where(mask > 0, spall[partner_ref[s]], spin_ref[...])
        onehot = jnp.where(
            spins == lax.broadcasted_iota(jnp.int32, (8, tokens), 0), 1.0, 0.0
        ).astype(BF)
        embs[s] = dot(onehot, g0[...])[:SPINS]
        for k in range(1, 8):
            other = lax.rem(s + k, 8)
            send(
                None,
                lambda other=other: rdma(embs.at[s], embs.at[s], em_s, em_r, {"samples": other}),
            )

    mine = partner_ref[s]
    eye = lax.broadcasted_iota(jnp.int32, (tokens, tokens), 0) == lax.broadcasted_iota(
        jnp.int32, (tokens, tokens), 1
    )
    keep = jnp.where(eye & (mask == 0), 1.0, 0.0).astype(BF)

    def rows_in(b, other_of):
        chunks = GROUPS[b]
        got(None, xrecv.at[pl.ds(chunks[0], len(chunks))], xs_r.at[b])
        for c in chunks:
            cols = slice(c * wide, (c + 1) * wide)
            chosen = jnp.where(mine // 4 == s // 4, other_of(c), xrecv[c])
            cot_ref[:, cols] = (dot(keep, g0[:, cols]) + dot(select, chosen, 0, 0)).astype(BF)

    def embed_sum():
        got(None, embs.at[pl.ds(0, 7)], em_r)
        total = embs[0]
        for k in range(1, 8):
            total += embs[k]
        emb_ref[...] = total

    def weights_out():
        got(None, wrecv, wr_r)
        for c in range(NC):
            cols = slice(c * wide, (c + 1) * wide)
            wg_ref[:, cols] = wown[:, cols] + wrecv[c].astype(F32)

    def end_tasks():
        def total_of(c):
            got(None, far_in.at[c, 0], far_r.at[c, 0])
            return pf[c, actual(3)] + far_in[c, 0].astype(F32)

        def part_out(c, n):
            zz = actual(n)
            send(
                None,
                lambda: rdma(
                    pb.at[c, zz], near_in.at[c, n], ps_s, near_r.at[c, n], inner_way
                ),
            )

        weights_seen = set()

        def weights(c):
            if c not in weights_seen:
                weights_seen.add(c)
                weights_in(c)

        def p2(c):
            weights(c)
            first = jnp.where(flip, 0, 2)
            sums = partials(c, first, 2)
            pf[c, pl.ds(first, 2)] = sums
            pb[c, pl.ds(first, 2)] = sums.astype(BF)

        def p01(c):
            weights(c)
            first = jnp.where(flip, 2, 0)
            pb[c, pl.ds(first, 2)] = partials(c, first, 2).astype(BF)

        def back(b):
            backward(b, total_of)
            tile_to(b, s - outward + 1 - 2 * x)
            tile_to(b, s - outward)

        def fin(b):
            got(None, irecv.at[pl.ds(GROUPS[b][0], len(GROUPS[b]))], si_r.at[b])
            rows_in(b, lambda c: irecv[c])

        def wt(c):
            for slot in range(3):
                att_got(c, 2 - slot, slot)
            weight_terms(c)

        return {
            "ga": lambda: gather((2,), 3),
            "gb": lambda: gather((1, 0), None),
            "attE": lambda c: att_to(c, 3, 0, True),
            "s0": lambda c: part_out(c, 0), "s1": lambda c: part_out(c, 1), "s2": lambda c: part_out(c, 2),
            "p2": p2, "p01": p01, "wt": wt,
            "back": back, "emb": embed, "fin": fin, "finw": weights_out, "embw": embed_sum,
        }

    def inner_tasks():
        def total_of(c):
            got(None, near_in.at[c, 2], near_r.at[c, 2])
            got(None, far_in.at[c, 1], far_r.at[c, 1])
            return pf[c, actual(2)] + near_in[c, 2].astype(F32) + far_in[c, 1].astype(F32)

        def part(c):
            weights_in(c)
            pf[c] = partials(c, 0, NZ)

        def far(c, n):
            got(None, near_in.at[c, n], near_r.at[c, n])
            pb[c, n] = (pf[c, actual(n)] + near_in[c, n].astype(F32)).astype(BF)
            send(
                None,
                lambda: rdma(pb.at[c, n], far_in.at[c, n], ps_s, far_r.at[c, n], inner_way),
            )

        def near(c):
            got(None, far_in.at[c, 0], far_r.at[c, 0])
            pb[c, 3] = (pf[c, actual(3)] + far_in[c, 0].astype(F32)).astype(BF)
            send(
                None,
                lambda: rdma(pb.at[c, 3], far_in.at[c, 0], ps_s, far_r.at[c, 0], outer_way),
            )

        def back(b):
            backward(b, total_of)
            tile_to(b, 2 * z + 1 - x)

        def across(b):
            part = pl.ds(GROUPS[b][0], len(GROUPS[b]))
            for k in range(1, 4):
                got(None, swz.at[part, 0], sw_r.at[b, lax.rem(s + k, 4)])
            for k, dest in enumerate((s - 2 * outward, s - outward, s + outward)):
                wanted = lax.rem(partner_ref[dest], 4)
                for c in GROUPS[b]:
                    xsend[k, c] = rows_of(c, wanted)
                into, rs = (irecv, si_r) if k == 2 else (xrecv, xs_r)
                send(
                    None,
                    lambda k=k, dest=dest, into=into, rs=rs: rdma(
                        xsend.at[k, part], into.at[part], xs_s, rs.at[b], {"samples": dest}
                    ),
                )

        def fin(b):
            rows_in(b, lambda c: rows_of(c, lax.rem(mine, 4)))

        def relay(n, slot, to_slot, inward):
            def run(c):
                att_got(c, n, slot)
                att_to(c, n, to_slot, inward)

            return run

        return {
            "gather": lambda: gather((3, 1, 0), 2),
            "attIi": lambda c: att_to(c, 2, 1, True), "attIo": lambda c: att_to(c, 2, 0, False),
            "part": part, "near": near,
            "far0": lambda c: far(c, 0), "far1": lambda c: far(c, 1),
            "r3": relay(3, 0, 2, True),
            "r1": relay(1, 1, 1, False),
            "r0": relay(0, 2, 2, False),
            "wt": weight_terms, "back": back, "across": across, "emb": embed, "fin": fin, "finw": weights_out,
            "embw": embed_sum,
        }

    def run(tasks, order):
        for name, *at in order:
            with T("_".join([name, *map(str, at)])):
                tasks[name](*at)

    @pl.when(is_end)
    def _():
        run(end_tasks(), END_ORDER)
        sent(None, att.at[:, 0], in_at_s)
        sent(None, swz.at[:, pl.ds(0, 2)], sw_s)

    @pl.when(jnp.logical_not(is_end))
    def _():
        run(inner_tasks(), INNER_ORDER)
        sent(None, att.at[:, pl.ds(0, 2)], in_at_s)
        sent(None, att.at[:, pl.ds(0, 3)], out_at_s)
        sent(None, swz.at[:, 0], sw_s)
        sent(None, xsend, xs_s)

    with T("sends_done"):
        sent(None, g_ref, gq_s)
        sent(first_core, gq.at[pl.ds(0, 3)], gf_s)
        sent(None, w2.at[0], w_s)
        sent(None, spall.at[pl.ds(0, 7)], sp_s)
        sent(None, embs.at[pl.ds(0, 7)], em_s)
        sent(None, pb.at[:, pl.ds(0, 3)], ps_s)
        sent(None, wsend, wr_s)


def put_out(wg_ref, cot_ref, emb_ref, wg_out, cot_out, emb_out, done):
    copies = [
        pltpu.make_async_copy(wg_ref, wg_out, done.at[0]),
        pltpu.make_async_copy(cot_ref, cot_out, done.at[1]),
        pltpu.make_async_copy(emb_ref, emb_out, done.at[2]),
    ]
    for copy in copies:
        copy.start()
    for copy in copies:
        copy.wait()


def one_layer(
    stored_inputs, top_cotangent, layer_weights, block_layout, region_mask, partner_samples, spins
):
    tokens, width = stored_inputs.shape[2:]
    rows = layer_weights.shape[1]
    hbm = pl.BlockSpec(memory_space=pltpu.HBM)
    vmem = pl.BlockSpec(memory_space=pltpu.VMEM)
    region = tokens // 2
    dma = pltpu.SemaphoreType.DMA
    half = width // 2
    wide = width // NC
    shapes = [
        ((NZ, tokens, 2 * rows), BF),
        ((2, rows, width), BF),
        ((NC, NZ, tokens, wide), F32),
        ((NC, NZ, tokens, wide), BF),
        ((NC, 3, tokens, wide), BF),
        ((NC, 2, tokens, wide), BF),
        ((NC, NZ, tokens, wide), BF),
        ((width // HEAD, tokens, tokens), F32),
        ((tokens, width), BF),
        ((tokens, width), BF),
        ((NC, 4, region, wide), BF),
        ((3, NC, region, wide), BF),
        ((NC, region, wide), BF),
        ((NC, region, wide), BF),
        ((8, 1, tokens), jnp.int32),
        ((8, SPINS, width), F32),
        ((NC, rows, wide), BF),
        ((NC, rows, wide), BF),
        ((rows, width), F32),
    ]
    one = dma
    sems = [
        dma((7,)), one, dma((NZ,)), one, dma((NZ,)), one, dma((NC,)), one, one, one, one, dma((NC, 3)), one,
        dma((NC, 3)), dma((NC, 2)), one, dma((len(GROUPS), 4)), one, dma((len(GROUPS),)), dma((len(GROUPS),)),
        one, one, one, one,
    ]
    wg, cot, emb = pl.pallas_call(
        kernel,
        out_shape=[
            jax.ShapeDtypeStruct((rows, width), F32),
            jax.ShapeDtypeStruct((tokens, width), BF),
            jax.ShapeDtypeStruct((SPINS, width), F32),
        ],
        in_specs=[hbm] * 7,
        out_specs=[vmem] * 3,
        scratch_shapes=[
            pltpu.VMEM((tokens, width), BF),
            pltpu.VMEM((tokens, width), BF),
            pltpu.SMEM((2, 2), jnp.int32),
            pltpu.VMEM((1, tokens), jnp.int32),
            pltpu.SMEM((8,), jnp.int32),
            pltpu.VMEM((1, tokens), jnp.int32),
        ]
        + [pltpu.VMEM(a, b) for a, b in shapes]
        + sems,
        compiler_params=pltpu.CompilerParams(
            collective_id=0, has_side_effects=True, vmem_limit_bytes=48 * 1024 * 1024
        ),
    )(
        *[
            pltpu.with_memory_space_constraint(value, pltpu.HBM)
            for value in (
                stored_inputs[0, 0], top_cotangent[0], layer_weights[0], block_layout[0],
                region_mask[None], partner_samples, spins,
            )
        ]
    )
    anywhere = pl.BlockSpec(memory_space=pl.ANY)
    wg, cot, emb = pl.pallas_call(
        put_out,
        out_shape=[jax.ShapeDtypeStruct(a.shape, a.dtype) for a in (wg, cot, emb)],
        in_specs=[vmem] * 3,
        out_specs=[anywhere] * 3,
        scratch_shapes=[dma((3,))],
        compiler_params=pltpu.CompilerParams(vmem_limit_bytes=8 * 1024 * 1024),
    )(wg, cot, emb)
    return wg[None], cot[None, None], emb


def solution(mesh):
    in_specs = (
        P("section", ("groups", "samples"), None, "mp"),
        P(("groups", "samples"), None, "mp"),
        P("section", "samples", "mp"),
        P("section", None, None),
        P(),
        P("groups"),
        P(("groups", "samples"), None),
    )
    out_specs = (
        P(("groups", "section"), "samples", "mp"),
        P("section", ("groups", "samples"), None, "mp"),
        P("groups", "mp"),
    )
    small = mesh.shape["samples"] == 8 and mesh.shape["section"] == 1 and mesh.shape["mp"] == 2
    body = one_layer if small else local
    return jax.shard_map(body, mesh=mesh, in_specs=in_specs, out_specs=out_specs, check_vma=False)
```

```python
import jax
import jax.numpy as jnp
from jax import lax
from jax.experimental import pallas as pl
from jax.experimental.pallas import tpu as pltpu
from jax.sharding import PartitionSpec as P

HEAD = 128
BLOCK = 64
SPINS = 2


def for_sending(value):

    def short(part):
        return part.astype(jnp.bfloat16) if part.dtype == jnp.float32 else part

    return jax.tree.map(short, value)


def passed_along(block, axis, distance):
    devices = range(lax.axis_size(axis))
    route = [(i - distance, i) for i in devices if i - distance in devices]
    return lax.ppermute(block, axis, route)


def softmax_parts(inputs_h, allowed, attention_scale):
    scores = (
        jnp.einsum("qhd,khd->hqk", inputs_h, inputs_h, preferred_element_type=jnp.float32)
        * attention_scale
    )
    scores = jnp.where(allowed[None], scores, -jnp.inf)
    top_score = jnp.max(scores, axis=-1, keepdims=True)
    expo_terms = jnp.exp(scores - top_score)
    probs = expo_terms / jnp.sum(expo_terms, axis=-1, keepdims=True)
    return (probs, probs.astype(jnp.bfloat16))


def local(
    stored_inputs, top_cotangent, layer_weights, block_layout, region_mask, partner_samples, spins
):
    section_index = lax.axis_index("section")
    section_count = lax.axis_size("section")
    micro_count = stored_inputs.shape[1]
    seq_len = stored_inputs.shape[2]
    half_width = stored_inputs.shape[3]
    head_count = half_width // HEAD
    attention_scale = 4.0 / HEAD
    weights = lax.all_gather(layer_weights[0], "samples", axis=0, tiled=True)
    pos_block = jnp.arange(seq_len) // BLOCK
    block_onehot = (pos_block[:, None] == jnp.arange(block_layout.shape[1])[None, :]).astype(
        jnp.float32
    )
    linked = jnp.dot(jnp.dot(block_onehot, block_layout[0].astype(jnp.float32)), block_onehot.T)
    allowed = (linked > 0.5) | (pos_block[:, None] == pos_block[None, :])
    every_layer_input = stored_inputs[0]
    inputs_h = every_layer_input[0].reshape(seq_len, head_count, HEAD)
    probs, probs_low = softmax_parts(inputs_h, allowed, attention_scale)
    attended = jnp.einsum(
        "hqk,khd->qhd", probs_low, inputs_h, preferred_element_type=jnp.float32
    ).astype(jnp.bfloat16)
    probs_list = [probs]
    low_list = [probs_low]
    attend_list = [attended.reshape(seq_len, half_width)]
    probs_all = jnp.stack(probs_list)
    low_all = jnp.stack(low_list)
    attend_store = jnp.stack(attend_list)

    def layer_back(grad_full, grad_own, inputs, probs, probs_low):
        grad_attn = jnp.dot(grad_full, weights, preferred_element_type=jnp.float32).astype(
            jnp.bfloat16
        )
        inputs_h = inputs.reshape(seq_len, head_count, HEAD)
        grad_h = grad_attn.reshape(seq_len, head_count, HEAD)
        grad_probs = jnp.einsum(
            "qhd,khd->hqk", grad_h, inputs_h, preferred_element_type=jnp.float32
        )
        grad_scores = (
            probs * (grad_probs - jnp.sum(grad_probs * probs, axis=-1, keepdims=True))
        ).astype(jnp.bfloat16)
        through = jnp.einsum("hqk,qhd->khd", probs_low, grad_h, preferred_element_type=jnp.float32)
        through = through + attention_scale * (
            jnp.einsum("hqk,khd->qhd", grad_scores, inputs_h, preferred_element_type=jnp.float32)
            + jnp.einsum("hqk,qhd->khd", grad_scores, inputs_h, preferred_element_type=jnp.float32)
        )
        grad_in = grad_own.astype(jnp.float32) + through.reshape(seq_len, half_width)
        return grad_in.astype(jnp.bfloat16)

    def resting(grad_full, grad_own, inputs, probs, probs_low):
        return jnp.zeros((seq_len, half_width), jnp.bfloat16)

    carried_state = jnp.zeros((seq_len, half_width), jnp.bfloat16)
    out_list = []
    grad_list = []
    total_steps = micro_count + section_count - 1
    for step_number in range(total_steps):
        micro_index = step_number - (section_count - 1 - section_index)
        active = (micro_index >= 0) & (micro_index < micro_count)
        slot_index = jnp.clip(micro_index, 0, micro_count - 1)
        from_top = lax.dynamic_index_in_dim(top_cotangent, slot_index, 0, keepdims=False)
        incoming = jnp.where(section_index == section_count - 1, from_top, carried_state)
        grad_full = lax.all_gather(incoming, "mp", axis=1, tiled=True)
        inputs_now = lax.dynamic_index_in_dim(every_layer_input, slot_index, 0, keepdims=False)
        probs_now = lax.dynamic_index_in_dim(probs_all, slot_index, 0, keepdims=False)
        low_now = lax.dynamic_index_in_dim(low_all, slot_index, 0, keepdims=False)
        grad_in = lax.cond(
            active, layer_back, resting, grad_full, incoming, inputs_now, probs_now, low_now
        )
        out_list.append(grad_in)
        grad_list.append(grad_full)
        if step_number < total_steps - 1:
            carried_state = jax.tree.map(
                lambda part, own: part.astype(own.dtype),
                passed_along(for_sending(grad_in), "section", -1),
                grad_in,
            )
    offset = section_count - 1 - section_index
    out_store = lax.dynamic_slice_in_dim(jnp.stack(out_list), offset, micro_count, 0)
    grad_store = lax.dynamic_slice_in_dim(jnp.stack(grad_list), offset, micro_count, 0)
    summed_weight = lax.psum_scatter(
        jnp.einsum(
            "mtf,mta->fa", grad_store, attend_store, preferred_element_type=jnp.float32
        ).astype(jnp.bfloat16),
        "samples",
        scatter_dimension=0,
        tiled=True,
    ).astype(jnp.float32)
    region_count = seq_len // 2
    place_in = jnp.arange(seq_len)
    rank_in_region = (
        jnp.sum(jnp.where(place_in[None, :] <= place_in[:, None], region_mask[None, :], 0), axis=1) - 1
    )
    select = (
        (rank_in_region[None, :] == jnp.arange(region_count)[:, None]) & (region_mask[None, :] > 0)
    ).astype(jnp.bfloat16)
    tiles = jnp.einsum("at,mtd->mad", select, out_store, preferred_element_type=jnp.float32).astype(
        jnp.bfloat16
    )
    shard_index = lax.axis_index("samples")
    my_partners = lax.dynamic_slice_in_dim(
        partner_samples, shard_index * micro_count, micro_count, 0
    )
    shard_count = lax.axis_size("samples")
    dest_shard = my_partners // micro_count
    dest_slot = my_partners % micro_count
    route = (
        (dest_shard[:, None, None] == jnp.arange(shard_count)[None, :, None])
        & (dest_slot[:, None, None] == jnp.arange(micro_count)[None, None, :])
    ).astype(jnp.bfloat16)
    outgoing = jnp.einsum("mku,mad->kuad", route, tiles, preferred_element_type=jnp.float32).astype(
        jnp.bfloat16
    )
    arrived = lax.all_to_all(outgoing, "samples", split_axis=0, concat_axis=0, tiled=True)
    ones_row = jnp.ones((shard_count,), jnp.bfloat16)
    received = jnp.einsum(
        "k,kuad->uad", ones_row, arrived, preferred_element_type=jnp.float32
    ).astype(jnp.bfloat16)
    placed = jnp.einsum("at,mad->mtd", select, received, preferred_element_type=jnp.float32)
    kept = jnp.where(region_mask[None, :, None] > 0, jnp.zeros_like(out_store), out_store)
    site_cot = (kept.astype(jnp.float32) + placed).astype(jnp.bfloat16)
    cotangents = jnp.where(section_index == 0, site_cot, out_store)
    onehot = (spins[:, :, None] == jnp.arange(SPINS)[None, None, :]).astype(jnp.bfloat16)
    embed_term = jnp.einsum("mtv,mtd->vd", onehot, site_cot, preferred_element_type=jnp.float32)
    embed_term = jnp.where(section_index == 0, embed_term, jnp.zeros_like(embed_term))
    embed_grad = lax.psum(embed_term, ("samples", "section"))
    return (summed_weight[None], cotangents[None], embed_grad)


NZ = 4
NC = 4
GROUPS = ((0,), (1,), (2,), (3,))
END_ORDER = (
    ("attE", 0), ("attE", 1), ("ga",), ("attE", 2), ("p2", 1), ("gb",),
    ("attE", 3), ("p01", 0), ("s0", 0), ("p01", 1), ("s1", 1), ("p2", 2),
    ("s0", 1), ("p01", 2), ("p2", 3), ("p01", 3), ("s1", 0), ("s1", 3),
    ("s0", 3), ("s0", 2), ("p2", 0), ("s2", 1), ("s2", 0), ("wt", 0),
    ("s1", 2), ("s2", 3), ("s2", 2), ("back", 0), ("back", 1), ("wt", 2),
    ("back", 3), ("wt", 1), ("back", 2), ("emb",), ("wt", 3), ("fin", 3),
    ("fin", 0), ("fin", 1), ("fin", 2), ("finw",), ("embw",),
)
INNER_ORDER = (
    ("gather",), ("attIi", 2), ("attIo", 0), ("attIo", 1), ("attIi", 1), ("attIi", 0),
    ("r3", 0), ("part", 0), ("attIo", 2), ("r1", 1), ("r3", 1), ("r1", 0),
    ("r1", 2), ("r0", 0), ("r3", 2), ("r3", 3), ("r0", 1), ("part", 2),
    ("far0", 0), ("part", 1), ("wt", 0), ("far0", 1), ("r0", 2), ("part", 3),
    ("wt", 1), ("far1", 1), ("near", 0), ("far1", 0), ("far0", 3), ("near", 1),
    ("wt", 2), ("attIi", 3), ("r0", 3), ("attIo", 3), ("far0", 2), ("near", 3),
    ("far1", 3), ("back", 0), ("back", 1), ("near", 2), ("far1", 2), ("r1", 3),
    ("back", 3), ("across", 0), ("across", 1), ("back", 2), ("emb",), ("wt", 3),
    ("across", 3), ("across", 2), ("fin", 0), ("fin", 1), ("fin", 2), ("fin", 3),
    ("finw",), ("embw",),
)
MESH = pl.DeviceIdType.MESH
F32 = jnp.float32
BF = jnp.bfloat16
T = jax.named_scope


def dot(a, b, ca=1, cb=0):
    return lax.dot_general(a, b, (((ca,), (cb,)), ((), ())), preferred_element_type=F32)


def kernel(
    x_hbm, g_hbm, w_hbm, layout_hbm, mask_hbm, partner_hbm, spin_hbm,
    wg_ref, cot_ref, emb_ref,
    x_ref, g_ref, layout_ref, mask_ref, partner_ref, spin_ref, gq, w2, pf, pb, near_in, far_in, att, probs, ga, g0,
    swz, xsend, xrecv, irecv, spall, embs, wsend, wrecv, wown,
    in_s, gq_s, gq_r, gf_s, gf_r, w_s, w_r, sp_s, sp_r, in_at_s, out_at_s, at_r, ps_s, near_r, far_r,
    sw_s, sw_r, xs_s, xs_r, si_r, em_s, em_r, wr_s, wr_r, last_in,
):
    s = lax.axis_index("samples")
    m = lax.axis_index("mp")
    z = s // 2
    x = s % 2
    flip = z < NZ // 2
    is_end = (z == 0) | (z == NZ - 1)
    outward = jnp.where(flip, -2, 2)
    scale = 4.0 / HEAD
    tokens, width = x_ref.shape
    heads = width // HEAD
    rows = w_hbm.shape[0]
    half = width // 2
    wide = width // NC
    per = wide // HEAD
    sibling = {"mp": 1 - m}
    beside = {"samples": 2 * z + 1 - x}
    inner_way = {"samples": lax.rem(s - outward + 8, 8)}
    outer_way = {"samples": lax.rem(s + outward + 8, 8)}

    def actual(n):
        return jnp.where(flip, NZ - 1 - n, n)

    def rdma(src, dst, ss, rs, dev):
        return pltpu.make_async_remote_copy(
            src_ref=src, dst_ref=dst, send_sem=ss, recv_sem=rs, device_id=dev, device_id_type=MESH
        )

    def send(cond, make):
        if cond is None:
            make().start()
        else:
            pl.when(cond)(lambda: make().start())

    def sent(cond, src, ss):
        def wait():
            rdma(src, src, ss, ss, sibling).wait_send()

        if cond is None:
            wait()
        else:
            pl.when(cond)(wait)

    def got(cond, dst, rs):
        def wait():
            rdma(dst, dst, rs, rs, sibling).wait_recv()

        if cond is None:
            wait()
        else:
            pl.when(cond)(wait)

    loads = [
        pltpu.make_async_copy(g_hbm, g_ref, in_s.at[0]),
        pltpu.make_async_copy(w_hbm, w2.at[x], in_s.at[1]),
        pltpu.make_async_copy(x_hbm, x_ref, in_s.at[2]),
        pltpu.make_async_copy(spin_hbm, spin_ref, in_s.at[3]),
        pltpu.make_async_copy(layout_hbm, layout_ref, in_s.at[4]),
        pltpu.make_async_copy(mask_hbm, mask_ref, in_s.at[5]),
        pltpu.make_async_copy(partner_hbm, partner_ref, in_s.at[6]),
    ]
    for load in loads:
        load.start()
    barrier = pltpu.get_barrier_semaphore()
    is_last = z == NZ - 1
    for k in range(1, 8):
        other = lax.rem(s + k, 8)

        @pl.when(jnp.logical_not(is_last) | (other // 2 == NZ - 1))
        def _(other=other):
            pl.semaphore_signal(
                barrier, inc=1, device_id={"samples": other}, device_id_type=MESH
            )

    pl.semaphore_signal(barrier, inc=1, device_id=sibling, device_id_type=MESH)
    for load in loads:
        load.wait()

    qb = lax.broadcasted_iota(jnp.int32, (tokens, tokens), 0) // BLOCK
    kb = lax.broadcasted_iota(jnp.int32, (tokens, tokens), 1) // BLOCK
    linked = jnp.where(qb < kb, layout_ref[0, 1], layout_ref[1, 0])
    allowed = (qb == kb) | (linked > 0)

    def attention():
        for h in range(heads):
            xh = x_ref[:, pl.ds(h * HEAD, HEAD)]
            scores = jnp.where(allowed, dot(xh, xh, 1, 1) * scale, -jnp.inf)
            expo = jnp.exp(scores - jnp.max(scores, axis=-1, keepdims=True))
            p = expo / jnp.sum(expo, axis=-1, keepdims=True)
            probs[h] = p
            att[h // per, z, :, pl.ds(h % per * HEAD, HEAD)] = dot(p.astype(BF), xh).astype(BF)

    @pl.when(flip)
    def _():
        with T("attn"):
            attention()

    with T("barrier"):
        pl.semaphore_wait(barrier, jnp.where(is_last, 8, 6))

    @pl.when(is_last)
    def _():
        for k in range(1, NZ):
            pl.semaphore_signal(
                last_in, inc=1, device_id={"samples": s - 2 * k}, device_id_type=MESH
            )

    def piece_out(far, cond):
        jj = m if far else 1 - m
        dz = 2 * m + jj
        columns = pl.ds(pl.multiple_of(jj * half, half), half)
        piece = g_ref.at[:, columns]
        send(
            cond & (dz != z),
            lambda: rdma(piece, gq.at[z], gq_s, gq_r.at[z], {"samples": 2 * dz + x}),
        )
        send(cond & (dz == z), lambda: rdma(piece, gq.at[z], gq_s, gf_r.at[z], sibling))

        @pl.when(cond & (dz == z))
        def _():
            gq[z] = g_ref[:, columns]

    to_last = (m == 1) & jnp.logical_not(is_last)
    piece_out(False, m < 2)
    piece_out(True, jnp.logical_not(to_last))
    for c in range(NC):
        block = w2.at[x, :, pl.ds(c * wide, wide)]
        send(None, lambda block=block, c=c: rdma(block, block, w_s, w_r.at[c], beside))
    spall[s] = spin_ref[...]

    @pl.when(jnp.logical_not(flip))
    def _():
        with T("attn"):
            attention()

    @pl.when(jnp.logical_not(is_last))
    def _():
        with T("last"):
            pl.semaphore_wait(last_in, 1)

    piece_out(True, to_last)
    for k in range(1, 8):
        other = lax.rem(s + k, 8)
        send(
            None,
            lambda other=other: rdma(spin_ref, spall.at[s], sp_s, sp_r, {"samples": other}),
        )

    mask = mask_ref[...]
    tri = (
        lax.broadcasted_iota(jnp.int32, (tokens, tokens), 0)
        <= lax.broadcasted_iota(jnp.int32, (tokens, tokens), 1)
    ).astype(F32).astype(BF)
    mask_rows = jnp.broadcast_to(mask, (8, tokens)).astype(F32)
    rank = dot(mask_rows.astype(BF), tri)[:1] - 1.0
    region = tokens // 2
    place = lax.broadcasted_iota(jnp.int32, (region, tokens), 0).astype(F32)
    select = jnp.where((rank == place) & (mask > 0), 1.0, 0.0).astype(BF)

    first_core = m == z // 2

    def gather(order, own):
        for n in order:
            zz = actual(n)
            got(first_core, gq.at[zz], gq_r.at[zz])
            send(
                first_core,
                lambda zz=zz: rdma(gq.at[zz], gq.at[zz], gf_s, gf_r.at[zz], sibling),
            )
        for n in (own, *order) if own else order:
            zz = actual(n)
            got(jnp.logical_not(first_core), gq.at[zz], gf_r.at[zz])

    def att_to(c, n, slot, inward):
        zz = actual(n)
        way, ss = (inner_way, in_at_s) if inward else (outer_way, out_at_s)
        send(None, lambda: rdma(att.at[c, zz], att.at[c, zz], ss, at_r.at[c, slot], way))

    def att_got(c, n, slot):
        got(None, att.at[c, actual(n)], at_r.at[c, slot])

    def weights_in(c):
        got(None, w2.at[1 - x, :, pl.ds(c * wide, wide)], w_r.at[c])

    def partials(c, first, count):
        cols = pl.ds(c * wide, wide)
        some = gq[pl.ds(first, count)].reshape(count * tokens, 2 * rows)
        sums = dot(some[:, :rows], w2[0, :, cols]) + dot(some[:, rows:], w2[1, :, cols])
        return sums.reshape(count, tokens, wide)

    def weight_terms(c):
        total = jnp.zeros((2 * rows, wide), F32)
        for zz in range(NZ):
            total += dot(gq[zz], att[c, zz], 0, 0).astype(BF).astype(F32)
        cols = pl.ds(c * wide, wide)

        @pl.when(x == 0)
        def _():
            wown[:, cols] = total[:rows]
            wsend[c] = total[rows:].astype(BF)

        @pl.when(x == 1)
        def _():
            wown[:, cols] = total[rows:]
            wsend[c] = total[:rows].astype(BF)

        send(None, lambda: rdma(wsend.at[c], wrecv.at[c], wr_s, wr_r, beside))

    def backward(b, total_of):
        chunks = GROUPS[b]
        for c in chunks:
            ga[:, c * wide : (c + 1) * wide] = total_of(c).astype(BF)
        for h in range(chunks[0] * per, (chunks[-1] + 1) * per):
            cols = slice(h * HEAD, (h + 1) * HEAD)
            xh = x_ref[:, cols]
            gh = ga[:, cols]
            p = probs[h]
            gp = dot(gh, xh, 1, 1)
            gs = (p * (gp - jnp.sum(gp * p, axis=-1, keepdims=True))).astype(BF)
            through = dot(p.astype(BF), gh, 0, 0) + scale * (dot(gs, xh) + dot(gs, xh, 0, 0))
            g0[:, cols] = (g_ref[:, cols].astype(F32) + through).astype(BF)
        for c in chunks:
            swz[c, s % 4] = dot(select, g0[:, c * wide : (c + 1) * wide]).astype(BF)

    def tile_to(b, other):
        rows_now = swz.at[pl.ds(GROUPS[b][0], len(GROUPS[b])), s % 4]
        send(
            None,
            lambda: rdma(rows_now, rows_now, sw_s, sw_r.at[b, s % 4], {"samples": other}),
        )

    def rows_of(c, which):
        rows_now = swz[c, 0]
        for k in range(1, 4):
            rows_now = jnp.where(which == k, swz[c, k], rows_now)
        return rows_now

    def embed():
        got(None, spall.at[pl.ds(0, 7)], sp_r)
        spins = jnp.where(mask > 0, spall[partner_ref[s]], spin_ref[...])
        onehot = jnp.where(
            spins == lax.broadcasted_iota(jnp.int32, (8, tokens), 0), 1.0, 0.0
        ).astype(BF)
        embs[s] = dot(onehot, g0[...])[:SPINS]
        for k in range(1, 8):
            other = lax.rem(s + k, 8)
            send(
                None,
                lambda other=other: rdma(embs.at[s], embs.at[s], em_s, em_r, {"samples": other}),
            )

    mine = partner_ref[s]
    eye = lax.broadcasted_iota(jnp.int32, (tokens, tokens), 0) == lax.broadcasted_iota(
        jnp.int32, (tokens, tokens), 1
    )
    keep = jnp.where(eye & (mask == 0), 1.0, 0.0).astype(BF)

    def rows_in(b, other_of):
        chunks = GROUPS[b]
        got(None, xrecv.at[pl.ds(chunks[0], len(chunks))], xs_r.at[b])
        for c in chunks:
            cols = slice(c * wide, (c + 1) * wide)
            chosen = jnp.where(mine // 4 == s // 4, other_of(c), xrecv[c])
            cot_ref[:, cols] = (dot(keep, g0[:, cols]) + dot(select, chosen, 0, 0)).astype(BF)

    def embed_sum():
        got(None, embs.at[pl.ds(0, 7)], em_r)
        total = embs[0]
        for k in range(1, 8):
            total += embs[k]
        emb_ref[...] = total

    def weights_out():
        got(None, wrecv, wr_r)
        for c in range(NC):
            cols = slice(c * wide, (c + 1) * wide)
            wg_ref[:, cols] = wown[:, cols] + wrecv[c].astype(F32)

    def end_tasks():
        def total_of(c):
            got(None, far_in.at[c, 0], far_r.at[c, 0])
            return pf[c, actual(3)] + far_in[c, 0].astype(F32)

        def part_out(c, n):
            zz = actual(n)
            send(
                None,
                lambda: rdma(
                    pb.at[c, zz], near_in.at[c, n], ps_s, near_r.at[c, n], inner_way
                ),
            )

        weights_seen = set()

        def weights(c):
            if c not in weights_seen:
                weights_seen.add(c)
                weights_in(c)

        def p2(c):
            weights(c)
            first = jnp.where(flip, 0, 2)
            sums = partials(c, first, 2)
            pf[c, pl.ds(first, 2)] = sums
            pb[c, pl.ds(first, 2)] = sums.astype(BF)

        def p01(c):
            weights(c)
            first = jnp.where(flip, 2, 0)
            pb[c, pl.ds(first, 2)] = partials(c, first, 2).astype(BF)

        def back(b):
            backward(b, total_of)
            tile_to(b, s - outward + 1 - 2 * x)
            tile_to(b, s - outward)

        def fin(b):
            got(None, irecv.at[pl.ds(GROUPS[b][0], len(GROUPS[b]))], si_r.at[b])
            rows_in(b, lambda c: irecv[c])

        def wt(c):
            for slot in range(3):
                att_got(c, 2 - slot, slot)
            weight_terms(c)

        return {
            "ga": lambda: gather((2,), 3),
            "gb": lambda: gather((1, 0), None),
            "attE": lambda c: att_to(c, 3, 0, True),
            "s0": lambda c: part_out(c, 0), "s1": lambda c: part_out(c, 1), "s2": lambda c: part_out(c, 2),
            "p2": p2, "p01": p01, "wt": wt,
            "back": back, "emb": embed, "fin": fin, "finw": weights_out, "embw": embed_sum,
        }

    def inner_tasks():
        def total_of(c):
            got(None, near_in.at[c, 2], near_r.at[c, 2])
            got(None, far_in.at[c, 1], far_r.at[c, 1])
            return pf[c, actual(2)] + near_in[c, 2].astype(F32) + far_in[c, 1].astype(F32)

        def part(c):
            weights_in(c)
            pf[c] = partials(c, 0, NZ)

        def far(c, n):
            got(None, near_in.at[c, n], near_r.at[c, n])
            pb[c, n] = (pf[c, actual(n)] + near_in[c, n].astype(F32)).astype(BF)
            send(
                None,
                lambda: rdma(pb.at[c, n], far_in.at[c, n], ps_s, far_r.at[c, n], inner_way),
            )

        def near(c):
            got(None, far_in.at[c, 0], far_r.at[c, 0])
            pb[c, 3] = (pf[c, actual(3)] + far_in[c, 0].astype(F32)).astype(BF)
            send(
                None,
                lambda: rdma(pb.at[c, 3], far_in.at[c, 0], ps_s, far_r.at[c, 0], outer_way),
            )

        def back(b):
            backward(b, total_of)
            tile_to(b, 2 * z + 1 - x)

        def across(b):
            part = pl.ds(GROUPS[b][0], len(GROUPS[b]))
            for k in range(1, 4):
                got(None, swz.at[part, 0], sw_r.at[b, lax.rem(s + k, 4)])
            for k, dest in enumerate((s - 2 * outward, s - outward, s + outward)):
                wanted = lax.rem(partner_ref[dest], 4)
                for c in GROUPS[b]:
                    xsend[k, c] = rows_of(c, wanted)
                into, rs = (irecv, si_r) if k == 2 else (xrecv, xs_r)
                send(
                    None,
                    lambda k=k, dest=dest, into=into, rs=rs: rdma(
                        xsend.at[k, part], into.at[part], xs_s, rs.at[b], {"samples": dest}
                    ),
                )

        def fin(b):
            rows_in(b, lambda c: rows_of(c, lax.rem(mine, 4)))

        def relay(n, slot, to_slot, inward):
            def run(c):
                att_got(c, n, slot)
                att_to(c, n, to_slot, inward)

            return run

        return {
            "gather": lambda: gather((3, 1, 0), 2),
            "attIi": lambda c: att_to(c, 2, 1, True), "attIo": lambda c: att_to(c, 2, 0, False),
            "part": part, "near": near,
            "far0": lambda c: far(c, 0), "far1": lambda c: far(c, 1),
            "r3": relay(3, 0, 2, True),
            "r1": relay(1, 1, 1, False),
            "r0": relay(0, 2, 2, False),
            "wt": weight_terms, "back": back, "across": across, "emb": embed, "fin": fin, "finw": weights_out,
            "embw": embed_sum,
        }

    def run(tasks, order):
        for name, *at in order:
            with T("_".join([name, *map(str, at)])):
                tasks[name](*at)

    @pl.when(is_end)
    def _():
        run(end_tasks(), END_ORDER)
        sent(None, att.at[:, 0], in_at_s)
        sent(None, swz.at[:, pl.ds(0, 2)], sw_s)

    @pl.when(jnp.logical_not(is_end))
    def _():
        run(inner_tasks(), INNER_ORDER)
        sent(None, att.at[:, pl.ds(0, 2)], in_at_s)
        sent(None, att.at[:, pl.ds(0, 3)], out_at_s)
        sent(None, swz.at[:, 0], sw_s)
        sent(None, xsend, xs_s)

    with T("sends_done"):
        sent(None, g_ref, gq_s)
        sent(first_core, gq.at[pl.ds(0, 3)], gf_s)
        sent(None, w2.at[0], w_s)
        sent(None, spall.at[pl.ds(0, 7)], sp_s)
        sent(None, embs.at[pl.ds(0, 7)], em_s)
        sent(None, pb.at[:, pl.ds(0, 3)], ps_s)
        sent(None, wsend, wr_s)


def put_out(wg_ref, cot_ref, emb_ref, wg_out, cot_out, emb_out, done):
    copies = [
        pltpu.make_async_copy(wg_ref, wg_out, done.at[0]),
        pltpu.make_async_copy(cot_ref, cot_out, done.at[1]),
        pltpu.make_async_copy(emb_ref, emb_out, done.at[2]),
    ]
    for copy in copies:
        copy.start()
    for copy in copies:
        copy.wait()


def one_layer(
    stored_inputs, top_cotangent, layer_weights, block_layout, region_mask, partner_samples, spins
):
    tokens, width = stored_inputs.shape[2:]
    rows = layer_weights.shape[1]
    hbm = pl.BlockSpec(memory_space=pltpu.HBM)
    vmem = pl.BlockSpec(memory_space=pltpu.VMEM)
    region = tokens // 2
    dma = pltpu.SemaphoreType.DMA
    half = width // 2
    wide = width // NC
    shapes = [
        ((NZ, tokens, 2 * rows), BF),
        ((2, rows, width), BF),
        ((NC, NZ, tokens, wide), F32),
        ((NC, NZ, tokens, wide), BF),
        ((NC, 3, tokens, wide), BF),
        ((NC, 2, tokens, wide), BF),
        ((NC, NZ, tokens, wide), BF),
        ((width // HEAD, tokens, tokens), F32),
        ((tokens, width), BF),
        ((tokens, width), BF),
        ((NC, 4, region, wide), BF),
        ((3, NC, region, wide), BF),
        ((NC, region, wide), BF),
        ((NC, region, wide), BF),
        ((8, 1, tokens), jnp.int32),
        ((8, SPINS, width), F32),
        ((NC, rows, wide), BF),
        ((NC, rows, wide), BF),
        ((rows, width), F32),
    ]
    one = dma
    sems = [
        dma((7,)), one, dma((NZ,)), one, dma((NZ,)), one, dma((NC,)), one, one, one, one, dma((NC, 3)), one,
        dma((NC, 3)), dma((NC, 2)), one, dma((len(GROUPS), 4)), one, dma((len(GROUPS),)), dma((len(GROUPS),)),
        one, one, one, one, pltpu.SemaphoreType.REGULAR,
    ]
    wg, cot, emb = pl.pallas_call(
        kernel,
        out_shape=[
            jax.ShapeDtypeStruct((rows, width), F32),
            jax.ShapeDtypeStruct((tokens, width), BF),
            jax.ShapeDtypeStruct((SPINS, width), F32),
        ],
        in_specs=[hbm] * 7,
        out_specs=[vmem] * 3,
        scratch_shapes=[
            pltpu.VMEM((tokens, width), BF),
            pltpu.VMEM((tokens, width), BF),
            pltpu.SMEM((2, 2), jnp.int32),
            pltpu.VMEM((1, tokens), jnp.int32),
            pltpu.SMEM((8,), jnp.int32),
            pltpu.VMEM((1, tokens), jnp.int32),
        ]
        + [pltpu.VMEM(a, b) for a, b in shapes]
        + sems,
        compiler_params=pltpu.CompilerParams(
            collective_id=0, has_side_effects=True, vmem_limit_bytes=48 * 1024 * 1024
        ),
    )(
        *[
            pltpu.with_memory_space_constraint(value, pltpu.HBM)
            for value in (
                stored_inputs[0, 0], top_cotangent[0], layer_weights[0], block_layout[0],
                region_mask[None], partner_samples, spins,
            )
        ]
    )
    anywhere = pl.BlockSpec(memory_space=pl.ANY)
    wg, cot, emb = pl.pallas_call(
        put_out,
        out_shape=[jax.ShapeDtypeStruct(a.shape, a.dtype) for a in (wg, cot, emb)],
        in_specs=[vmem] * 3,
        out_specs=[anywhere] * 3,
        scratch_shapes=[dma((3,))],
        compiler_params=pltpu.CompilerParams(vmem_limit_bytes=8 * 1024 * 1024),
    )(wg, cot, emb)
    return wg[None], cot[None, None], emb


def solution(mesh):
    in_specs = (
        P("section", ("groups", "samples"), None, "mp"),
        P(("groups", "samples"), None, "mp"),
        P("section", "samples", "mp"),
        P("section", None, None),
        P(),
        P("groups"),
        P(("groups", "samples"), None),
    )
    out_specs = (
        P(("groups", "section"), "samples", "mp"),
        P("section", ("groups", "samples"), None, "mp"),
        P("groups", "mp"),
    )
    small = mesh.shape["samples"] == 8 and mesh.shape["section"] == 1 and mesh.shape["mp"] == 2
    body = one_layer if small else local
    return jax.shard_map(body, mesh=mesh, in_specs=in_specs, out_specs=out_specs, check_vma=False)
```

```python
import jax
import jax.numpy as jnp
from jax import lax
from jax.experimental import pallas as pl
from jax.experimental.pallas import tpu as pltpu
from jax.sharding import PartitionSpec as P

HEAD = 128
BLOCK = 64
SPINS = 2


def for_sending(value):

    def short(part):
        return part.astype(jnp.bfloat16) if part.dtype == jnp.float32 else part

    return jax.tree.map(short, value)


def passed_along(block, axis, distance):
    devices = range(lax.axis_size(axis))
    route = [(i - distance, i) for i in devices if i - distance in devices]
    return lax.ppermute(block, axis, route)


def softmax_parts(inputs_h, allowed, attention_scale):
    scores = (
        jnp.einsum("qhd,khd->hqk", inputs_h, inputs_h, preferred_element_type=jnp.float32)
        * attention_scale
    )
    scores = jnp.where(allowed[None], scores, -jnp.inf)
    top_score = jnp.max(scores, axis=-1, keepdims=True)
    expo_terms = jnp.exp(scores - top_score)
    probs = expo_terms / jnp.sum(expo_terms, axis=-1, keepdims=True)
    return (probs, probs.astype(jnp.bfloat16))


def local(
    stored_inputs, top_cotangent, layer_weights, block_layout, region_mask, partner_samples, spins
):
    section_index = lax.axis_index("section")
    section_count = lax.axis_size("section")
    micro_count = stored_inputs.shape[1]
    seq_len = stored_inputs.shape[2]
    half_width = stored_inputs.shape[3]
    head_count = half_width // HEAD
    attention_scale = 4.0 / HEAD
    weights = lax.all_gather(layer_weights[0], "samples", axis=0, tiled=True)
    pos_block = jnp.arange(seq_len) // BLOCK
    block_onehot = (pos_block[:, None] == jnp.arange(block_layout.shape[1])[None, :]).astype(
        jnp.float32
    )
    linked = jnp.dot(jnp.dot(block_onehot, block_layout[0].astype(jnp.float32)), block_onehot.T)
    allowed = (linked > 0.5) | (pos_block[:, None] == pos_block[None, :])
    every_layer_input = stored_inputs[0]
    inputs_h = every_layer_input[0].reshape(seq_len, head_count, HEAD)
    probs, probs_low = softmax_parts(inputs_h, allowed, attention_scale)
    attended = jnp.einsum(
        "hqk,khd->qhd", probs_low, inputs_h, preferred_element_type=jnp.float32
    ).astype(jnp.bfloat16)
    probs_list = [probs]
    low_list = [probs_low]
    attend_list = [attended.reshape(seq_len, half_width)]
    probs_all = jnp.stack(probs_list)
    low_all = jnp.stack(low_list)
    attend_store = jnp.stack(attend_list)

    def layer_back(grad_full, grad_own, inputs, probs, probs_low):
        grad_attn = jnp.dot(grad_full, weights, preferred_element_type=jnp.float32).astype(
            jnp.bfloat16
        )
        inputs_h = inputs.reshape(seq_len, head_count, HEAD)
        grad_h = grad_attn.reshape(seq_len, head_count, HEAD)
        grad_probs = jnp.einsum(
            "qhd,khd->hqk", grad_h, inputs_h, preferred_element_type=jnp.float32
        )
        grad_scores = (
            probs * (grad_probs - jnp.sum(grad_probs * probs, axis=-1, keepdims=True))
        ).astype(jnp.bfloat16)
        through = jnp.einsum("hqk,qhd->khd", probs_low, grad_h, preferred_element_type=jnp.float32)
        through = through + attention_scale * (
            jnp.einsum("hqk,khd->qhd", grad_scores, inputs_h, preferred_element_type=jnp.float32)
            + jnp.einsum("hqk,qhd->khd", grad_scores, inputs_h, preferred_element_type=jnp.float32)
        )
        grad_in = grad_own.astype(jnp.float32) + through.reshape(seq_len, half_width)
        return grad_in.astype(jnp.bfloat16)

    def resting(grad_full, grad_own, inputs, probs, probs_low):
        return jnp.zeros((seq_len, half_width), jnp.bfloat16)

    carried_state = jnp.zeros((seq_len, half_width), jnp.bfloat16)
    out_list = []
    grad_list = []
    total_steps = micro_count + section_count - 1
    for step_number in range(total_steps):
        micro_index = step_number - (section_count - 1 - section_index)
        active = (micro_index >= 0) & (micro_index < micro_count)
        slot_index = jnp.clip(micro_index, 0, micro_count - 1)
        from_top = lax.dynamic_index_in_dim(top_cotangent, slot_index, 0, keepdims=False)
        incoming = jnp.where(section_index == section_count - 1, from_top, carried_state)
        grad_full = lax.all_gather(incoming, "mp", axis=1, tiled=True)
        inputs_now = lax.dynamic_index_in_dim(every_layer_input, slot_index, 0, keepdims=False)
        probs_now = lax.dynamic_index_in_dim(probs_all, slot_index, 0, keepdims=False)
        low_now = lax.dynamic_index_in_dim(low_all, slot_index, 0, keepdims=False)
        grad_in = lax.cond(
            active, layer_back, resting, grad_full, incoming, inputs_now, probs_now, low_now
        )
        out_list.append(grad_in)
        grad_list.append(grad_full)
        if step_number < total_steps - 1:
            carried_state = jax.tree.map(
                lambda part, own: part.astype(own.dtype),
                passed_along(for_sending(grad_in), "section", -1),
                grad_in,
            )
    offset = section_count - 1 - section_index
    out_store = lax.dynamic_slice_in_dim(jnp.stack(out_list), offset, micro_count, 0)
    grad_store = lax.dynamic_slice_in_dim(jnp.stack(grad_list), offset, micro_count, 0)
    summed_weight = lax.psum_scatter(
        jnp.einsum(
            "mtf,mta->fa", grad_store, attend_store, preferred_element_type=jnp.float32
        ).astype(jnp.bfloat16),
        "samples",
        scatter_dimension=0,
        tiled=True,
    ).astype(jnp.float32)
    region_count = seq_len // 2
    place_in = jnp.arange(seq_len)
    rank_in_region = (
        jnp.sum(jnp.where(place_in[None, :] <= place_in[:, None], region_mask[None, :], 0), axis=1) - 1
    )
    select = (
        (rank_in_region[None, :] == jnp.arange(region_count)[:, None]) & (region_mask[None, :] > 0)
    ).astype(jnp.bfloat16)
    tiles = jnp.einsum("at,mtd->mad", select, out_store, preferred_element_type=jnp.float32).astype(
        jnp.bfloat16
    )
    shard_index = lax.axis_index("samples")
    my_partners = lax.dynamic_slice_in_dim(
        partner_samples, shard_index * micro_count, micro_count, 0
    )
    shard_count = lax.axis_size("samples")
    dest_shard = my_partners // micro_count
    dest_slot = my_partners % micro_count
    route = (
        (dest_shard[:, None, None] == jnp.arange(shard_count)[None, :, None])
        & (dest_slot[:, None, None] == jnp.arange(micro_count)[None, None, :])
    ).astype(jnp.bfloat16)
    outgoing = jnp.einsum("mku,mad->kuad", route, tiles, preferred_element_type=jnp.float32).astype(
        jnp.bfloat16
    )
    arrived = lax.all_to_all(outgoing, "samples", split_axis=0, concat_axis=0, tiled=True)
    ones_row = jnp.ones((shard_count,), jnp.bfloat16)
    received = jnp.einsum(
        "k,kuad->uad", ones_row, arrived, preferred_element_type=jnp.float32
    ).astype(jnp.bfloat16)
    placed = jnp.einsum("at,mad->mtd", select, received, preferred_element_type=jnp.float32)
    kept = jnp.where(region_mask[None, :, None] > 0, jnp.zeros_like(out_store), out_store)
    site_cot = (kept.astype(jnp.float32) + placed).astype(jnp.bfloat16)
    cotangents = jnp.where(section_index == 0, site_cot, out_store)
    onehot = (spins[:, :, None] == jnp.arange(SPINS)[None, None, :]).astype(jnp.bfloat16)
    embed_term = jnp.einsum("mtv,mtd->vd", onehot, site_cot, preferred_element_type=jnp.float32)
    embed_term = jnp.where(section_index == 0, embed_term, jnp.zeros_like(embed_term))
    embed_grad = lax.psum(embed_term, ("samples", "section"))
    return (summed_weight[None], cotangents[None], embed_grad)


NZ = 4
NC = 4
GROUPS = ((0,), (1,), (2,), (3,))
END_ORDER = (
    ("attE", 0), ("attE", 1), ("ga",), ("attE", 2), ("p2", 1), ("gb",),
    ("attE", 3), ("p01", 0), ("s0", 0), ("p01", 1), ("s1", 1), ("p2", 2),
    ("s0", 1), ("p01", 2), ("p2", 3), ("p01", 3), ("s1", 0), ("s1", 3),
    ("s0", 3), ("s0", 2), ("p2", 0), ("s2", 1), ("s2", 0), ("wt", 0),
    ("s1", 2), ("s2", 3), ("s2", 2), ("back", 0), ("back", 1), ("wt", 2),
    ("back", 3), ("wt", 1), ("back", 2), ("emb",), ("wt", 3), ("fin", 3),
    ("fin", 0), ("fin", 1), ("fin", 2), ("finw",), ("embw",),
)
INNER_ORDER = (
    ("gather",), ("attIi", 2), ("attIo", 0), ("attIo", 1), ("attIi", 1), ("attIi", 0),
    ("r3", 0), ("part", 0), ("attIo", 2), ("r1", 1), ("r3", 1), ("r1", 0),
    ("r1", 2), ("r0", 0), ("r3", 2), ("r3", 3), ("r0", 1), ("part", 2),
    ("far0", 0), ("part", 1), ("wt", 0), ("far0", 1), ("r0", 2), ("part", 3),
    ("wt", 1), ("far1", 1), ("near", 0), ("far1", 0), ("far0", 3), ("near", 1),
    ("wt", 2), ("r0", 3), ("attIo", 3), ("far0", 2), ("near", 3), ("far1", 3),
    ("attIi", 3), ("back", 0), ("back", 1), ("near", 2), ("far1", 2), ("r1", 3),
    ("back", 3), ("across", 0), ("across", 1), ("back", 2), ("emb",), ("wt", 3),
    ("across", 3), ("across", 2), ("fin", 0), ("fin", 1), ("fin", 2), ("fin", 3),
    ("finw",), ("embw",),
)
MESH = pl.DeviceIdType.MESH
F32 = jnp.float32
BF = jnp.bfloat16
T = jax.named_scope


def dot(a, b, ca=1, cb=0):
    return lax.dot_general(a, b, (((ca,), (cb,)), ((), ())), preferred_element_type=F32)


def kernel(
    x_hbm, g_hbm, w_hbm, layout_hbm, mask_hbm, partner_hbm, spin_hbm,
    wg_ref, cot_ref, emb_ref,
    x_ref, g_ref, layout_ref, mask_ref, partner_ref, spin_ref, gq, w2, pf, pb, near_in, far_in, att, probs, ga, g0,
    swz, xsend, xrecv, irecv, spall, embs, wsend, wrecv, wown,
    in_s, gq_s, gq_r, gf_s, gf_r, w_s, w_r, sp_s, sp_r, in_at_s, out_at_s, at_r, ps_s, near_r, far_r,
    sw_s, sw_r, xs_s, xs_r, si_r, em_s, em_r, wr_s, wr_r, last_in,
):
    s = lax.axis_index("samples")
    m = lax.axis_index("mp")
    z = s // 2
    x = s % 2
    flip = z < NZ // 2
    is_end = (z == 0) | (z == NZ - 1)
    outward = jnp.where(flip, -2, 2)
    scale = 4.0 / HEAD
    tokens, width = x_ref.shape
    heads = width // HEAD
    rows = w_hbm.shape[0]
    half = width // 2
    wide = width // NC
    per = wide // HEAD
    sibling = {"mp": 1 - m}
    beside = {"samples": 2 * z + 1 - x}
    inner_way = {"samples": lax.rem(s - outward + 8, 8)}
    outer_way = {"samples": lax.rem(s + outward + 8, 8)}

    def actual(n):
        return jnp.where(flip, NZ - 1 - n, n)

    def rdma(src, dst, ss, rs, dev):
        return pltpu.make_async_remote_copy(
            src_ref=src, dst_ref=dst, send_sem=ss, recv_sem=rs, device_id=dev, device_id_type=MESH
        )

    def send(cond, make):
        if cond is None:
            make().start()
        else:
            pl.when(cond)(lambda: make().start())

    def sent(cond, src, ss):
        def wait():
            rdma(src, src, ss, ss, sibling).wait_send()

        if cond is None:
            wait()
        else:
            pl.when(cond)(wait)

    def got(cond, dst, rs):
        def wait():
            rdma(dst, dst, rs, rs, sibling).wait_recv()

        if cond is None:
            wait()
        else:
            pl.when(cond)(wait)

    loads = [
        pltpu.make_async_copy(g_hbm, g_ref, in_s.at[0]),
        pltpu.make_async_copy(w_hbm, w2.at[x], in_s.at[1]),
        pltpu.make_async_copy(x_hbm, x_ref, in_s.at[2]),
        pltpu.make_async_copy(spin_hbm, spin_ref, in_s.at[3]),
        pltpu.make_async_copy(layout_hbm, layout_ref, in_s.at[4]),
        pltpu.make_async_copy(mask_hbm, mask_ref, in_s.at[5]),
        pltpu.make_async_copy(partner_hbm, partner_ref, in_s.at[6]),
    ]
    for load in loads:
        load.start()
    barrier = pltpu.get_barrier_semaphore()
    is_last = z == NZ - 1
    for k in range(1, 8):
        other = lax.rem(s + k, 8)

        @pl.when(jnp.logical_not(is_last) | (other // 2 == NZ - 1))
        def _(other=other):
            pl.semaphore_signal(
                barrier, inc=1, device_id={"samples": other}, device_id_type=MESH
            )

    pl.semaphore_signal(barrier, inc=1, device_id=sibling, device_id_type=MESH)
    for load in loads:
        load.wait()

    qb = lax.broadcasted_iota(jnp.int32, (tokens, tokens), 0) // BLOCK
    kb = lax.broadcasted_iota(jnp.int32, (tokens, tokens), 1) // BLOCK
    linked = jnp.where(qb < kb, layout_ref[0, 1], layout_ref[1, 0])
    allowed = (qb == kb) | (linked > 0)

    def attention():
        for h in range(heads):
            xh = x_ref[:, pl.ds(h * HEAD, HEAD)]
            scores = jnp.where(allowed, dot(xh, xh, 1, 1) * scale, -jnp.inf)
            expo = jnp.exp(scores - jnp.max(scores, axis=-1, keepdims=True))
            p = expo / jnp.sum(expo, axis=-1, keepdims=True)
            probs[h] = p
            att[h // per, z, :, pl.ds(h % per * HEAD, HEAD)] = dot(p.astype(BF), xh).astype(BF)

    @pl.when(flip)
    def _():
        with T("attn"):
            attention()

    with T("barrier"):
        pl.semaphore_wait(barrier, jnp.where(is_last, 8, 6))

    @pl.when(is_last)
    def _():
        for k in range(1, NZ):
            pl.semaphore_signal(
                last_in, inc=1, device_id={"samples": s - 2 * k}, device_id_type=MESH
            )

    def piece_out(far, cond):
        jj = m if far else 1 - m
        dz = 2 * m + jj
        columns = pl.ds(pl.multiple_of(jj * half, half), half)
        piece = g_ref.at[:, columns]
        send(
            cond & (dz != z),
            lambda: rdma(piece, gq.at[z], gq_s, gq_r.at[z], {"samples": 2 * dz + x}),
        )
        send(cond & (dz == z), lambda: rdma(piece, gq.at[z], gq_s, gf_r.at[z], sibling))

        @pl.when(cond & (dz == z))
        def _():
            gq[z] = g_ref[:, columns]

    to_last = (m == 1) & jnp.logical_not(is_last)
    piece_out(False, m < 2)
    piece_out(True, jnp.logical_not(to_last))
    for c in range(NC):
        block = w2.at[x, :, pl.ds(c * wide, wide)]
        send(None, lambda block=block, c=c: rdma(block, block, w_s, w_r.at[c], beside))
    spall[s] = spin_ref[...]

    @pl.when(jnp.logical_not(flip))
    def _():
        with T("attn"):
            attention()

    @pl.when(jnp.logical_not(is_last))
    def _():
        with T("last"):
            pl.semaphore_wait(last_in, 1)

    piece_out(True, to_last)
    for k in range(1, 8):
        other = lax.rem(s + k, 8)
        send(
            None,
            lambda other=other: rdma(spin_ref, spall.at[s], sp_s, sp_r, {"samples": other}),
        )

    mask = mask_ref[...]
    tri = (
        lax.broadcasted_iota(jnp.int32, (tokens, tokens), 0)
        <= lax.broadcasted_iota(jnp.int32, (tokens, tokens), 1)
    ).astype(F32).astype(BF)
    mask_rows = jnp.broadcast_to(mask, (8, tokens)).astype(F32)
    rank = dot(mask_rows.astype(BF), tri)[:1] - 1.0
    region = tokens // 2
    place = lax.broadcasted_iota(jnp.int32, (region, tokens), 0).astype(F32)
    select = jnp.where((rank == place) & (mask > 0), 1.0, 0.0).astype(BF)

    first_core = m == z // 2

    def gather(order, own):
        for n in order:
            zz = actual(n)
            got(first_core, gq.at[zz], gq_r.at[zz])
            send(
                first_core,
                lambda zz=zz: rdma(gq.at[zz], gq.at[zz], gf_s, gf_r.at[zz], sibling),
            )
        for n in (own, *order) if own else order:
            zz = actual(n)
            got(jnp.logical_not(first_core), gq.at[zz], gf_r.at[zz])

    def att_to(c, n, slot, inward):
        zz = actual(n)
        way, ss = (inner_way, in_at_s) if inward else (outer_way, out_at_s)
        send(None, lambda: rdma(att.at[c, zz], att.at[c, zz], ss, at_r.at[c, slot], way))

    def att_got(c, n, slot):
        got(None, att.at[c, actual(n)], at_r.at[c, slot])

    def weights_in(c):
        got(None, w2.at[1 - x, :, pl.ds(c * wide, wide)], w_r.at[c])

    def partials(c, first, count):
        cols = pl.ds(c * wide, wide)
        some = gq[pl.ds(first, count)].reshape(count * tokens, 2 * rows)
        sums = dot(some[:, :rows], w2[0, :, cols]) + dot(some[:, rows:], w2[1, :, cols])
        return sums.reshape(count, tokens, wide)

    def weight_terms(c):
        total = jnp.zeros((2 * rows, wide), F32)
        for zz in range(NZ):
            total += dot(gq[zz], att[c, zz], 0, 0).astype(BF).astype(F32)
        cols = pl.ds(c * wide, wide)

        @pl.when(x == 0)
        def _():
            wown[:, cols] = total[:rows]
            wsend[c] = total[rows:].astype(BF)

        @pl.when(x == 1)
        def _():
            wown[:, cols] = total[rows:]
            wsend[c] = total[:rows].astype(BF)

        send(None, lambda: rdma(wsend.at[c], wrecv.at[c], wr_s, wr_r, beside))

    def backward(b, total_of):
        chunks = GROUPS[b]
        for c in chunks:
            ga[:, c * wide : (c + 1) * wide] = total_of(c).astype(BF)
        for h in range(chunks[0] * per, (chunks[-1] + 1) * per):
            cols = slice(h * HEAD, (h + 1) * HEAD)
            xh = x_ref[:, cols]
            gh = ga[:, cols]
            p = probs[h]
            gp = dot(gh, xh, 1, 1)
            gs = (p * (gp - jnp.sum(gp * p, axis=-1, keepdims=True))).astype(BF)
            through = dot(p.astype(BF), gh, 0, 0) + scale * (dot(gs, xh) + dot(gs, xh, 0, 0))
            g0[:, cols] = (g_ref[:, cols].astype(F32) + through).astype(BF)
        for c in chunks:
            swz[c, s % 4] = dot(select, g0[:, c * wide : (c + 1) * wide]).astype(BF)

    def tile_to(b, other):
        rows_now = swz.at[pl.ds(GROUPS[b][0], len(GROUPS[b])), s % 4]
        send(
            None,
            lambda: rdma(rows_now, rows_now, sw_s, sw_r.at[b, s % 4], {"samples": other}),
        )

    def rows_of(c, which):
        rows_now = swz[c, 0]
        for k in range(1, 4):
            rows_now = jnp.where(which == k, swz[c, k], rows_now)
        return rows_now

    def embed():
        got(None, spall.at[pl.ds(0, 7)], sp_r)
        spins = jnp.where(mask > 0, spall[partner_ref[s]], spin_ref[...])
        onehot = jnp.where(
            spins == lax.broadcasted_iota(jnp.int32, (8, tokens), 0), 1.0, 0.0
        ).astype(BF)
        embs[s] = dot(onehot, g0[...])[:SPINS]
        for k in range(1, 8):
            other = lax.rem(s + k, 8)
            send(
                None,
                lambda other=other: rdma(embs.at[s], embs.at[s], em_s, em_r, {"samples": other}),
            )

    mine = partner_ref[s]
    eye = lax.broadcasted_iota(jnp.int32, (tokens, tokens), 0) == lax.broadcasted_iota(
        jnp.int32, (tokens, tokens), 1
    )
    keep = jnp.where(eye & (mask == 0), 1.0, 0.0).astype(BF)

    def rows_in(b, other_of):
        chunks = GROUPS[b]
        got(None, xrecv.at[pl.ds(chunks[0], len(chunks))], xs_r.at[b])
        for c in chunks:
            cols = slice(c * wide, (c + 1) * wide)
            chosen = jnp.where(mine // 4 == s // 4, other_of(c), xrecv[c])
            cot_ref[:, cols] = (dot(keep, g0[:, cols]) + dot(select, chosen, 0, 0)).astype(BF)

    def embed_sum():
        got(None, embs.at[pl.ds(0, 7)], em_r)
        total = embs[0]
        for k in range(1, 8):
            total += embs[k]
        emb_ref[...] = total

    def weights_out():
        got(None, wrecv, wr_r)
        for c in range(NC):
            cols = slice(c * wide, (c + 1) * wide)
            wg_ref[:, cols] = wown[:, cols] + wrecv[c].astype(F32)

    def end_tasks():
        def total_of(c):
            got(None, far_in.at[c, 0], far_r.at[c, 0])
            return pf[c, actual(3)] + far_in[c, 0].astype(F32)

        def part_out(c, n):
            zz = actual(n)
            send(
                None,
                lambda: rdma(
                    pb.at[c, zz], near_in.at[c, n], ps_s, near_r.at[c, n], inner_way
                ),
            )

        weights_seen = set()

        def weights(c):
            if c not in weights_seen:
                weights_seen.add(c)
                weights_in(c)

        def p2(c):
            weights(c)
            first = jnp.where(flip, 0, 2)
            sums = partials(c, first, 2)
            pf[c, pl.ds(first, 2)] = sums
            pb[c, pl.ds(first, 2)] = sums.astype(BF)

        def p01(c):
            weights(c)
            first = jnp.where(flip, 2, 0)
            pb[c, pl.ds(first, 2)] = partials(c, first, 2).astype(BF)

        def back(b):
            backward(b, total_of)
            tile_to(b, s - outward + 1 - 2 * x)
            tile_to(b, s - outward)

        def fin(b):
            got(None, irecv.at[pl.ds(GROUPS[b][0], len(GROUPS[b]))], si_r.at[b])
            rows_in(b, lambda c: irecv[c])

        def wt(c):
            for slot in range(3):
                att_got(c, 2 - slot, slot)
            weight_terms(c)

        return {
            "ga": lambda: gather((2,), 3),
            "gb": lambda: gather((1, 0), None),
            "attE": lambda c: att_to(c, 3, 0, True),
            "s0": lambda c: part_out(c, 0), "s1": lambda c: part_out(c, 1), "s2": lambda c: part_out(c, 2),
            "p2": p2, "p01": p01, "wt": wt,
            "back": back, "emb": embed, "fin": fin, "finw": weights_out, "embw": embed_sum,
        }

    def inner_tasks():
        def total_of(c):
            got(None, near_in.at[c, 2], near_r.at[c, 2])
            got(None, far_in.at[c, 1], far_r.at[c, 1])
            return pf[c, actual(2)] + near_in[c, 2].astype(F32) + far_in[c, 1].astype(F32)

        def part(c):
            weights_in(c)
            pf[c] = partials(c, 0, NZ)

        def far(c, n):
            got(None, near_in.at[c, n], near_r.at[c, n])
            pb[c, n] = (pf[c, actual(n)] + near_in[c, n].astype(F32)).astype(BF)
            send(
                None,
                lambda: rdma(pb.at[c, n], far_in.at[c, n], ps_s, far_r.at[c, n], inner_way),
            )

        def near(c):
            got(None, far_in.at[c, 0], far_r.at[c, 0])
            pb[c, 3] = (pf[c, actual(3)] + far_in[c, 0].astype(F32)).astype(BF)
            send(
                None,
                lambda: rdma(pb.at[c, 3], far_in.at[c, 0], ps_s, far_r.at[c, 0], outer_way),
            )

        def back(b):
            backward(b, total_of)
            tile_to(b, 2 * z + 1 - x)

        def across(b):
            part = pl.ds(GROUPS[b][0], len(GROUPS[b]))
            for k in range(1, 4):
                got(None, swz.at[part, 0], sw_r.at[b, lax.rem(s + k, 4)])
            for k, dest in enumerate((s - 2 * outward, s - outward, s + outward)):
                wanted = lax.rem(partner_ref[dest], 4)
                for c in GROUPS[b]:
                    xsend[k, c] = rows_of(c, wanted)
                into, rs = (irecv, si_r) if k == 2 else (xrecv, xs_r)
                send(
                    None,
                    lambda k=k, dest=dest, into=into, rs=rs: rdma(
                        xsend.at[k, part], into.at[part], xs_s, rs.at[b], {"samples": dest}
                    ),
                )

        def fin(b):
            rows_in(b, lambda c: rows_of(c, lax.rem(mine, 4)))

        def relay(n, slot, to_slot, inward):
            def run(c):
                att_got(c, n, slot)
                att_to(c, n, to_slot, inward)

            return run

        return {
            "gather": lambda: gather((3, 1, 0), 2),
            "attIi": lambda c: att_to(c, 2, 1, True), "attIo": lambda c: att_to(c, 2, 0, False),
            "part": part, "near": near,
            "far0": lambda c: far(c, 0), "far1": lambda c: far(c, 1),
            "r3": relay(3, 0, 2, True),
            "r1": relay(1, 1, 1, False),
            "r0": relay(0, 2, 2, False),
            "wt": weight_terms, "back": back, "across": across, "emb": embed, "fin": fin, "finw": weights_out,
            "embw": embed_sum,
        }

    def run(tasks, order):
        for name, *at in order:
            with T("_".join([name, *map(str, at)])):
                tasks[name](*at)

    @pl.when(is_end)
    def _():
        run(end_tasks(), END_ORDER)
        sent(None, att.at[:, 0], in_at_s)
        sent(None, swz.at[:, pl.ds(0, 2)], sw_s)

    @pl.when(jnp.logical_not(is_end))
    def _():
        run(inner_tasks(), INNER_ORDER)
        sent(None, att.at[:, pl.ds(0, 2)], in_at_s)
        sent(None, att.at[:, pl.ds(0, 3)], out_at_s)
        sent(None, swz.at[:, 0], sw_s)
        sent(None, xsend, xs_s)

    with T("sends_done"):
        sent(None, g_ref, gq_s)
        sent(first_core, gq.at[pl.ds(0, 3)], gf_s)
        sent(None, w2.at[0], w_s)
        sent(None, spall.at[pl.ds(0, 7)], sp_s)
        sent(None, embs.at[pl.ds(0, 7)], em_s)
        sent(None, pb.at[:, pl.ds(0, 3)], ps_s)
        sent(None, wsend, wr_s)


def put_out(wg_ref, cot_ref, emb_ref, wg_out, cot_out, emb_out, done):
    copies = [
        pltpu.make_async_copy(wg_ref, wg_out, done.at[0]),
        pltpu.make_async_copy(cot_ref, cot_out, done.at[1]),
        pltpu.make_async_copy(emb_ref, emb_out, done.at[2]),
    ]
    for copy in copies:
        copy.start()
    for copy in copies:
        copy.wait()


def one_layer(
    stored_inputs, top_cotangent, layer_weights, block_layout, region_mask, partner_samples, spins
):
    tokens, width = stored_inputs.shape[2:]
    rows = layer_weights.shape[1]
    hbm = pl.BlockSpec(memory_space=pltpu.HBM)
    vmem = pl.BlockSpec(memory_space=pltpu.VMEM)
    region = tokens // 2
    dma = pltpu.SemaphoreType.DMA
    half = width // 2
    wide = width // NC
    shapes = [
        ((NZ, tokens, 2 * rows), BF),
        ((2, rows, width), BF),
        ((NC, NZ, tokens, wide), F32),
        ((NC, NZ, tokens, wide), BF),
        ((NC, 3, tokens, wide), BF),
        ((NC, 2, tokens, wide), BF),
        ((NC, NZ, tokens, wide), BF),
        ((width // HEAD, tokens, tokens), F32),
        ((tokens, width), BF),
        ((tokens, width), BF),
        ((NC, 4, region, wide), BF),
        ((3, NC, region, wide), BF),
        ((NC, region, wide), BF),
        ((NC, region, wide), BF),
        ((8, 1, tokens), jnp.int32),
        ((8, SPINS, width), F32),
        ((NC, rows, wide), BF),
        ((NC, rows, wide), BF),
        ((rows, width), F32),
    ]
    one = dma
    sems = [
        dma((7,)), one, dma((NZ,)), one, dma((NZ,)), one, dma((NC,)), one, one, one, one, dma((NC, 3)), one,
        dma((NC, 3)), dma((NC, 2)), one, dma((len(GROUPS), 4)), one, dma((len(GROUPS),)), dma((len(GROUPS),)),
        one, one, one, one, pltpu.SemaphoreType.REGULAR,
    ]
    wg, cot, emb = pl.pallas_call(
        kernel,
        out_shape=[
            jax.ShapeDtypeStruct((rows, width), F32),
            jax.ShapeDtypeStruct((tokens, width), BF),
            jax.ShapeDtypeStruct((SPINS, width), F32),
        ],
        in_specs=[hbm] * 7,
        out_specs=[vmem] * 3,
        scratch_shapes=[
            pltpu.VMEM((tokens, width), BF),
            pltpu.VMEM((tokens, width), BF),
            pltpu.SMEM((2, 2), jnp.int32),
            pltpu.VMEM((1, tokens), jnp.int32),
            pltpu.SMEM((8,), jnp.int32),
            pltpu.VMEM((1, tokens), jnp.int32),
        ]
        + [pltpu.VMEM(a, b) for a, b in shapes]
        + sems,
        compiler_params=pltpu.CompilerParams(
            collective_id=0, has_side_effects=True, vmem_limit_bytes=48 * 1024 * 1024
        ),
    )(
        *[
            pltpu.with_memory_space_constraint(value, pltpu.HBM)
            for value in (
                stored_inputs[0, 0], top_cotangent[0], layer_weights[0], block_layout[0],
                region_mask[None], partner_samples, spins,
            )
        ]
    )
    anywhere = pl.BlockSpec(memory_space=pl.ANY)
    wg, cot, emb = pl.pallas_call(
        put_out,
        out_shape=[jax.ShapeDtypeStruct(a.shape, a.dtype) for a in (wg, cot, emb)],
        in_specs=[vmem] * 3,
        out_specs=[anywhere] * 3,
        scratch_shapes=[dma((3,))],
        compiler_params=pltpu.CompilerParams(vmem_limit_bytes=8 * 1024 * 1024),
    )(wg, cot, emb)
    return wg[None], cot[None, None], emb


def solution(mesh):
    in_specs = (
        P("section", ("groups", "samples"), None, "mp"),
        P(("groups", "samples"), None, "mp"),
        P("section", "samples", "mp"),
        P("section", None, None),
        P(),
        P("groups"),
        P(("groups", "samples"), None),
    )
    out_specs = (
        P(("groups", "section"), "samples", "mp"),
        P("section", ("groups", "samples"), None, "mp"),
        P("groups", "mp"),
    )
    small = mesh.shape["samples"] == 8 and mesh.shape["section"] == 1 and mesh.shape["mp"] == 2
    body = one_layer if small else local
    return jax.shard_map(body, mesh=mesh, in_specs=in_specs, out_specs=out_specs, check_vma=False)
```

```python
import jax
import jax.numpy as jnp
from jax import lax
from jax.experimental import pallas as pl
from jax.experimental.pallas import tpu as pltpu
from jax.sharding import PartitionSpec as P

HEAD = 128
BLOCK = 64
SPINS = 2


def for_sending(value):

    def short(part):
        return part.astype(jnp.bfloat16) if part.dtype == jnp.float32 else part

    return jax.tree.map(short, value)


def passed_along(block, axis, distance):
    devices = range(lax.axis_size(axis))
    route = [(i - distance, i) for i in devices if i - distance in devices]
    return lax.ppermute(block, axis, route)


def softmax_parts(inputs_h, allowed, attention_scale):
    scores = (
        jnp.einsum("qhd,khd->hqk", inputs_h, inputs_h, preferred_element_type=jnp.float32)
        * attention_scale
    )
    scores = jnp.where(allowed[None], scores, -jnp.inf)
    top_score = jnp.max(scores, axis=-1, keepdims=True)
    expo_terms = jnp.exp(scores - top_score)
    probs = expo_terms / jnp.sum(expo_terms, axis=-1, keepdims=True)
    return (probs, probs.astype(jnp.bfloat16))


def local(
    stored_inputs, top_cotangent, layer_weights, block_layout, region_mask, partner_samples, spins
):
    section_index = lax.axis_index("section")
    section_count = lax.axis_size("section")
    micro_count = stored_inputs.shape[1]
    seq_len = stored_inputs.shape[2]
    half_width = stored_inputs.shape[3]
    head_count = half_width // HEAD
    attention_scale = 4.0 / HEAD
    weights = lax.all_gather(layer_weights[0], "samples", axis=0, tiled=True)
    pos_block = jnp.arange(seq_len) // BLOCK
    block_onehot = (pos_block[:, None] == jnp.arange(block_layout.shape[1])[None, :]).astype(
        jnp.float32
    )
    linked = jnp.dot(jnp.dot(block_onehot, block_layout[0].astype(jnp.float32)), block_onehot.T)
    allowed = (linked > 0.5) | (pos_block[:, None] == pos_block[None, :])
    every_layer_input = stored_inputs[0]
    inputs_h = every_layer_input[0].reshape(seq_len, head_count, HEAD)
    probs, probs_low = softmax_parts(inputs_h, allowed, attention_scale)
    attended = jnp.einsum(
        "hqk,khd->qhd", probs_low, inputs_h, preferred_element_type=jnp.float32
    ).astype(jnp.bfloat16)
    probs_list = [probs]
    low_list = [probs_low]
    attend_list = [attended.reshape(seq_len, half_width)]
    probs_all = jnp.stack(probs_list)
    low_all = jnp.stack(low_list)
    attend_store = jnp.stack(attend_list)

    def layer_back(grad_full, grad_own, inputs, probs, probs_low):
        grad_attn = jnp.dot(grad_full, weights, preferred_element_type=jnp.float32).astype(
            jnp.bfloat16
        )
        inputs_h = inputs.reshape(seq_len, head_count, HEAD)
        grad_h = grad_attn.reshape(seq_len, head_count, HEAD)
        grad_probs = jnp.einsum(
            "qhd,khd->hqk", grad_h, inputs_h, preferred_element_type=jnp.float32
        )
        grad_scores = (
            probs * (grad_probs - jnp.sum(grad_probs * probs, axis=-1, keepdims=True))
        ).astype(jnp.bfloat16)
        through = jnp.einsum("hqk,qhd->khd", probs_low, grad_h, preferred_element_type=jnp.float32)
        through = through + attention_scale * (
            jnp.einsum("hqk,khd->qhd", grad_scores, inputs_h, preferred_element_type=jnp.float32)
            + jnp.einsum("hqk,qhd->khd", grad_scores, inputs_h, preferred_element_type=jnp.float32)
        )
        grad_in = grad_own.astype(jnp.float32) + through.reshape(seq_len, half_width)
        return grad_in.astype(jnp.bfloat16)

    def resting(grad_full, grad_own, inputs, probs, probs_low):
        return jnp.zeros((seq_len, half_width), jnp.bfloat16)

    carried_state = jnp.zeros((seq_len, half_width), jnp.bfloat16)
    out_list = []
    grad_list = []
    total_steps = micro_count + section_count - 1
    for step_number in range(total_steps):
        micro_index = step_number - (section_count - 1 - section_index)
        active = (micro_index >= 0) & (micro_index < micro_count)
        slot_index = jnp.clip(micro_index, 0, micro_count - 1)
        from_top = lax.dynamic_index_in_dim(top_cotangent, slot_index, 0, keepdims=False)
        incoming = jnp.where(section_index == section_count - 1, from_top, carried_state)
        grad_full = lax.all_gather(incoming, "mp", axis=1, tiled=True)
        inputs_now = lax.dynamic_index_in_dim(every_layer_input, slot_index, 0, keepdims=False)
        probs_now = lax.dynamic_index_in_dim(probs_all, slot_index, 0, keepdims=False)
        low_now = lax.dynamic_index_in_dim(low_all, slot_index, 0, keepdims=False)
        grad_in = lax.cond(
            active, layer_back, resting, grad_full, incoming, inputs_now, probs_now, low_now
        )
        out_list.append(grad_in)
        grad_list.append(grad_full)
        if step_number < total_steps - 1:
            carried_state = jax.tree.map(
                lambda part, own: part.astype(own.dtype),
                passed_along(for_sending(grad_in), "section", -1),
                grad_in,
            )
    offset = section_count - 1 - section_index
    out_store = lax.dynamic_slice_in_dim(jnp.stack(out_list), offset, micro_count, 0)
    grad_store = lax.dynamic_slice_in_dim(jnp.stack(grad_list), offset, micro_count, 0)
    summed_weight = lax.psum_scatter(
        jnp.einsum(
            "mtf,mta->fa", grad_store, attend_store, preferred_element_type=jnp.float32
        ).astype(jnp.bfloat16),
        "samples",
        scatter_dimension=0,
        tiled=True,
    ).astype(jnp.float32)
    region_count = seq_len // 2
    place_in = jnp.arange(seq_len)
    rank_in_region = (
        jnp.sum(jnp.where(place_in[None, :] <= place_in[:, None], region_mask[None, :], 0), axis=1) - 1
    )
    select = (
        (rank_in_region[None, :] == jnp.arange(region_count)[:, None]) & (region_mask[None, :] > 0)
    ).astype(jnp.bfloat16)
    tiles = jnp.einsum("at,mtd->mad", select, out_store, preferred_element_type=jnp.float32).astype(
        jnp.bfloat16
    )
    shard_index = lax.axis_index("samples")
    my_partners = lax.dynamic_slice_in_dim(
        partner_samples, shard_index * micro_count, micro_count, 0
    )
    shard_count = lax.axis_size("samples")
    dest_shard = my_partners // micro_count
    dest_slot = my_partners % micro_count
    route = (
        (dest_shard[:, None, None] == jnp.arange(shard_count)[None, :, None])
        & (dest_slot[:, None, None] == jnp.arange(micro_count)[None, None, :])
    ).astype(jnp.bfloat16)
    outgoing = jnp.einsum("mku,mad->kuad", route, tiles, preferred_element_type=jnp.float32).astype(
        jnp.bfloat16
    )
    arrived = lax.all_to_all(outgoing, "samples", split_axis=0, concat_axis=0, tiled=True)
    ones_row = jnp.ones((shard_count,), jnp.bfloat16)
    received = jnp.einsum(
        "k,kuad->uad", ones_row, arrived, preferred_element_type=jnp.float32
    ).astype(jnp.bfloat16)
    placed = jnp.einsum("at,mad->mtd", select, received, preferred_element_type=jnp.float32)
    kept = jnp.where(region_mask[None, :, None] > 0, jnp.zeros_like(out_store), out_store)
    site_cot = (kept.astype(jnp.float32) + placed).astype(jnp.bfloat16)
    cotangents = jnp.where(section_index == 0, site_cot, out_store)
    onehot = (spins[:, :, None] == jnp.arange(SPINS)[None, None, :]).astype(jnp.bfloat16)
    embed_term = jnp.einsum("mtv,mtd->vd", onehot, site_cot, preferred_element_type=jnp.float32)
    embed_term = jnp.where(section_index == 0, embed_term, jnp.zeros_like(embed_term))
    embed_grad = lax.psum(embed_term, ("samples", "section"))
    return (summed_weight[None], cotangents[None], embed_grad)


NZ = 4
NC = 4
GROUPS = ((0,), (1,), (2,), (3,))
END_ORDER = (
    ("attE", 0), ("attE", 1), ("ga",), ("attE", 2), ("p2", 1), ("gb",),
    ("attE", 3), ("p01", 0), ("s0", 0), ("p01", 1), ("s1", 1), ("p2", 2),
    ("s0", 1), ("p01", 2), ("p2", 3), ("p01", 3), ("s1", 0), ("s1", 3),
    ("s0", 3), ("s0", 2), ("p2", 0), ("s2", 1), ("s2", 0), ("s1", 2),
    ("s2", 3), ("s2", 2), ("wt", 0), ("back", 0), ("back", 1), ("wt", 2),
    ("back", 3), ("wt", 1), ("back", 2), ("emb",), ("wt", 3), ("fin", 3),
    ("fin", 0), ("fin", 1), ("fin", 2), ("finw",), ("embw",),
)
INNER_ORDER = (
    ("gather",), ("attIi", 2), ("attIo", 0), ("attIo", 1), ("attIi", 1), ("attIi", 0),
    ("r3", 0), ("part", 0), ("attIo", 2), ("r1", 1), ("r3", 1), ("r1", 0),
    ("r1", 2), ("r0", 0), ("r3", 2), ("r3", 3), ("r0", 1), ("part", 2),
    ("far0", 0), ("part", 1), ("wt", 0), ("far0", 1), ("r0", 2), ("part", 3),
    ("wt", 1), ("far1", 1), ("near", 0), ("far1", 0), ("far0", 3), ("near", 1),
    ("wt", 2), ("r0", 3), ("attIo", 3), ("far0", 2), ("near", 3), ("far1", 3),
    ("attIi", 3), ("back", 0), ("back", 1), ("near", 2), ("far1", 2), ("r1", 3),
    ("back", 3), ("across", 0), ("across", 1), ("back", 2), ("emb",), ("wt", 3),
    ("across", 3), ("across", 2), ("fin", 0), ("fin", 1), ("fin", 2), ("fin", 3),
    ("finw",), ("embw",),
)
MESH = pl.DeviceIdType.MESH
F32 = jnp.float32
BF = jnp.bfloat16
T = jax.named_scope


def dot(a, b, ca=1, cb=0):
    return lax.dot_general(a, b, (((ca,), (cb,)), ((), ())), preferred_element_type=F32)


def kernel(
    x_hbm, g_hbm, w_hbm, layout_hbm, mask_hbm, partner_hbm, spin_hbm,
    wg_ref, cot_ref, emb_ref,
    x_ref, g_ref, layout_ref, mask_ref, partner_ref, spin_ref, gq, w2, pf, pb, near_in, far_in, att, probs, ga, g0,
    swz, xsend, xrecv, irecv, spall, embs, wsend, wrecv, wown,
    in_s, gq_s, gq_r, gf_s, gf_r, w_s, w_r, sp_s, sp_r, in_at_s, out_at_s, at_r, ps_s, near_r, far_r,
    sw_s, sw_r, xs_s, xs_r, si_r, em_s, em_r, wr_s, wr_r, last_in,
):
    s = lax.axis_index("samples")
    m = lax.axis_index("mp")
    z = s // 2
    x = s % 2
    flip = z < NZ // 2
    is_end = (z == 0) | (z == NZ - 1)
    outward = jnp.where(flip, -2, 2)
    scale = 4.0 / HEAD
    tokens, width = x_ref.shape
    heads = width // HEAD
    rows = w_hbm.shape[0]
    half = width // 2
    wide = width // NC
    per = wide // HEAD
    sibling = {"mp": 1 - m}
    beside = {"samples": 2 * z + 1 - x}
    inner_way = {"samples": lax.rem(s - outward + 8, 8)}
    outer_way = {"samples": lax.rem(s + outward + 8, 8)}

    def actual(n):
        return jnp.where(flip, NZ - 1 - n, n)

    def rdma(src, dst, ss, rs, dev):
        return pltpu.make_async_remote_copy(
            src_ref=src, dst_ref=dst, send_sem=ss, recv_sem=rs, device_id=dev, device_id_type=MESH
        )

    def send(cond, make):
        if cond is None:
            make().start()
        else:
            pl.when(cond)(lambda: make().start())

    def sent(cond, src, ss):
        def wait():
            rdma(src, src, ss, ss, sibling).wait_send()

        if cond is None:
            wait()
        else:
            pl.when(cond)(wait)

    def got(cond, dst, rs):
        def wait():
            rdma(dst, dst, rs, rs, sibling).wait_recv()

        if cond is None:
            wait()
        else:
            pl.when(cond)(wait)

    loads = [
        pltpu.make_async_copy(g_hbm, g_ref, in_s.at[0]),
        pltpu.make_async_copy(w_hbm, w2.at[x], in_s.at[1]),
        pltpu.make_async_copy(x_hbm, x_ref, in_s.at[2]),
        pltpu.make_async_copy(spin_hbm, spin_ref, in_s.at[3]),
        pltpu.make_async_copy(layout_hbm, layout_ref, in_s.at[4]),
        pltpu.make_async_copy(mask_hbm, mask_ref, in_s.at[5]),
        pltpu.make_async_copy(partner_hbm, partner_ref, in_s.at[6]),
    ]
    for load in loads:
        load.start()
    barrier = pltpu.get_barrier_semaphore()
    is_last = z == NZ - 1
    for k in range(1, 8):
        other = lax.rem(s + k, 8)

        @pl.when(jnp.logical_not(is_last) | (other // 2 == NZ - 1))
        def _(other=other):
            pl.semaphore_signal(
                barrier, inc=1, device_id={"samples": other}, device_id_type=MESH
            )

    pl.semaphore_signal(barrier, inc=1, device_id=sibling, device_id_type=MESH)
    for load in loads:
        load.wait()

    qb = lax.broadcasted_iota(jnp.int32, (tokens, tokens), 0) // BLOCK
    kb = lax.broadcasted_iota(jnp.int32, (tokens, tokens), 1) // BLOCK
    linked = jnp.where(qb < kb, layout_ref[0, 1], layout_ref[1, 0])
    allowed = (qb == kb) | (linked > 0)

    def attention():
        for h in range(heads):
            xh = x_ref[:, pl.ds(h * HEAD, HEAD)]
            scores = jnp.where(allowed, dot(xh, xh, 1, 1) * scale, -jnp.inf)
            expo = jnp.exp(scores - jnp.max(scores, axis=-1, keepdims=True))
            p = expo / jnp.sum(expo, axis=-1, keepdims=True)
            probs[h] = p
            att[h // per, z, :, pl.ds(h % per * HEAD, HEAD)] = dot(p.astype(BF), xh).astype(BF)

    @pl.when(flip)
    def _():
        with T("attn"):
            attention()

    with T("barrier"):
        pl.semaphore_wait(barrier, jnp.where(is_last, 8, 6))

    @pl.when(is_last)
    def _():
        for k in range(1, NZ):
            pl.semaphore_signal(
                last_in, inc=1, device_id={"samples": s - 2 * k}, device_id_type=MESH
            )

    def piece_out(far, cond):
        jj = m if far else 1 - m
        dz = 2 * m + jj
        columns = pl.ds(pl.multiple_of(jj * half, half), half)
        piece = g_ref.at[:, columns]
        send(
            cond & (dz != z),
            lambda: rdma(piece, gq.at[z], gq_s, gq_r.at[z], {"samples": 2 * dz + x}),
        )
        send(cond & (dz == z), lambda: rdma(piece, gq.at[z], gq_s, gf_r.at[z], sibling))

        @pl.when(cond & (dz == z))
        def _():
            gq[z] = g_ref[:, columns]

    to_last = (m == 1) & jnp.logical_not(is_last)
    piece_out(False, m < 2)
    piece_out(True, jnp.logical_not(to_last))
    for c in range(NC):
        block = w2.at[x, :, pl.ds(c * wide, wide)]
        send(None, lambda block=block, c=c: rdma(block, block, w_s, w_r.at[c], beside))
    spall[s] = spin_ref[...]

    @pl.when(jnp.logical_not(flip))
    def _():
        with T("attn"):
            attention()

    @pl.when(jnp.logical_not(is_last))
    def _():
        with T("last"):
            pl.semaphore_wait(last_in, 1)

    piece_out(True, to_last)
    for k in range(1, 8):
        other = lax.rem(s + k, 8)
        send(
            None,
            lambda other=other: rdma(spin_ref, spall.at[s], sp_s, sp_r, {"samples": other}),
        )

    mask = mask_ref[...]
    tri = (
        lax.broadcasted_iota(jnp.int32, (tokens, tokens), 0)
        <= lax.broadcasted_iota(jnp.int32, (tokens, tokens), 1)
    ).astype(F32).astype(BF)
    mask_rows = jnp.broadcast_to(mask, (8, tokens)).astype(F32)
    rank = dot(mask_rows.astype(BF), tri)[:1] - 1.0
    region = tokens // 2
    place = lax.broadcasted_iota(jnp.int32, (region, tokens), 0).astype(F32)
    select = jnp.where((rank == place) & (mask > 0), 1.0, 0.0).astype(BF)

    first_core = m == z // 2

    def gather(order, own):
        for n in order:
            zz = actual(n)
            got(first_core, gq.at[zz], gq_r.at[zz])
            send(
                first_core,
                lambda zz=zz: rdma(gq.at[zz], gq.at[zz], gf_s, gf_r.at[zz], sibling),
            )
        for n in (own, *order) if own else order:
            zz = actual(n)
            got(jnp.logical_not(first_core), gq.at[zz], gf_r.at[zz])

    def att_to(c, n, slot, inward):
        zz = actual(n)
        way, ss = (inner_way, in_at_s) if inward else (outer_way, out_at_s)
        send(None, lambda: rdma(att.at[c, zz], att.at[c, zz], ss, at_r.at[c, slot], way))

    def att_got(c, n, slot):
        got(None, att.at[c, actual(n)], at_r.at[c, slot])

    def weights_in(c):
        got(None, w2.at[1 - x, :, pl.ds(c * wide, wide)], w_r.at[c])

    def partials(c, first, count):
        cols = pl.ds(c * wide, wide)
        some = gq[pl.ds(first, count)].reshape(count * tokens, 2 * rows)
        sums = dot(some[:, :rows], w2[0, :, cols]) + dot(some[:, rows:], w2[1, :, cols])
        return sums.reshape(count, tokens, wide)

    def weight_terms(c):
        total = jnp.zeros((2 * rows, wide), F32)
        for zz in range(NZ):
            total += dot(gq[zz], att[c, zz], 0, 0).astype(BF).astype(F32)
        cols = pl.ds(c * wide, wide)

        @pl.when(x == 0)
        def _():
            wown[:, cols] = total[:rows]
            wsend[c] = total[rows:].astype(BF)

        @pl.when(x == 1)
        def _():
            wown[:, cols] = total[rows:]
            wsend[c] = total[:rows].astype(BF)

        send(None, lambda: rdma(wsend.at[c], wrecv.at[c], wr_s, wr_r, beside))

    def backward(b, total_of):
        chunks = GROUPS[b]
        for c in chunks:
            ga[:, c * wide : (c + 1) * wide] = total_of(c).astype(BF)
        for h in range(chunks[0] * per, (chunks[-1] + 1) * per):
            cols = slice(h * HEAD, (h + 1) * HEAD)
            xh = x_ref[:, cols]
            gh = ga[:, cols]
            p = probs[h]
            gp = dot(gh, xh, 1, 1)
            gs = (p * (gp - jnp.sum(gp * p, axis=-1, keepdims=True))).astype(BF)
            through = dot(p.astype(BF), gh, 0, 0) + scale * (dot(gs, xh) + dot(gs, xh, 0, 0))
            g0[:, cols] = (g_ref[:, cols].astype(F32) + through).astype(BF)
        for c in chunks:
            swz[c, s % 4] = dot(select, g0[:, c * wide : (c + 1) * wide]).astype(BF)

    def tile_to(b, other):
        rows_now = swz.at[pl.ds(GROUPS[b][0], len(GROUPS[b])), s % 4]
        send(
            None,
            lambda: rdma(rows_now, rows_now, sw_s, sw_r.at[b, s % 4], {"samples": other}),
        )

    def rows_of(c, which):
        rows_now = swz[c, 0]
        for k in range(1, 4):
            rows_now = jnp.where(which == k, swz[c, k], rows_now)
        return rows_now

    def embed():
        got(None, spall.at[pl.ds(0, 7)], sp_r)
        spins = jnp.where(mask > 0, spall[partner_ref[s]], spin_ref[...])
        onehot = jnp.where(
            spins == lax.broadcasted_iota(jnp.int32, (8, tokens), 0), 1.0, 0.0
        ).astype(BF)
        embs[s] = dot(onehot, g0[...])[:SPINS]
        for k in range(1, 8):
            other = lax.rem(s + k, 8)
            send(
                None,
                lambda other=other: rdma(embs.at[s], embs.at[s], em_s, em_r, {"samples": other}),
            )

    mine = partner_ref[s]
    eye = lax.broadcasted_iota(jnp.int32, (tokens, tokens), 0) == lax.broadcasted_iota(
        jnp.int32, (tokens, tokens), 1
    )
    keep = jnp.where(eye & (mask == 0), 1.0, 0.0).astype(BF)

    def rows_in(b, other_of):
        chunks = GROUPS[b]
        got(None, xrecv.at[pl.ds(chunks[0], len(chunks))], xs_r.at[b])
        for c in chunks:
            cols = slice(c * wide, (c + 1) * wide)
            chosen = jnp.where(mine // 4 == s // 4, other_of(c), xrecv[c])
            cot_ref[:, cols] = (dot(keep, g0[:, cols]) + dot(select, chosen, 0, 0)).astype(BF)

    def embed_sum():
        got(None, embs.at[pl.ds(0, 7)], em_r)
        total = embs[0]
        for k in range(1, 8):
            total += embs[k]
        emb_ref[...] = total

    def weights_out():
        got(None, wrecv, wr_r)
        for c in range(NC):
            cols = slice(c * wide, (c + 1) * wide)
            wg_ref[:, cols] = wown[:, cols] + wrecv[c].astype(F32)

    def end_tasks():
        def total_of(c):
            got(None, far_in.at[c, 0], far_r.at[c, 0])
            return pf[c, actual(3)] + far_in[c, 0].astype(F32)

        def part_out(c, n):
            zz = actual(n)
            send(
                None,
                lambda: rdma(
                    pb.at[c, zz], near_in.at[c, n], ps_s, near_r.at[c, n], inner_way
                ),
            )

        weights_seen = set()

        def weights(c):
            if c not in weights_seen:
                weights_seen.add(c)
                weights_in(c)

        def p2(c):
            weights(c)
            first = jnp.where(flip, 0, 2)
            sums = partials(c, first, 2)
            pf[c, pl.ds(first, 2)] = sums
            pb[c, pl.ds(first, 2)] = sums.astype(BF)

        def p01(c):
            weights(c)
            first = jnp.where(flip, 2, 0)
            pb[c, pl.ds(first, 2)] = partials(c, first, 2).astype(BF)

        def back(b):
            backward(b, total_of)
            tile_to(b, s - outward + 1 - 2 * x)
            tile_to(b, s - outward)

        def fin(b):
            got(None, irecv.at[pl.ds(GROUPS[b][0], len(GROUPS[b]))], si_r.at[b])
            rows_in(b, lambda c: irecv[c])

        def wt(c):
            for slot in range(3):
                att_got(c, 2 - slot, slot)
            weight_terms(c)

        return {
            "ga": lambda: gather((2,), 3),
            "gb": lambda: gather((1, 0), None),
            "attE": lambda c: att_to(c, 3, 0, True),
            "s0": lambda c: part_out(c, 0), "s1": lambda c: part_out(c, 1), "s2": lambda c: part_out(c, 2),
            "p2": p2, "p01": p01, "wt": wt,
            "back": back, "emb": embed, "fin": fin, "finw": weights_out, "embw": embed_sum,
        }

    def inner_tasks():
        def total_of(c):
            got(None, near_in.at[c, 2], near_r.at[c, 2])
            got(None, far_in.at[c, 1], far_r.at[c, 1])
            return pf[c, actual(2)] + near_in[c, 2].astype(F32) + far_in[c, 1].astype(F32)

        def part(c):
            weights_in(c)
            pf[c] = partials(c, 0, NZ)

        def far(c, n):
            got(None, near_in.at[c, n], near_r.at[c, n])
            pb[c, n] = (pf[c, actual(n)] + near_in[c, n].astype(F32)).astype(BF)
            send(
                None,
                lambda: rdma(pb.at[c, n], far_in.at[c, n], ps_s, far_r.at[c, n], inner_way),
            )

        def near(c):
            got(None, far_in.at[c, 0], far_r.at[c, 0])
            pb[c, 3] = (pf[c, actual(3)] + far_in[c, 0].astype(F32)).astype(BF)
            send(
                None,
                lambda: rdma(pb.at[c, 3], far_in.at[c, 0], ps_s, far_r.at[c, 0], outer_way),
            )

        def back(b):
            backward(b, total_of)
            tile_to(b, 2 * z + 1 - x)

        def across(b):
            part = pl.ds(GROUPS[b][0], len(GROUPS[b]))
            for k in range(1, 4):
                got(None, swz.at[part, 0], sw_r.at[b, lax.rem(s + k, 4)])
            for k, dest in enumerate((s - 2 * outward, s - outward, s + outward)):
                wanted = lax.rem(partner_ref[dest], 4)
                for c in GROUPS[b]:
                    xsend[k, c] = rows_of(c, wanted)
                into, rs = (irecv, si_r) if k == 2 else (xrecv, xs_r)
                send(
                    None,
                    lambda k=k, dest=dest, into=into, rs=rs: rdma(
                        xsend.at[k, part], into.at[part], xs_s, rs.at[b], {"samples": dest}
                    ),
                )

        def fin(b):
            rows_in(b, lambda c: rows_of(c, lax.rem(mine, 4)))

        def relay(n, slot, to_slot, inward):
            def run(c):
                att_got(c, n, slot)
                att_to(c, n, to_slot, inward)

            return run

        return {
            "gather": lambda: gather((3, 1, 0), 2),
            "attIi": lambda c: att_to(c, 2, 1, True), "attIo": lambda c: att_to(c, 2, 0, False),
            "part": part, "near": near,
            "far0": lambda c: far(c, 0), "far1": lambda c: far(c, 1),
            "r3": relay(3, 0, 2, True),
            "r1": relay(1, 1, 1, False),
            "r0": relay(0, 2, 2, False),
            "wt": weight_terms, "back": back, "across": across, "emb": embed, "fin": fin, "finw": weights_out,
            "embw": embed_sum,
        }

    def run(tasks, order):
        for name, *at in order:
            with T("_".join([name, *map(str, at)])):
                tasks[name](*at)

    @pl.when(is_end)
    def _():
        run(end_tasks(), END_ORDER)
        sent(None, att.at[:, 0], in_at_s)
        sent(None, swz.at[:, pl.ds(0, 2)], sw_s)

    @pl.when(jnp.logical_not(is_end))
    def _():
        run(inner_tasks(), INNER_ORDER)
        sent(None, att.at[:, pl.ds(0, 2)], in_at_s)
        sent(None, att.at[:, pl.ds(0, 3)], out_at_s)
        sent(None, swz.at[:, 0], sw_s)
        sent(None, xsend, xs_s)

    with T("sends_done"):
        sent(None, g_ref, gq_s)
        sent(first_core, gq.at[pl.ds(0, 3)], gf_s)
        sent(None, w2.at[0], w_s)
        sent(None, spall.at[pl.ds(0, 7)], sp_s)
        sent(None, embs.at[pl.ds(0, 7)], em_s)
        sent(None, pb.at[:, pl.ds(0, 3)], ps_s)
        sent(None, wsend, wr_s)


def put_out(wg_ref, cot_ref, emb_ref, wg_out, cot_out, emb_out, done):
    copies = [
        pltpu.make_async_copy(wg_ref, wg_out, done.at[0]),
        pltpu.make_async_copy(cot_ref, cot_out, done.at[1]),
        pltpu.make_async_copy(emb_ref, emb_out, done.at[2]),
    ]
    for copy in copies:
        copy.start()
    for copy in copies:
        copy.wait()


def one_layer(
    stored_inputs, top_cotangent, layer_weights, block_layout, region_mask, partner_samples, spins
):
    tokens, width = stored_inputs.shape[2:]
    rows = layer_weights.shape[1]
    hbm = pl.BlockSpec(memory_space=pltpu.HBM)
    vmem = pl.BlockSpec(memory_space=pltpu.VMEM)
    region = tokens // 2
    dma = pltpu.SemaphoreType.DMA
    half = width // 2
    wide = width // NC
    shapes = [
        ((NZ, tokens, 2 * rows), BF),
        ((2, rows, width), BF),
        ((NC, NZ, tokens, wide), F32),
        ((NC, NZ, tokens, wide), BF),
        ((NC, 3, tokens, wide), BF),
        ((NC, 2, tokens, wide), BF),
        ((NC, NZ, tokens, wide), BF),
        ((width // HEAD, tokens, tokens), F32),
        ((tokens, width), BF),
        ((tokens, width), BF),
        ((NC, 4, region, wide), BF),
        ((3, NC, region, wide), BF),
        ((NC, region, wide), BF),
        ((NC, region, wide), BF),
        ((8, 1, tokens), jnp.int32),
        ((8, SPINS, width), F32),
        ((NC, rows, wide), BF),
        ((NC, rows, wide), BF),
        ((rows, width), F32),
    ]
    one = dma
    sems = [
        dma((7,)), one, dma((NZ,)), one, dma((NZ,)), one, dma((NC,)), one, one, one, one, dma((NC, 3)), one,
        dma((NC, 3)), dma((NC, 2)), one, dma((len(GROUPS), 4)), one, dma((len(GROUPS),)), dma((len(GROUPS),)),
        one, one, one, one, pltpu.SemaphoreType.REGULAR,
    ]
    wg, cot, emb = pl.pallas_call(
        kernel,
        out_shape=[
            jax.ShapeDtypeStruct((rows, width), F32),
            jax.ShapeDtypeStruct((tokens, width), BF),
            jax.ShapeDtypeStruct((SPINS, width), F32),
        ],
        in_specs=[hbm] * 7,
        out_specs=[vmem] * 3,
        scratch_shapes=[
            pltpu.VMEM((tokens, width), BF),
            pltpu.VMEM((tokens, width), BF),
            pltpu.SMEM((2, 2), jnp.int32),
            pltpu.VMEM((1, tokens), jnp.int32),
            pltpu.SMEM((8,), jnp.int32),
            pltpu.VMEM((1, tokens), jnp.int32),
        ]
        + [pltpu.VMEM(a, b) for a, b in shapes]
        + sems,
        compiler_params=pltpu.CompilerParams(
            collective_id=0, has_side_effects=True, vmem_limit_bytes=48 * 1024 * 1024
        ),
    )(
        *[
            pltpu.with_memory_space_constraint(value, pltpu.HBM)
            for value in (
                stored_inputs[0, 0], top_cotangent[0], layer_weights[0], block_layout[0],
                region_mask[None], partner_samples, spins,
            )
        ]
    )
    anywhere = pl.BlockSpec(memory_space=pl.ANY)
    wg, cot, emb = pl.pallas_call(
        put_out,
        out_shape=[jax.ShapeDtypeStruct(a.shape, a.dtype) for a in (wg, cot, emb)],
        in_specs=[vmem] * 3,
        out_specs=[anywhere] * 3,
        scratch_shapes=[dma((3,))],
        compiler_params=pltpu.CompilerParams(vmem_limit_bytes=8 * 1024 * 1024),
    )(wg, cot, emb)
    return wg[None], cot[None, None], emb


def solution(mesh):
    in_specs = (
        P("section", ("groups", "samples"), None, "mp"),
        P(("groups", "samples"), None, "mp"),
        P("section", "samples", "mp"),
        P("section", None, None),
        P(),
        P("groups"),
        P(("groups", "samples"), None),
    )
    out_specs = (
        P(("groups", "section"), "samples", "mp"),
        P("section", ("groups", "samples"), None, "mp"),
        P("groups", "mp"),
    )
    small = mesh.shape["samples"] == 8 and mesh.shape["section"] == 1 and mesh.shape["mp"] == 2
    body = one_layer if small else local
    return jax.shard_map(body, mesh=mesh, in_specs=in_specs, out_specs=out_specs, check_vma=False)
```
